32 devices in a mesh: expert: 8 (over z, y), tensor: 4 (over x, core).
Axes of the slice: x: 2, y: 2, z: 4, core: 2. Of those that a mesh axis runs over, the one named last changes fastest.
Arguments:
- tokens: bfloat16 [3152, 768], P('expert'), may hold values from -6 to 6
- norm1_gain: float32 [768], replicated, may hold values from 0.5 to 1.5
- norm1_shift: float32 [768], replicated, may hold values from -4 to 4
- qkv_weight: bfloat16 [768, 2304], P(None, 'tensor'), may hold values from -3 to 3
- proj_weight: bfloat16 [768, 768], P('tensor'), may hold values from -1.75 to 1.75
- proj_shift: float32 [768], replicated, may hold values from -6 to 6
- norm2_gain: float32 [768], replicated, may hold values from 0.5 to 1.5
- norm2_shift: float32 [768], replicated, may hold values from -4 to 4
- router_weight: bfloat16 [768, 8], replicated, may hold values from -8 to 8
- expand_weight: bfloat16 [8, 768, 3072], P('expert', None, 'tensor'), may hold values from -0.21875 to 0.21875
- expand_shift: float32 [8, 3072], P('expert', 'tensor'), may hold values from -6 to 6
- shrink_weight: bfloat16 [8, 3072, 768], P('expert', 'tensor'), may hold values from -0.109375 to 0.109375
- shrink_shift: float32 [8, 768], P('expert'), may hold values from -4 to 4
- route_expert: int32 [3152, 2], P('expert'), may hold values from 0 to 7, as said below
- route_slot: int32 [3152, 2], P('expert'), may hold values from -1 to 123, as said below
- cotangent: bfloat16 [3152, 768], P('expert'), may hold values from -6 to 6
Outputs:
- output: float32 [3152, 768], P('expert')
- tokens_grad: float32 [3152, 768], P('expert')
- gain1_grad: float32 [768], replicated
- shift1_grad: float32 [768], replicated
- qkv_grad: float32 [768, 2304], P(None, 'tensor')
- proj_grad: float32 [768, 768], P('tensor')
- pshift_grad: float32 [768], replicated
- gain2_grad: float32 [768], replicated
- shift2_grad: float32 [768], replicated
- router_grad: float32 [768, 8], replicated
- expand_grad: float32 [8, 768, 3072], P('expert', None, 'tensor')
- eshift_grad: float32 [8, 3072], P('expert', 'tensor')
- shrink_grad: float32 [8, 3072, 768], P('expert', 'tensor')
- sshift_grad: float32 [8, 768], P('expert')
The draws below stay inside these ranges and needn't reach their ends.
Inputs may be any that keep to these rules, and one draw needn't show every extreme that they name: `route_expert`: each row names two different experts. In some expert's column more than 124 first choices fall in the rows of one device, in every draw. `route_slot`: within the rows of one device and for each expert, the first choices of all rows in row order and then the second choices in row order take slots 0, 1, 2, ... of that expert; once 124 slots are taken, further choices of it get -1. Some expert has all 124 slots taken in every device's rows, in every draw.
All inputs are finite; a program needn't handle non-finite values.
Results may differ from the reference program's by a relative error of at most 0.03.
Values may be sent and summed in bfloat16 or wider, within the bound.
A program may use at most 128 MiB of HBM per device.

```python
import jax
import jax.numpy as jnp
from jax import lax

D = 768
H = 12
DH = 64
FF = 3072
SEQ = 197
IMG_DEV = 2
TOK_DEV = 394
TOKENS = 3152
EXPERTS = 8
CAP = 124
N_TENSOR = 4


def route_pair(key):
    blocks = TOKENS // TOK_DEV
    first_key = jax.random.fold_in(key, 101)
    second_key = jax.random.fold_in(key, 202)
    label_key = jax.random.fold_in(key, 303)
    order_key = jax.random.fold_in(key, 404)
    other_key = jax.random.fold_in(key, 505)
    raw_pick = jax.random.randint(first_key, (TOKENS,), 0, EXPERTS) * jax.random.randint(second_key, (TOKENS,), 0, EXPERTS) // EXPERTS
    relabel = jax.random.permutation(label_key, EXPERTS).astype(jnp.int32)
    first_choice = relabel[raw_pick]

    def block_order(block_key):
        return jax.random.permutation(block_key, TOK_DEV)
    orders = jax.vmap(block_order)(jax.random.split(order_key, blocks))
    ranks = jnp.argsort(orders, axis=1)
    forced = (ranks < CAP + 2).reshape(TOKENS)
    first_choice = jnp.where(forced, relabel[0], first_choice)
    second_choice = (first_choice + 1 + jax.random.randint(other_key, (TOKENS,), 0, EXPERTS - 1)) % EXPERTS
    expert_ids = jnp.stack([first_choice, second_choice], axis=1).astype(jnp.int32)
    ordered = jnp.transpose(expert_ids.reshape(blocks, TOK_DEV, 2), (0, 2, 1)).reshape(blocks, 2 * TOK_DEV)
    hits = (ordered[:, :, None] == jnp.arange(EXPERTS, dtype=jnp.int32)[None, None, :]).astype(jnp.int32)
    before = jnp.cumsum(hits, axis=1) - hits
    position = jnp.sum(before * hits, axis=2)
    position = jnp.transpose(position.reshape(blocks, 2, TOK_DEV), (0, 2, 1)).reshape(TOKENS, 2)
    slot_ids = jnp.where(position < CAP, position, -1).astype(jnp.int32)
    return (expert_ids, slot_ids)


def draw_route_expert(key, part):
    return route_pair(key)[0]


def draw_route_slot(key, part):
    return route_pair(key)[1]


def draw_qkv_weight(key, part):
    base = jnp.clip(jax.random.normal(key, (D, 3 * H * DH), jnp.float32), -6.0, 6.0) * D ** (-0.5)
    return jnp.clip(base, -3.0, 3.0).astype(jnp.bfloat16)


def draw_router_weight(key, part):
    base = jnp.clip(jax.random.normal(key, (D, EXPERTS), jnp.float32), -6.0, 6.0) * D ** (-0.5)
    return jnp.clip(base, -8.0, 8.0).astype(jnp.bfloat16)


def shard_levels(own_key, shape, cuts, low, high):
    loudness = 1.0
    for dim, blocks in cuts:
        draws = jax.random.uniform(jax.random.fold_in(jax.random.fold_in(own_key, 6), dim), (blocks,), jnp.float32, low / len(cuts), high / len(cuts))
        loudness = loudness * jnp.repeat(jnp.exp(draws), shape[dim] // blocks).reshape((-1,) + (1,) * (len(shape) - 1 - dim))
    return loudness


def bell_draw(stream_key, shape, width, limit, pieces=(), held_as=jnp.bfloat16):
    result = width * jax.random.normal(stream_key, shape, jnp.float32)
    if pieces:
        result = result * shard_levels(stream_key, shape, pieces, -0.22, 0.18)
    return jnp.clip(result, -limit, limit).astype(held_as)


def setup_inputs(seed: int = 0) -> dict:
    streams_of = jax.random.split(jax.random.key(seed), 17)
    return {
        "tokens": bell_draw(streams_of[0], (TOKENS, D), 1.0, 6.0, ((0, 8),)),
        "norm1_gain": jnp.clip(1.0 + 0.1 * jax.random.normal(streams_of[1], (D,), jnp.float32), 0.5, 1.5),
        "norm1_shift": bell_draw(streams_of[2], (D,), 0.3, 4.0, (), jnp.float32),
        "qkv_weight": draw_qkv_weight(jax.random.fold_in(streams_of[16], 71), 0),
        "proj_weight": bell_draw(streams_of[4], (H * DH, D), (H * DH // 64) ** -0.5, 1.75, ((0, 4),)),
        "proj_shift": bell_draw(streams_of[5], (D,), 1.0, 6.0, (), jnp.float32),
        "norm2_gain": jnp.clip(1.0 + 0.1 * jax.random.normal(streams_of[6], (D,), jnp.float32), 0.5, 1.5),
        "norm2_shift": bell_draw(streams_of[7], (D,), 0.3, 4.0, (), jnp.float32),
        "router_weight": draw_router_weight(jax.random.fold_in(streams_of[16], 71), 0),
        "expand_weight": bell_draw(streams_of[9], (EXPERTS, D, FF), D ** -0.5, 0.21875, ((0, 8), (2, 4))),
        "expand_shift": bell_draw(streams_of[10], (EXPERTS, FF), 0.5, 6.0, ((0, 8), (1, 4)), jnp.float32),
        "shrink_weight": bell_draw(streams_of[11], (EXPERTS, FF, D), FF ** -0.5, 0.109375, ((0, 8), (1, 4))),
        "shrink_shift": bell_draw(streams_of[12], (EXPERTS, D), 0.3, 4.0, ((0, 8),), jnp.float32),
        "route_expert": draw_route_expert(jax.random.fold_in(streams_of[16], 71), 0),
        "route_slot": draw_route_slot(jax.random.fold_in(streams_of[16], 71), 0),
        "cotangent": bell_draw(streams_of[15], (TOKENS, D), 1.0, 6.0, ((0, 8),)),
    }


norm_eps = 1e-06
half_root = 0.7071067811865476
gauss_peak = 0.3989422804014327

def normalize(values, norm_gain, norm_shift):
    row_mean = lax.optimization_barrier(jnp.mean(values, axis=1, keepdims=True))
    centered = values - row_mean
    variance = lax.optimization_barrier(jnp.mean(centered * centered, axis=1, keepdims=True))
    inverse = lax.rsqrt(variance + norm_eps)
    scaled = centered * inverse
    return (scaled * norm_gain + norm_shift, scaled, inverse)

def norm_back(upstream, scaled, inverse, norm_gain):
    weighted = upstream * norm_gain
    first_mean = lax.optimization_barrier(jnp.mean(weighted, axis=1, keepdims=True))
    second_mean = lax.optimization_barrier(jnp.mean(weighted * scaled, axis=1, keepdims=True))
    return inverse * (weighted - first_mean - scaled * second_mean)

def gelu_exact(preact):
    return 0.5 * preact * (1.0 + lax.erf(preact * half_root))

def gelu_slope(preact):
    return 0.5 * (1.0 + lax.erf(preact * half_root)) + preact * jnp.exp(-0.5 * preact * preact) * gauss_peak

def route_tables(route_expert, route_slot, experts, capacity):
    tok_count = route_expert.shape[0]
    kept = route_slot >= 0
    targets = jnp.where(kept, route_expert * capacity + route_slot, experts * capacity).reshape(-1).astype(jnp.int32)
    numbers = jnp.arange(2 * tok_count, dtype=jnp.int32)
    owners = jnp.full((experts * capacity,), 2 * tok_count, jnp.int32).at[targets].set(numbers, mode='drop')
    return (targets, owners)

def attend_front(normed_b, qkv_weight, images):
    tok_count = normed_b.shape[0]
    head_count = qkv_weight.shape[1] // (3 * DH)
    projected = jnp.dot(normed_b, qkv_weight, preferred_element_type=jnp.float32).astype(jnp.bfloat16)
    projected = projected.reshape(images, SEQ, head_count, 3, DH)
    queries = projected[:, :, :, 0]
    keys_b = projected[:, :, :, 1]
    values_b = projected[:, :, :, 2]
    scores = jnp.einsum('bqhd,bkhd->bhqk', queries.astype(jnp.float32), keys_b.astype(jnp.float32)) * DH ** (-0.5)
    row_top = lax.optimization_barrier(jnp.max(scores, axis=3, keepdims=True))
    log_total = row_top + jnp.log(lax.optimization_barrier(jnp.sum(jnp.exp(scores - row_top), axis=3, keepdims=True)))
    attn_b = jnp.exp(scores - log_total).astype(jnp.bfloat16)
    context = jnp.einsum('bhqk,bkhd->bqhd', attn_b.astype(jnp.float32), values_b.astype(jnp.float32))
    context_b = context.astype(jnp.bfloat16).reshape(tok_count, head_count * DH)
    return (queries, keys_b, values_b, log_total, context_b)

def attend_back(queries, keys_b, values_b, log_total, context_b, context_grad, images):
    tok_count = context_b.shape[0]
    head_count = queries.shape[2]
    factor = DH ** (-0.5)
    scores = jnp.einsum('bqhd,bkhd->bhqk', queries.astype(jnp.float32), keys_b.astype(jnp.float32)) * factor
    attention = jnp.exp(scores - log_total)
    attn_b = attention.astype(jnp.bfloat16)
    grad_ctx = context_grad.reshape(images, SEQ, head_count, DH).astype(jnp.float32)
    context_f = context_b.reshape(images, SEQ, head_count, DH).astype(jnp.float32)
    value_grad = jnp.einsum('bhqk,bqhd->bkhd', attn_b.astype(jnp.float32), grad_ctx)
    attn_grad = jnp.einsum('bqhd,bkhd->bhqk', grad_ctx, values_b.astype(jnp.float32))
    row_dot = jnp.transpose(lax.optimization_barrier(jnp.sum(grad_ctx * context_f, axis=3)), (0, 2, 1))[:, :, :, None]
    score_grad = (attention * (attn_grad - row_dot) * factor).astype(jnp.bfloat16).astype(jnp.float32)
    query_grad = jnp.einsum('bhqk,bkhd->bqhd', score_grad, keys_b.astype(jnp.float32))
    key_grad = jnp.einsum('bhqk,bqhd->bkhd', score_grad, queries.astype(jnp.float32))
    stacked = jnp.stack([query_grad, key_grad, value_grad], axis=3)
    return stacked.astype(jnp.bfloat16).reshape(tok_count, head_count * 3 * DH)

def quarter_sum(left_b, right_b):
    span_cols = left_b.shape[1] // N_TENSOR
    summed = jnp.zeros((left_b.shape[0], right_b.shape[1]), jnp.float32)
    for quarter in range(N_TENSOR):
        partial_value = jnp.dot(left_b[:, quarter * span_cols:(quarter + 1) * span_cols], right_b[quarter * span_cols:(quarter + 1) * span_cols], preferred_element_type=jnp.float32)
        summed = summed + lax.optimization_barrier(partial_value.astype(jnp.bfloat16)).astype(jnp.float32)
    return summed

def reference(tokens, norm1_gain, norm1_shift, qkv_weight, proj_weight, proj_shift, norm2_gain, norm2_shift, router_weight, expand_weight, expand_shift, shrink_weight, shrink_shift, route_expert, route_slot, cotangent):
    blocks = TOKENS // TOK_DEV
    tok_blocks = tokens.reshape(blocks, TOK_DEV, D)
    exp_blocks = route_expert.reshape(blocks, TOK_DEV, 2)
    slot_blocks = route_slot.reshape(blocks, TOK_DEV, 2)
    cot_blocks = cotangent.reshape(blocks, TOK_DEV, D)

    def front(token_blk, expert_blk, slot_blk):
        token_f = token_blk.astype(jnp.float32)
        normed, scaled1, inverse1 = normalize(token_f, norm1_gain, norm1_shift)
        normed_b = normed.astype(jnp.bfloat16)
        queries, keys_b, values_b, log_total, context_b = attend_front(normed_b, qkv_weight, IMG_DEV)
        hidden = token_f + jnp.dot(context_b, proj_weight, preferred_element_type=jnp.float32) + proj_shift
        normed2, scaled2, inverse2 = normalize(hidden, norm2_gain, norm2_shift)
        mixed_b = normed2.astype(jnp.bfloat16)
        logits = jnp.dot(mixed_b, router_weight, preferred_element_type=jnp.float32)
        pick_mask = (lax.broadcasted_iota(jnp.int32, (TOK_DEV, 2, EXPERTS), 2) == expert_blk[:, :, None]).astype(jnp.float32)
        chosen = lax.optimization_barrier(jnp.sum(logits[:, None, :] * pick_mask, axis=2))
        gate_top = lax.optimization_barrier(jnp.max(chosen, axis=1, keepdims=True))
        lifted = jnp.exp(chosen - gate_top)
        gate_weights = lifted / lax.optimization_barrier(jnp.sum(lifted, axis=1, keepdims=True))
        targets, owners = route_tables(expert_blk, slot_blk, EXPERTS, CAP)
        return (token_f, scaled1, inverse1, normed_b, queries, keys_b, values_b, log_total, context_b, hidden, scaled2, inverse2, mixed_b, pick_mask, gate_weights, targets, owners)

    def to_experts(stacked):
        return jnp.transpose(stacked.reshape(blocks, EXPERTS, CAP, D), (1, 0, 2, 3)).reshape(EXPERTS, blocks * CAP, D)

    def from_experts(stacked):
        return jnp.transpose(stacked.reshape(EXPERTS, blocks, CAP, D), (1, 0, 2, 3)).reshape(blocks, EXPERTS * CAP, D)

    def gather_rows(inputs):
        state = front(inputs[0], inputs[1], inputs[2])
        return jnp.take(state[12], state[16] // 2, axis=0, mode='fill', fill_value=0)
    buffers = lax.map(gather_rows, (tok_blocks, exp_blocks, slot_blocks))
    expert_rows = to_experts(buffers)

    def expert_front(inputs):
        rows_e, expand_e, eshift_e, shrink_e, sshift_e = inputs
        preact = jnp.dot(rows_e, expand_e, preferred_element_type=jnp.float32) + eshift_e
        activ_b = gelu_exact(preact).astype(jnp.bfloat16)
        return (quarter_sum(activ_b, shrink_e) + sshift_e).astype(jnp.bfloat16)
    expert_out = lax.map(expert_front, (expert_rows, expand_weight, expand_shift, shrink_weight, shrink_shift))
    returned = from_experts(expert_out)

    def middle(inputs):
        token_blk, expert_blk, slot_blk, returned_blk, cot_blk = inputs
        state = front(token_blk, expert_blk, slot_blk)
        hidden = state[9]
        gate_weights = state[14]
        picked = jnp.take(returned_blk, state[15], axis=0, mode='fill', fill_value=0).reshape(TOK_DEV, 2, D).astype(jnp.float32)
        output_blk = hidden + lax.optimization_barrier(jnp.sum(gate_weights[:, :, None] * picked, axis=1))
        weighted = (gate_weights[:, :, None] * cot_blk.astype(jnp.float32)[:, None, :]).astype(jnp.bfloat16).reshape(2 * TOK_DEV, D)
        grad_buf = jnp.take(weighted, state[16], axis=0, mode='fill', fill_value=0)
        return (output_blk, grad_buf)
    output_blocks, grad_buffers = lax.map(middle, (tok_blocks, exp_blocks, slot_blocks, returned, cot_blocks))
    slot_grad = to_experts(grad_buffers)

    def expert_back(inputs):
        rows_e, grad_e, expand_e, eshift_e, shrink_e = inputs
        preact = jnp.dot(rows_e, expand_e, preferred_element_type=jnp.float32) + eshift_e
        activ_b = gelu_exact(preact).astype(jnp.bfloat16)
        shrink_g = jnp.dot(activ_b.T, grad_e, preferred_element_type=jnp.float32)
        sshift_g = lax.optimization_barrier(jnp.sum(grad_e.astype(jnp.float32), axis=0))
        pre_grad = jnp.dot(grad_e, shrink_e.T, preferred_element_type=jnp.float32) * gelu_slope(preact)
        pre_gradb = pre_grad.astype(jnp.bfloat16)
        expand_g = jnp.dot(rows_e.T, pre_gradb, preferred_element_type=jnp.float32)
        eshift_g = lax.optimization_barrier(jnp.sum(pre_grad, axis=0))
        rows_grad = quarter_sum(pre_gradb, expand_e.T).astype(jnp.bfloat16)
        return (rows_grad, expand_g, eshift_g, shrink_g, sshift_g)
    rows_grad, expand_grad, eshift_grad, shrink_grad, sshift_grad = lax.map(expert_back, (expert_rows, slot_grad, expand_weight, expand_shift, shrink_weight))
    back_rows = from_experts(rows_grad)

    def backward_block(running, inputs):
        token_blk, expert_blk, slot_blk, returned_blk, back_blk, cot_blk = inputs
        token_f, scaled1, inverse1, normed_b, queries, keys_b, values_b, log_total, context_b, hidden, scaled2, inverse2, mixed_b, pick_mask, gate_weights, targets, owners = front(token_blk, expert_blk, slot_blk)
        upstream = cot_blk.astype(jnp.float32)
        picked = jnp.take(returned_blk, targets, axis=0, mode='fill', fill_value=0).reshape(TOK_DEV, 2, D).astype(jnp.float32)
        gate_grad = lax.optimization_barrier(jnp.sum(upstream[:, None, :] * picked, axis=2))
        common = lax.optimization_barrier(jnp.sum(gate_weights * gate_grad, axis=1, keepdims=True))
        chosen_grad = gate_weights * (gate_grad - common)
        logit_grad = lax.optimization_barrier(jnp.sum(pick_mask * chosen_grad[:, :, None], axis=1)).astype(jnp.bfloat16)
        router_g = jnp.dot(mixed_b.T, logit_grad, preferred_element_type=jnp.float32)
        back_pick = jnp.take(back_blk, targets, axis=0, mode='fill', fill_value=0).reshape(TOK_DEV, 2, D).astype(jnp.float32)
        mixed_grad = lax.optimization_barrier(jnp.sum(back_pick, axis=1)) + jnp.dot(logit_grad, router_weight.T, preferred_element_type=jnp.float32)
        gain2_g = lax.optimization_barrier(jnp.sum(mixed_grad * scaled2, axis=0))
        shift2_g = lax.optimization_barrier(jnp.sum(mixed_grad, axis=0))
        hidden_grad = upstream + norm_back(mixed_grad, scaled2, inverse2, norm2_gain)
        pshift_g = lax.optimization_barrier(jnp.sum(hidden_grad, axis=0))
        hidden_gradb = hidden_grad.astype(jnp.bfloat16)
        proj_g = jnp.dot(context_b.T, hidden_gradb, preferred_element_type=jnp.float32)
        context_grad = jnp.dot(hidden_gradb, proj_weight.T, preferred_element_type=jnp.float32).astype(jnp.bfloat16)
        qkv_gradb = attend_back(queries, keys_b, values_b, log_total, context_b, context_grad, IMG_DEV)
        qkv_g = jnp.dot(normed_b.T, qkv_gradb, preferred_element_type=jnp.float32)
        normed_grad = jnp.dot(qkv_gradb, qkv_weight.T, preferred_element_type=jnp.float32)
        gain1_g = lax.optimization_barrier(jnp.sum(normed_grad * scaled1, axis=0))
        shift1_g = lax.optimization_barrier(jnp.sum(normed_grad, axis=0))
        tokens_g = hidden_grad + norm_back(normed_grad, scaled1, inverse1, norm1_gain)
        terms = (gain1_g, shift1_g, qkv_g, proj_g, pshift_g, gain2_g, shift2_g, router_g)
        return (jax.tree.map(jnp.add, running, terms), tokens_g)
    zero_width = jnp.zeros((D,), jnp.float32)
    initial = (zero_width, zero_width, jnp.zeros((D, 3 * H * DH), jnp.float32), jnp.zeros((H * DH, D), jnp.float32), zero_width, zero_width, zero_width, jnp.zeros((D, EXPERTS), jnp.float32))
    running, tokens_blocks = lax.scan(backward_block, initial, (tok_blocks, exp_blocks, slot_blocks, returned, back_rows, cot_blocks))
    return (output_blocks.reshape(TOKENS, D), tokens_blocks.reshape(TOKENS, D), running[0], running[1], running[2], running[3], running[4], running[5], running[6], running[7], expand_grad, eshift_grad, shrink_grad, sshift_grad)
```

```python
import jax
import jax.numpy as jnp
from jax import lax
from jax.experimental import pallas as pl
from jax.experimental.pallas import tpu as pltpu
from jax.sharding import PartitionSpec as P

DH = 64
SEQ = 197


norm_eps = 1e-06
half_root = 0.7071067811865476
gauss_peak = 0.3989422804014327


def normalize(values, norm_gain, norm_shift):
    row_mean = jnp.mean(values, axis=1, keepdims=True)
    centered = values - row_mean
    variance = jnp.mean(centered * centered, axis=1, keepdims=True)
    inverse = lax.rsqrt(variance + norm_eps)
    scaled = centered * inverse
    return (scaled * norm_gain + norm_shift, scaled, inverse)


def norm_back(upstream, scaled, inverse, norm_gain):
    weighted = upstream * norm_gain
    first_mean = jnp.mean(weighted, axis=1, keepdims=True)
    second_mean = jnp.mean(weighted * scaled, axis=1, keepdims=True)
    return inverse * (weighted - first_mean - scaled * second_mean)


def gelu_exact(preact):
    return 0.5 * preact * (1.0 + lax.erf(preact * half_root))


def gelu_slope(preact):
    return (
        0.5 * (1.0 + lax.erf(preact * half_root))
        + preact * jnp.exp(-0.5 * preact * preact) * gauss_peak
    )


def inner_rows(left_b, right_b):
    return lax.dot_general(
        left_b, right_b, (((0,), (0,)), ((), ())), preferred_element_type=jnp.float32
    )


def outer_cols(left_b, right_b):
    return lax.dot_general(
        left_b, right_b, (((1,), (1,)), ((), ())), preferred_element_type=jnp.float32
    )


def route_tables(route_expert, route_slot, experts, capacity):
    tok_count = route_expert.shape[0]
    kept = route_slot >= 0
    targets = jnp.where(kept, route_expert * capacity + route_slot, experts * capacity).reshape(-1)
    numbers = jnp.arange(2 * tok_count, dtype=jnp.int32)
    owners = (
        jnp.full((experts * capacity,), 2 * tok_count, jnp.int32)
        .at[targets]
        .set(numbers, mode="drop")
    )
    return (targets, owners)


def heads_total(partial_value):
    return lax.psum(partial_value.astype(jnp.bfloat16), "tensor").astype(jnp.float32)


def send_rows(buffer):
    return lax.all_to_all(buffer, "expert", split_axis=0, concat_axis=0, tiled=True)


def return_rows(partial_value, offset):
    summed = lax.psum(partial_value.astype(jnp.bfloat16), "tensor").astype(jnp.float32)
    ready = (summed + offset).astype(jnp.bfloat16)
    return lax.all_to_all(ready, "expert", split_axis=0, concat_axis=0, tiled=True)


def attend_front(normed_b, qkv_weight, images):
    tok_count = normed_b.shape[0]
    head_count = qkv_weight.shape[1] // (3 * DH)
    projected = jnp.dot(normed_b, qkv_weight, preferred_element_type=jnp.float32).astype(
        jnp.bfloat16
    )
    projected = projected.reshape(images, SEQ, head_count, 3, DH)
    queries = projected[:, :, :, 0]
    keys_b = projected[:, :, :, 1]
    values_b = projected[:, :, :, 2]
    scores = jnp.einsum(
        "bqhd,bkhd->bhqk", queries, keys_b, preferred_element_type=jnp.float32
    ) * DH ** (-0.5)
    row_top = jnp.max(scores, axis=3, keepdims=True)
    log_total = row_top + jnp.log(jnp.sum(jnp.exp(scores - row_top), axis=3, keepdims=True))
    attn_b = jnp.exp(scores - log_total).astype(jnp.bfloat16)
    context = jnp.einsum("bhqk,bkhd->bqhd", attn_b, values_b, preferred_element_type=jnp.float32)
    context_b = context.astype(jnp.bfloat16).reshape(tok_count, head_count * DH)
    return (queries, keys_b, values_b, log_total, context_b, projected)


def attend_back(queries, keys_b, values_b, log_total, context_b, context_grad, images):
    tok_count = context_b.shape[0]
    head_count = queries.shape[2]
    factor = DH ** (-0.5)
    scores = (
        jnp.einsum("bqhd,bkhd->bhqk", queries, keys_b, preferred_element_type=jnp.float32) * factor
    )
    attention = jnp.exp(scores - log_total)
    attn_b = attention.astype(jnp.bfloat16)
    grad_ctx = context_grad.reshape(images, SEQ, head_count, DH)
    context_four = context_b.reshape(images, SEQ, head_count, DH)
    value_grad = jnp.einsum("bhqk,bqhd->bkhd", attn_b, grad_ctx, preferred_element_type=jnp.float32)
    attn_grad = jnp.einsum(
        "bqhd,bkhd->bhqk", grad_ctx, values_b, preferred_element_type=jnp.float32
    )
    row_dot = jnp.sum(grad_ctx.astype(jnp.float32) * context_four.astype(jnp.float32), axis=3)
    row_dot = jnp.transpose(row_dot, (0, 2, 1))[:, :, :, None]
    score_grad = (attention * (attn_grad - row_dot) * factor).astype(jnp.bfloat16)
    query_grad = jnp.einsum(
        "bhqk,bkhd->bqhd", score_grad, keys_b, preferred_element_type=jnp.float32
    )
    key_grad = jnp.einsum(
        "bhqk,bqhd->bkhd", score_grad, queries, preferred_element_type=jnp.float32
    )
    stacked = jnp.stack([query_grad, key_grad, value_grad], axis=3)
    return stacked.astype(jnp.bfloat16).reshape(tok_count, head_count * 3 * DH)


def plain_device(
    tokens,
    norm1_gain,
    norm1_shift,
    qkv_weight,
    proj_weight,
    proj_shift,
    norm2_gain,
    norm2_shift,
    router_weight,
    expand_weight,
    expand_shift,
    shrink_weight,
    shrink_shift,
    route_expert,
    route_slot,
    cotangent,
):
    experts = lax.axis_size("expert")
    tensor_count = lax.axis_size("tensor")
    tok_count = tokens.shape[0]
    images = tok_count // SEQ
    capacity = tensor_count * (5 * tok_count // (2 * experts * tensor_count) + 1)
    width = tokens.shape[1]
    token_f = tokens.astype(jnp.float32)
    normed, scaled1, inverse1 = normalize(token_f, norm1_gain, norm1_shift)
    normed_b = normed.astype(jnp.bfloat16)
    queries, keys_b, values_b, log_total, context_b, _ = attend_front(normed_b, qkv_weight, images)
    attn_part = jnp.dot(context_b, proj_weight, preferred_element_type=jnp.float32)
    hidden = token_f + heads_total(attn_part) + proj_shift
    normed2, scaled2, inverse2 = normalize(hidden, norm2_gain, norm2_shift)
    mixed_b = normed2.astype(jnp.bfloat16)
    logits = jnp.dot(mixed_b, router_weight, preferred_element_type=jnp.float32)
    pick_mask = (
        lax.broadcasted_iota(jnp.int32, (tok_count, 2, experts), 2) == route_expert[:, :, None]
    ).astype(jnp.float32)
    chosen = jnp.sum(logits[:, None, :] * pick_mask, axis=2)
    gate_top = jnp.max(chosen, axis=1, keepdims=True)
    lifted = jnp.exp(chosen - gate_top)
    gate_weights = lifted / jnp.sum(lifted, axis=1, keepdims=True)
    targets, owners = route_tables(route_expert, route_slot, experts, capacity)
    buffer = jnp.take(mixed_b, owners // 2, axis=0, mode="fill", fill_value=0).reshape(
        experts, capacity, width
    )
    received = send_rows(buffer).reshape(experts * capacity, width)
    preact = (
        jnp.dot(received, expand_weight[0], preferred_element_type=jnp.float32) + expand_shift[0]
    )
    activ_b = gelu_exact(preact).astype(jnp.bfloat16)
    out_part = jnp.dot(activ_b, shrink_weight[0], preferred_element_type=jnp.float32).reshape(
        experts, capacity, width
    )
    returned = return_rows(out_part, shrink_shift[0]).reshape(experts * capacity, width)
    picked = (
        jnp.take(returned, targets, axis=0, mode="fill", fill_value=0)
        .reshape(tok_count, 2, width)
        .astype(jnp.float32)
    )
    output = hidden + jnp.sum(gate_weights[:, :, None] * picked, axis=1)
    upstream = cotangent.astype(jnp.float32)
    gate_grad = jnp.sum(upstream[:, None, :] * picked, axis=2)
    weighted = (
        (gate_weights[:, :, None] * upstream[:, None, :])
        .astype(jnp.bfloat16)
        .reshape(2 * tok_count, width)
    )
    grad_buffer = jnp.take(weighted, owners, axis=0, mode="fill", fill_value=0).reshape(
        experts, capacity, width
    )
    grad_recv = send_rows(grad_buffer).reshape(experts * capacity, width)
    shrink_g = inner_rows(activ_b, grad_recv)
    sshift_g = jnp.sum(grad_recv.astype(jnp.float32), axis=0)
    pre_grad = outer_cols(grad_recv, shrink_weight[0]) * gelu_slope(preact)
    pre_gradb = pre_grad.astype(jnp.bfloat16)
    expand_g = inner_rows(received, pre_gradb)
    eshift_g = jnp.sum(pre_grad, axis=0)
    rows_part = outer_cols(pre_gradb, expand_weight[0]).reshape(experts, capacity, width)
    back_rows = return_rows(rows_part, 0.0).reshape(experts * capacity, width)
    common = jnp.sum(gate_weights * gate_grad, axis=1, keepdims=True)
    chosen_grad = gate_weights * (gate_grad - common)
    logit_grad = jnp.sum(pick_mask * chosen_grad[:, :, None], axis=1).astype(jnp.bfloat16)
    router_g = inner_rows(mixed_b, logit_grad)
    back_pick = (
        jnp.take(back_rows, targets, axis=0, mode="fill", fill_value=0)
        .reshape(tok_count, 2, width)
        .astype(jnp.float32)
    )
    mixed_grad = jnp.sum(back_pick, axis=1) + outer_cols(logit_grad, router_weight)
    gain2_g = jnp.sum(mixed_grad * scaled2, axis=0)
    shift2_g = jnp.sum(mixed_grad, axis=0)
    hidden_grad = upstream + norm_back(mixed_grad, scaled2, inverse2, norm2_gain)
    pshift_g = jnp.sum(hidden_grad, axis=0)
    hidden_gradb = hidden_grad.astype(jnp.bfloat16)
    proj_g = inner_rows(context_b, hidden_gradb)
    context_grad = outer_cols(hidden_gradb, proj_weight).astype(jnp.bfloat16)
    qkv_gradb = attend_back(queries, keys_b, values_b, log_total, context_b, context_grad, images)
    qkv_g = inner_rows(normed_b, qkv_gradb)
    normed_grad = heads_total(outer_cols(qkv_gradb, qkv_weight))
    gain1_g = jnp.sum(normed_grad * scaled1, axis=0)
    shift1_g = jnp.sum(normed_grad, axis=0)
    tokens_grad = hidden_grad + norm_back(normed_grad, scaled1, inverse1, norm1_gain)
    summed = lax.psum(
        (gain1_g, shift1_g, qkv_g, proj_g, pshift_g, gain2_g, shift2_g, router_g), "expert"
    )
    return (
        output,
        tokens_grad,
        summed[0],
        summed[1],
        summed[2],
        summed[3],
        summed[4],
        summed[5],
        summed[6],
        summed[7],
        expand_g[None],
        eshift_g[None],
        shrink_g[None],
        sshift_g[None],
    )

MESH = pl.DeviceIdType.MESH
F32 = jnp.float32
BF16 = jnp.bfloat16


def place():
    e = lax.axis_index("expert")
    t = lax.axis_index("tensor")
    a = t // 2
    c = t % 2
    return e, t, a, c, (e, 2 * a + 1 - c), (e, 2 * (1 - a) + c)


def greet(devices):
    barrier = pltpu.get_barrier_semaphore()
    for device in devices:
        pl.semaphore_signal(barrier, inc=1, device_id=device, device_id_type=MESH)
    pl.semaphore_wait(barrier, len(devices))


def remote(src, dst, send, recv, device):
    return pltpu.make_async_remote_copy(
        src_ref=src, dst_ref=dst, send_sem=send, recv_sem=recv, device_id=device, device_id_type=MESH
    )


def turns(count):
    far = list(range(count // 2, count))
    near = list(range(1, count // 2))
    order = []
    for i, step in enumerate(far):
        order.append(step)
        if i < len(near):
            order.append(near[i])
    return order


def lanes(index, width):
    return pl.ds(pl.multiple_of(index * width, 128), width)


def call(kernel, outs, scratch, number, args):
    vmem = pl.BlockSpec(memory_space=pltpu.VMEM)
    return pl.pallas_call(
        kernel,
        out_shape=outs,
        in_specs=[vmem] * len(args),
        out_specs=jax.tree.map(lambda _: vmem, outs),
        scratch_shapes=scratch,
        compiler_params=pltpu.CompilerParams(
            collective_id=number, has_side_effects=True, vmem_limit_bytes=48 * 1024 * 1024
        ),
    )(*args)


def tensor_sum_kernel(x, out, got1, part, got2, send, recv):
    e, t, a, c, core, across = place()
    greet([core, across])
    half = x.shape[1] // 2
    mine, other = lanes(c, half), lanes(1 - c, half)
    copy = remote(x.at[:, other], got1, send.at[0], recv.at[0], core)
    copy.start()
    copy.wait()
    part[...] = (x[:, mine].astype(F32) + got1[...].astype(F32)).astype(BF16)
    copy = remote(part, got2, send.at[1], recv.at[1], across)
    copy.start()
    copy.wait()
    out[:, mine] = (part[...].astype(F32) + got2[...].astype(F32)).astype(BF16)
    copy = remote(out.at[:, mine], out.at[:, mine], send.at[2], recv.at[2], core)
    copy.start()
    copy.wait()


def tensor_sum(x, number):
    rows, width = x.shape
    half = pltpu.VMEM((rows, width // 2), BF16)
    sems = pltpu.SemaphoreType.DMA((3,))
    return call(
        tensor_sum_kernel,
        jax.ShapeDtypeStruct((rows, width), BF16),
        [half, half, half, sems, sems],
        number,
        (x,),
    )


def expert_kernel(
    first, second, up_w, up_b, down_w, shift,
    rows_in, grads_in, activ, pre_b, bias_grad, out0, out1,
    part, got1, half1, got2, ready,
    send_far, send_across, send_core, recv,
    send1, recv1, send2, recv2, send3, recv3, send4, recv4, local,
):
    e, t, a, c, core, across = place()
    count = first.shape[0]
    greet([(e ^ d, t) for d in range(1, count)] + [core, across])
    ins, taken, outs = (first, second), (rows_in, grads_in), (out0, out1)
    far = 2 * (1 - a) + c
    near, cross = 2 * a + 1 - c, 2 * (1 - a) + 1 - c
    rows, width = part.shape[2] // 2, part.shape[3] // 2
    mine, other = pl.ds(c * rows, rows), pl.ds((1 - c) * rows, rows)
    left, right = lanes(a, width), lanes(1 - a, width)

    def origin_of(i):
        return e ^ (i // 2 + (i % 2) * (count // 2))

    def far_copy(k, dst):
        return remote(ins[k].at[dst], taken[k].at[e, t], send_far.at[k, dst], recv.at[k, e, t], (dst, t))

    def across_copy(k, origin):
        spot = taken[k].at[origin, t]
        return remote(spot, spot, send_across.at[k, origin], recv.at[k, origin, t], across)

    def core_copy(k, origin, quarter):
        spot = taken[k].at[origin, quarter]
        return remote(spot, spot, send_core.at[k, origin, quarter], recv.at[k, origin, quarter], core)

    def one_copy(k, dst):
        return remote(part.at[k, dst, other], got1.at[k, dst], send1.at[k, dst], recv1.at[k, dst], core)

    def two_copy(k, dst):
        return remote(
            half1.at[k, dst, :, right], got2.at[k, dst], send2.at[k, dst], recv2.at[k, dst], across
        )

    def three_copy(k, dst):
        return remote(ready.at[k, dst], outs[k].at[e, c], send3.at[k, dst], recv3.at[k, e], (dst, t))

    def four_copy(k, origin, side):
        spot = outs[k].at[origin, side]
        return remote(spot, spot, send4.at[k, origin], recv4.at[k, origin], core)

    for d in turns(count):
        for k in range(2):
            far_copy(k, e ^ d).start()
    keeps = [pltpu.make_async_copy(ins[k].at[e], taken[k].at[e, t], local.at[k]) for k in range(2)]
    for keep in keeps:
        keep.start()
    bias_grad[...] = jnp.zeros_like(bias_grad)
    for keep in keeps:
        keep.wait()

    def step(i, carry):
        @pl.when(i < count)
        def _():
            origin = origin_of(i)
            for k in range(2):

                @pl.when(i > 0)
                def _():
                    core_copy(k, origin, t).wait_recv()

                across_copy(k, origin).start()
                core_copy(k, origin, t).start()

        @pl.when((i >= 1) & (i < count + 1))
        def _():
            origin = origin_of(i - 1)
            for k in range(2):
                core_copy(k, origin, far).wait_recv()
                core_copy(k, origin, far).start()

        @pl.when((i >= 2) & (i < count + 2))
        def _():
            origin = origin_of(i - 2)
            for k in range(2):
                core_copy(k, origin, near).wait_recv()
                core_copy(k, origin, cross).wait_recv()
            tokens = rows_in[origin].reshape(2 * rows, 2 * width)
            grads = grads_in[origin].reshape(2 * rows, 2 * width)
            preact = jnp.dot(tokens, up_w[...], preferred_element_type=F32) + up_b[...]
            bell = 0.5 * (1.0 + lax.erf(preact * half_root))
            active = (preact * bell).astype(BF16)
            activ[origin] = active
            part[0, origin] = jnp.dot(active, down_w[...], preferred_element_type=F32).astype(BF16)
            one_copy(0, origin).start()
            slope = bell + preact * jnp.exp(-0.5 * preact * preact) * gauss_peak
            pre_grad = outer_cols(grads, down_w[...]) * slope
            bias_grad[...] += jnp.sum(pre_grad, axis=0, keepdims=True)
            pre_low = pre_grad.astype(BF16)
            pre_b[origin] = pre_low
            part[1, origin] = outer_cols(pre_low, up_w[...]).astype(BF16)
            one_copy(1, origin).start()

        @pl.when((i >= 3) & (i < count + 3))
        def _():
            dst = origin_of(i - 3)
            for k in range(2):
                one_copy(k, dst).wait_recv()
                half1[k, dst] = (
                    part[k, dst, mine].astype(F32) + got1[k, dst].astype(F32)
                ).astype(BF16)
                two_copy(k, dst).start()

        @pl.when(i >= 4)
        def _():
            dst = origin_of(i - 4)
            for k in range(2):
                two_copy(k, dst).wait_recv()
                total = half1[k, dst, :, left].astype(F32) + got2[k, dst].astype(F32)
                if k == 0:
                    total = total + shift[:, left]
                ready[k, dst] = total.astype(BF16)

                @pl.when(i == 4)
                def _():
                    keep = pltpu.make_async_copy(ready.at[k, dst], outs[k].at[e, c], local.at[k])
                    keep.start()
                    keep.wait()
                    four_copy(k, e, c).start()

                @pl.when(i > 4)
                def _():
                    three_copy(k, dst).start()

        return carry

    lax.fori_loop(0, count + 4, step, 0)
    for d in turns(count):
        origin = e ^ d
        for k in range(2):
            spot = outs[k].at[origin, c]
            remote(spot, spot, send4.at[k, origin], recv3.at[k, origin], core).wait_recv()
            four_copy(k, origin, c).start()

    def finish(d, carry):
        origin = e ^ d
        for k in range(2):
            four_copy(k, origin, 1 - c).wait_recv()
            across_copy(k, origin).wait_send()
            core_copy(k, origin, t).wait_send()
            core_copy(k, origin, far).wait_send()
            one_copy(k, origin).wait_send()
            two_copy(k, origin).wait_send()
            four_copy(k, origin, c).wait_send()

            @pl.when(d > 0)
            def _():
                far_copy(k, origin).wait_send()
                three_copy(k, origin).wait_send()

        return carry

    lax.fori_loop(0, count, finish, 0)


def run_experts(first, second, up_w, up_b, down_w, shift, number):
    count, rows, width = first.shape
    hidden = up_w.shape[1]
    taken = jax.ShapeDtypeStruct((count, 4, rows, width), BF16)
    inner = jax.ShapeDtypeStruct((count, 4 * rows, hidden), BF16)
    out = jax.ShapeDtypeStruct((count, 2, 2 * rows, width // 2), BF16)
    dma = pltpu.SemaphoreType.DMA
    full = pltpu.VMEM((2, count, 2 * rows, width), BF16)
    half = pltpu.VMEM((2, count, 2 * rows, width // 2), BF16)
    return call(
        expert_kernel,
        (taken, taken, inner, inner, jax.ShapeDtypeStruct((1, hidden), F32), out, out),
        [pltpu.VMEM((2, count, 4 * rows, width), BF16), full, full, half, half]
        + [dma((2, count)), dma((2, count)), dma((2, count, 4)), dma((2, count, 4))]
        + [dma((2, count))] * 8
        + [dma((2,))],
        number,
        (first, second, up_w, up_b, down_w, shift),
    )


def split(index):
    return index * 192


def unit(size):
    rows = lax.broadcasted_iota(jnp.int32, (size, size), 0)
    columns = lax.broadcasted_iota(jnp.int32, (size, size), 1)
    return jnp.where(rows == columns, 1.0, 0.0).astype(BF16)


def back_kernel(
    ret, bak, spots, route, gates, cot, hid, mixed, router, gain1, gain2, tok, normed, proj, ctx,
    proj_w, qkv_w, received, grad_recv, activ, pre_b,
    out, tok_g, fin, sums, shrink_g, expand_g,
    back_s, back_r, added_s, added_r, gate_s, gate_r, wide_b, hid_g,
    heads, upper, turned, gsrc, got1, part, got2,
    xsum, xgot1, xpart, xgot2, xdone, xgot3, sm, sgot, sq, sgy, sgz,
    bsem, asem, gsem, s1, r1, s2, r2, s3, r3, s4, r4, xsem, tsem, ysem, zsend, zrecv, osem,
):
    e, t, a, c, core, across = place()
    z, y = e // 2, e % 2
    diag = (e, 2 * (1 - a) + 1 - c)
    beside = (2 * z + 1 - y, t)
    deep = got2.shape[1]
    rows, width = tok.shape
    tall = wide_b.shape[0]
    half = width // 2
    block = back_s.shape[1]
    chunks = gsrc.shape[0]
    factor = DH ** (-0.5)
    greet([core, across, diag, beside] + [(2 * lax.rem(z + d, deep) + y, t) for d in range(1, deep)])
    left, right = lanes(a, half), lanes(1 - a, half)
    ymine, yother = lanes(y, half), lanes(1 - y, half)
    cmine, cother = lanes(c, half), lanes(1 - c, half)

    def peers(order=(2, 1, 3)):
        return [lax.rem(z + d, deep) for d in order]

    total_slots = ret.shape[0] * ret.shape[1] * ret.shape[2]
    slots = lax.broadcasted_iota(jnp.int32, (rows, total_slots), 1)
    marks = [jnp.where(slots == spots[:, j : j + 1], 1.0, 0.0).astype(BF16) for j in range(2)]
    ret_all = ret[...].reshape(total_slots, half)
    bak_all = bak[...].reshape(total_slots, half)
    back_here = jnp.dot(marks[0] + marks[1], bak_all, preferred_element_type=F32).astype(BF16)
    picked = [jnp.dot(mark, ret_all, preferred_element_type=F32) for mark in marks]
    g = [gates[:, 0:1], gates[:, 1:2]]
    back_s[1, block - 32 :, :] = jnp.zeros((32, half), BF16)
    added_s[1, block - 32 :, :] = jnp.zeros((32, half), BF16)
    back_s[0] = back_here[:block]
    back_s[1, : rows - block] = back_here[block:]
    back_across = remote(back_s.at[c], back_r.at[c], bsem.at[0], bsem.at[1], across)
    back_across.start()
    cot_half = cot[:, left].astype(F32)
    lane = lax.broadcasted_iota(jnp.int32, (rows, 128), 1)
    dots = [jnp.sum(cot_half * value, axis=1, keepdims=True) for value in picked]
    turned[...] = jnp.zeros_like(turned)
    turned[:rows] = jnp.where(lane == 0, dots[0], jnp.where(lane == 1, dots[1], 0.0))
    gate_s[...] = jnp.transpose(turned[...])[:8]
    gate_across = remote(gate_s, gate_r, gsem.at[0], gsem.at[1], across)
    gate_across.start()
    added_here = (g[0] * picked[0] + g[1] * picked[1]).astype(BF16)
    added_s[0] = added_here[:block]
    added_s[1, : rows - block] = added_here[block:]
    added_across = remote(added_s.at[c], added_r.at[c], asem.at[0], asem.at[1], across)
    added_across.start()
    mixed_row = mixed[...]
    hidden = hid[...]
    centered = hidden - jnp.mean(hidden, axis=1, keepdims=True)
    inverse2 = lax.rsqrt(jnp.mean(centered * centered, axis=1, keepdims=True) + norm_eps)
    scaled2 = centered * inverse2
    wide_b[:rows, left] = back_here
    for i in range(3):
        for j in range(3):
            spot = proj[:, split(i) + DH * j : split(i) + DH * (j + 1)]
            heads[i, j, tall - 16 :] = jnp.zeros((16, DH), BF16)
            heads[i, j, :rows] = spot
        upper[i, tall - 16 :] = jnp.zeros((16, DH), BF16)

    @pl.loop(0, 3)
    def _(i):
        spot = lanes(i, width // 3)
        expand_g[:, spot] = inner_rows(received[...], pre_b[:, spot])

    back_across.wait_recv()
    back_core = remote(back_r.at[c], back_r.at[c], bsem.at[2], bsem.at[3], core)
    back_core.start()
    gate_across.wait_recv()
    gate_sum = gate_s[...] + gate_r[...]
    gate_cols = jnp.transpose(jnp.concatenate([gate_sum] * 16, axis=0))[:rows]
    gate_grad = [gate_cols[:, 0:1], gate_cols[:, 1:2]]
    common = g[0] * gate_grad[0] + g[1] * gate_grad[1]
    experts = lax.broadcasted_iota(jnp.int32, (rows, router.shape[1]), 1)
    logit_grad = (
        jnp.where(experts == route[:, 0:1], g[0] * (gate_grad[0] - common), 0.0)
        + jnp.where(experts == route[:, 1:2], g[1] * (gate_grad[1] - common), 0.0)
    ).astype(BF16)
    sm[1] = inner_rows(logit_grad, mixed_row) * 0.25
    from_router = outer_cols(logit_grad, router[...])
    back_other = remote(back_r.at[1 - c], back_r.at[1 - c], bsem.at[2], bsem.at[3], core)
    back_other.wait_recv()
    wide_b[:block, right] = back_r[0]
    wide_b[block:rows, right] = back_r[1, : rows - block]
    mixed_grad = wide_b[:rows].astype(F32) + from_router
    hidden_grad = cot[...].astype(F32) + norm_back(mixed_grad, scaled2, inverse2, gain2[...])
    hid_g[...] = hidden_grad
    hidden_low = hidden_grad.astype(BF16)
    gsrc[0] = inner_rows(ctx[...], hidden_low).astype(BF16).reshape(gsrc.shape[1:])

    def y_copy(k):
        return remote(gsrc.at[k, :, :, yother], got1.at[k], s1.at[k], r1.at[k], beside)

    def z_copy(k, zz):
        return remote(part.at[k, zz], got2.at[k, z], s2.at[k, zz], r2.at[k, z], (2 * zz + y, t))

    def spread_copy(k, zz):
        spot = fin.at[k, z, :, ymine]
        return remote(spot, spot, s3.at[k, zz], r3.at[k, z], (2 * zz + y, t))

    def pass_copy(k, zz):
        spot = fin.at[k, zz, :, ymine]
        return remote(spot, spot, s4.at[k, zz], r4.at[k, zz], beside)

    def step_two(k):
        y_copy(k).wait_recv()
        part[k] = (gsrc[k, :, :, ymine].astype(F32) + got1[k].astype(F32)).astype(BF16)
        for zz in peers():
            z_copy(k, zz).start()

    def step_three(k):
        value = part[k, z].astype(F32)
        for zz in peers((1, 3, 2)):
            spot = got2.at[k, zz]
            remote(spot, spot, s2.at[k, zz], r2.at[k, zz], beside).wait_recv()
            value = value + got2[k, zz].astype(F32)
        fin[k, z, :, ymine] = value.astype(BF16)
        for zz in peers():
            spread_copy(k, zz).start()
        pass_copy(k, z).start()

    def step_four(k):
        for zz in peers((1, 3, 2)):
            spot = fin.at[k, zz, :, ymine]
            remote(spot, spot, s3.at[k, zz], r3.at[k, zz], beside).wait_recv()
            pass_copy(k, zz).start()

    y_copy(0).start()
    context_grad = outer_cols(hidden_low, proj_w[...]).astype(BF16)
    for i in range(3):
        upper[i, :rows] = context_grad[:, DH * i : DH * (i + 1)]
    sm[0, 2:3] = jnp.sum(hidden_grad, axis=0, keepdims=True) * 0.25
    sm[0, 3:4] = jnp.sum(mixed_grad * scaled2, axis=0, keepdims=True) * 0.25
    sm[0, 4:5] = jnp.sum(mixed_grad, axis=0, keepdims=True) * 0.25
    sm[0, 5:8] = jnp.zeros((3, width), F32)

    span = block
    for i in range(3):
        for image in range(rows // SEQ):
            base = image * SEQ // 16 * 16
            area = pl.ds(base, span)
            spot_k = lax.broadcasted_iota(jnp.int32, (span, 1), 0) + base
            spot_q = lax.broadcasted_iota(jnp.int32, (1, span), 1) + base
            low, high = image * SEQ, (image + 1) * SEQ
            good_k = (spot_k >= low) & (spot_k < high)
            good_q = (spot_q >= low) & (spot_q < high)
            queries, keys_b, values_b = heads[i, 0, area], heads[i, 1, area], heads[i, 2, area]
            up = upper[i, area]
            scores = outer_cols(keys_b, queries) * factor
            scores = jnp.where(good_k, scores, -1e30)
            top = jnp.max(scores, axis=0, keepdims=True)
            weight = jnp.exp(scores - top)
            share = jnp.where(good_q, 1.0 / jnp.sum(weight, axis=0, keepdims=True), 0.0)
            attention = weight * share
            attn_b = attention.astype(BF16)
            value_grad = jnp.dot(attn_b, up, preferred_element_type=F32)
            attn_grad = outer_cols(values_b, up)
            row_dot = jnp.sum(attention * attn_grad, axis=0, keepdims=True)
            score_grad = (attention * (attn_grad - row_dot) * factor).astype(BF16)
            key_grad = jnp.dot(score_grad, queries, preferred_element_type=F32)
            query_grad = inner_rows(score_grad, keys_b)
            for j, value in enumerate((query_grad, key_grad, value_grad)):
                columns = pl.ds(split(i) + DH * j, DH)
                if image == 0:
                    xsum_low = value.astype(BF16)
                    wide_b[base : base + span, columns] = xsum_low
                else:
                    over = (image - 1) * SEQ // 16 * 16 + span - base
                    xsum_low = value.astype(BF16)
                    wide_b[base : base + over, columns] += xsum_low[:over]
                    wide_b[base + over : base + span, columns] = xsum_low[over:]
        mine = wide_b[:rows, split(i) : split(i + 1)]
        gsrc[1 + i] = inner_rows(mine, normed[...]).astype(BF16).reshape(gsrc.shape[1:])
        y_copy(1 + i).start()
        step_two(i)
        if i >= 1:
            step_three(i - 1)
        if i >= 2:
            step_four(i - 2)
    qkv_low = wide_b[:rows, : qkv_w.shape[1]]
    normed_part = outer_cols(qkv_low, qkv_w[...])
    xsum[tall - 16 :] = jnp.zeros((16, width), BF16)
    xsum[:rows] = normed_part.astype(BF16)
    x1 = remote(xsum.at[:, cother], xgot1, xsem.at[0], xsem.at[1], core)
    x1.start()
    token_f = tok[...].astype(F32)
    centered1 = token_f - jnp.mean(token_f, axis=1, keepdims=True)
    inverse1 = lax.rsqrt(jnp.mean(centered1 * centered1, axis=1, keepdims=True) + norm_eps)
    scaled1 = centered1 * inverse1
    sm[0, 0:1] = jnp.sum(normed_part * scaled1, axis=0, keepdims=True)
    sm[0, 1:2] = jnp.sum(normed_part, axis=0, keepdims=True)

    def quarter(aa, cc):
        return sm.at[aa, :, lanes(cc, half)]

    trade = [
        remote(quarter(a, 1 - c), sgot.at[0], tsem.at[0, 0], tsem.at[1, 0], core),
        remote(quarter(1 - a, c), sgot.at[1], tsem.at[0, 1], tsem.at[1, 1], across),
        remote(quarter(1 - a, 1 - c), sgot.at[2], tsem.at[0, 2], tsem.at[1, 2], diag),
    ]
    for copy in trade:
        copy.start()
    x1.wait_recv()
    xpart[...] = (xsum[:, cmine].astype(F32) + xgot1[...].astype(F32)).astype(BF16)
    x2 = remote(xpart, xgot2, xsem.at[2], xsem.at[3], across)
    x2.start()
    step_two(3)
    step_three(2)
    step_four(1)
    for copy in trade:
        copy.wait_recv()
    sq[0] = (sm[a, :, cmine] + sgot[0]) + (sgot[1] + sgot[2])
    small_y = remote(sq.at[0], sgy, ysem.at[0], ysem.at[1], beside)
    small_y.start()

    @pl.loop(0, 3)
    def _(i):
        spot = lanes(i, width // 3)
        shrink_g[:, spot] = inner_rows(activ[...], grad_recv[:, spot])

    step_three(3)
    step_four(2)
    small_y.wait_recv()
    sq[1] = sq[0] + sgy[...]
    small_z = [
        remote(sq.at[1], sgz.at[z], zsend.at[zz], zrecv.at[z], (2 * zz + y, t)) for zz in peers()
    ]
    for copy in small_z:
        copy.start()
    sgz[z] = sq[1]
    step_four(3)
    for zz in peers((1, 3, 2)):
        spot = sgz.at[zz]
        remote(spot, spot, zsend.at[zz], zrecv.at[zz], beside).wait_recv()
    sums[a, :, cmine] = (sgz[0] + sgz[1]) + (sgz[2] + sgz[3])
    here = sums.at[a, :, cmine]
    tell = [
        remote(here, here, osem.at[0, i], osem.at[1, i], device)
        for i, device in enumerate((core, across, diag))
    ]
    for copy in tell:
        copy.start()
    added_across.wait_recv()
    added_core = remote(added_r.at[c], added_r.at[c], asem.at[2], asem.at[3], core)
    added_core.start()
    x2.wait_recv()
    xpart_sum = (xpart[...].astype(F32) + xgot2[...].astype(F32)).astype(BF16)
    xdone[...] = xpart_sum
    x3 = remote(xdone, xgot3, xsem.at[4], xsem.at[5], core)
    x3.start()
    wide_b[:, cmine] = xpart_sum
    added_other = remote(added_r.at[1 - c], added_r.at[1 - c], asem.at[2], asem.at[3], core)
    added_other.wait_recv()
    out[:, left] = hid[:, left] + jnp.concatenate([added_s[0], added_s[1, : rows - block]], 0).astype(F32)
    out[:, right] = hid[:, right] + jnp.concatenate([added_r[0], added_r[1, : rows - block]], 0).astype(F32)
    x3.wait_recv()
    wide_b[:, cother] = xgot3[...]
    normed_grad = wide_b[:rows].astype(F32)
    tok_g[...] = hid_g[...] + norm_back(normed_grad, scaled1, inverse1, gain1[...])
    for k in range(chunks):
        for zz in range(deep):
            spot = fin.at[k, zz, :, yother]
            remote(spot, spot, s4.at[k, zz], r4.at[k, zz], beside).wait_recv()
    for copy, (aa, cc) in zip(tell, ((a, 1 - c), (1 - a, c), (1 - a, 1 - c))):
        copy.wait_recv()
    for copy in trade + tell + small_z:
        copy.wait_send()
    for copy in (
        back_across, back_core, gate_across, added_across, added_core, x1, x2, x3, small_y,
    ):
        copy.wait_send()
    for k in range(chunks):
        y_copy(k).wait_send()
        pass_copy(k, z).wait_send()
        for zz in peers():
            z_copy(k, zz).wait_send()
            spread_copy(k, zz).wait_send()
            pass_copy(k, zz).wait_send()


def run_back(args, number):
    ret, tok, received = args[0], args[11], args[17]
    rows, width = tok.shape
    half = width // 2
    tall = -(-rows // 16) * 16
    block = -(-rows // 32) * 16
    deep = ret.shape[0] // 2
    chunks = 4
    depth = width // chunks // deep
    dma = pltpu.SemaphoreType.DMA

    def low(*shape):
        return pltpu.VMEM(shape, BF16)

    def wide(*shape):
        return pltpu.VMEM(shape, F32)

    token_like = jax.ShapeDtypeStruct((rows, width), F32)
    square = jax.ShapeDtypeStruct((width, width), F32)
    pair = low(2, block, half)
    line = wide(8, 512)
    stage = low(chunks, deep, depth, half)
    quarter = wide(8, half)
    return call(
        back_kernel,
        (
            token_like,
            token_like,
            jax.ShapeDtypeStruct((chunks, deep, depth, width), BF16),
            jax.ShapeDtypeStruct((2, 8, width), F32),
            square,
            square,
        ),
        [pair, pair, pair, pair, line, line, low(tall, width), wide(rows, width)]
        + [low(3, 3, tall, DH), low(3, tall, DH), wide(512, 128)]
        + [low(chunks, deep, depth, width), stage, stage, stage]
        + [low(tall, width)] + [low(tall, half)] * 5
        + [wide(2, 8, width), wide(3, 8, half), wide(2, 8, half), quarter, wide(deep, 8, half)]
        + [dma((4,)), dma((4,)), dma((2,)), dma((chunks,)), dma((chunks,))]
        + [dma((chunks, deep))] * 6
        + [dma((6,)), dma((2, 3)), dma((2,)), dma((deep,)), dma((deep,)), dma((2, 3))],
        number,
        args,
    )


def fast_device(
    tokens,
    norm1_gain,
    norm1_shift,
    qkv_weight,
    proj_weight,
    proj_shift,
    norm2_gain,
    norm2_shift,
    router_weight,
    expand_weight,
    expand_shift,
    shrink_weight,
    shrink_shift,
    route_expert,
    route_slot,
    cotangent,
):
    experts = lax.axis_size("expert")
    tensor_count = lax.axis_size("tensor")
    tensor_index = lax.axis_index("tensor")
    tok_count = tokens.shape[0]
    images = tok_count // SEQ
    capacity = tensor_count * (5 * tok_count // (2 * experts * tensor_count) + 1)
    quarter = -(-capacity // (16 * tensor_count)) * 16
    padded = quarter * tensor_count
    width = tokens.shape[1]
    token_f = tokens.astype(F32)
    normed, scaled1, inverse1 = normalize(token_f, norm1_gain, norm1_shift)
    normed_b = normed.astype(BF16)
    _, _, _, _, context_b, projected = attend_front(normed_b, qkv_weight, images)
    attn_part = jnp.dot(context_b, proj_weight, preferred_element_type=F32).astype(BF16)
    hidden = token_f + tensor_sum(attn_part, 1).astype(F32) + proj_shift
    normed2, scaled2, inverse2 = normalize(hidden, norm2_gain, norm2_shift)
    mixed_b = normed2.astype(BF16)
    logits = jnp.dot(mixed_b, router_weight, preferred_element_type=F32)
    picks = [
        lax.broadcasted_iota(jnp.int32, (tok_count, experts), 1) == route_expert[:, j : j + 1]
        for j in range(2)
    ]
    chosen = [jnp.sum(jnp.where(pick, logits, 0.0), axis=1, keepdims=True) for pick in picks]
    gate_top = jnp.maximum(chosen[0], chosen[1])
    lifted = [jnp.exp(value - gate_top) for value in chosen]
    gates = [value / (lifted[0] + lifted[1]) for value in lifted]
    spots = jnp.where(route_slot >= 0, route_expert * padded + route_slot, -1)
    spots_t = spots.T
    row_ids = lax.broadcasted_iota(jnp.int32, (experts, quarter, 1), 0) * padded
    row_ids = row_ids + lax.broadcasted_iota(jnp.int32, (experts, quarter, 1), 1)
    row_ids = (row_ids + tensor_index * quarter).reshape(experts * quarter, 1)
    hits = [row_ids == spots_t[j][None, :] for j in range(2)]
    chooser = (hits[0] | hits[1]).astype(BF16)
    slot_gate = jnp.sum(
        jnp.where(hits[0], gates[0].reshape(1, -1), 0.0)
        + jnp.where(hits[1], gates[1].reshape(1, -1), 0.0),
        axis=1,
        keepdims=True,
    )
    rows_out = jnp.dot(chooser, mixed_b, preferred_element_type=F32).astype(BF16)
    grad_out = (slot_gate * jnp.dot(chooser, cotangent, preferred_element_type=F32)).astype(BF16)
    received, grad_recv, activ_b, pre_gradb, eshift_g, returned, back_rows = run_experts(
        rows_out.reshape(experts, quarter, width),
        grad_out.reshape(experts, quarter, width),
        expand_weight[0],
        expand_shift,
        shrink_weight[0],
        shrink_shift,
        2,
    )
    received = received.reshape(experts * padded, width)
    grad_recv = grad_recv.reshape(experts * padded, width)
    activ_b = activ_b.reshape(experts * padded, -1)
    pre_gradb = pre_gradb.reshape(experts * padded, -1)
    sshift_g = jnp.sum(grad_recv.astype(F32), axis=0)
    output, tokens_grad, big, small, shrink_g, expand_g = run_back(
        (
            returned,
            back_rows,
            spots,
            route_expert,
            jnp.concatenate(gates, axis=1),
            cotangent,
            hidden,
            mixed_b,
            router_weight,
            norm1_gain[None],
            norm2_gain[None],
            tokens,
            normed_b,
            projected.reshape(tok_count, -1),
            context_b,
            proj_weight,
            qkv_weight,
            received,
            grad_recv,
            activ_b,
            pre_gradb,
        ),
        4,
    )
    big = big.reshape(width, width)
    split_row = proj_weight.shape[0]
    return (
        output,
        tokens_grad,
        small[0, 0],
        small[0, 1],
        big[split_row:].T.astype(F32),
        big[:split_row].astype(F32),
        small[0, 2],
        small[0, 3],
        small[0, 4],
        small[1].T,
        expand_g[None],
        eshift_g,
        shrink_g[None],
        sshift_g[None],
    )


def solution(mesh):
    small_mesh = mesh.shape["expert"] == 8 and mesh.shape["tensor"] == 4
    on_device = fast_device if small_mesh else plain_device
    return jax.shard_map(
        on_device,
        mesh=mesh,
        in_specs=(
            P("expert", None),
            P(),
            P(),
            P(None, "tensor"),
            P("tensor", None),
            P(),
            P(),
            P(),
            P(),
            P("expert", None, "tensor"),
            P("expert", "tensor"),
            P("expert", "tensor", None),
            P("expert", None),
            P("expert", None),
            P("expert", None),
            P("expert", None),
        ),
        out_specs=(
            P("expert", None),
            P("expert", None),
            P(),
            P(),
            P(None, "tensor"),
            P("tensor", None),
            P(),
            P(),
            P(),
            P(),
            P("expert", None, "tensor"),
            P("expert", "tensor"),
            P("expert", "tensor", None),
            P("expert", None),
        ),
        check_vma=False,
    )
```

```python
import jax
import jax.numpy as jnp
from jax import lax
from jax.experimental import pallas as pl
from jax.experimental.pallas import tpu as pltpu
from jax.sharding import PartitionSpec as P

DH = 64
SEQ = 197


norm_eps = 1e-06
half_root = 0.7071067811865476
gauss_peak = 0.3989422804014327


def normalize(values, norm_gain, norm_shift):
    row_mean = jnp.mean(values, axis=1, keepdims=True)
    centered = values - row_mean
    variance = jnp.mean(centered * centered, axis=1, keepdims=True)
    inverse = lax.rsqrt(variance + norm_eps)
    scaled = centered * inverse
    return (scaled * norm_gain + norm_shift, scaled, inverse)


def norm_back(upstream, scaled, inverse, norm_gain):
    weighted = upstream * norm_gain
    first_mean = jnp.mean(weighted, axis=1, keepdims=True)
    second_mean = jnp.mean(weighted * scaled, axis=1, keepdims=True)
    return inverse * (weighted - first_mean - scaled * second_mean)


def gelu_exact(preact):
    return 0.5 * preact * (1.0 + lax.erf(preact * half_root))


def gelu_slope(preact):
    return (
        0.5 * (1.0 + lax.erf(preact * half_root))
        + preact * jnp.exp(-0.5 * preact * preact) * gauss_peak
    )


def inner_rows(left_b, right_b):
    return lax.dot_general(
        left_b, right_b, (((0,), (0,)), ((), ())), preferred_element_type=jnp.float32
    )


def outer_cols(left_b, right_b):
    return lax.dot_general(
        left_b, right_b, (((1,), (1,)), ((), ())), preferred_element_type=jnp.float32
    )


def route_tables(route_expert, route_slot, experts, capacity):
    tok_count = route_expert.shape[0]
    kept = route_slot >= 0
    targets = jnp.where(kept, route_expert * capacity + route_slot, experts * capacity).reshape(-1)
    numbers = jnp.arange(2 * tok_count, dtype=jnp.int32)
    owners = (
        jnp.full((experts * capacity,), 2 * tok_count, jnp.int32)
        .at[targets]
        .set(numbers, mode="drop")
    )
    return (targets, owners)


def heads_total(partial_value):
    return lax.psum(partial_value.astype(jnp.bfloat16), "tensor").astype(jnp.float32)


def send_rows(buffer):
    return lax.all_to_all(buffer, "expert", split_axis=0, concat_axis=0, tiled=True)


def return_rows(partial_value, offset):
    summed = lax.psum(partial_value.astype(jnp.bfloat16), "tensor").astype(jnp.float32)
    ready = (summed + offset).astype(jnp.bfloat16)
    return lax.all_to_all(ready, "expert", split_axis=0, concat_axis=0, tiled=True)


def attend_front(normed_b, qkv_weight, images):
    tok_count = normed_b.shape[0]
    head_count = qkv_weight.shape[1] // (3 * DH)
    projected = jnp.dot(normed_b, qkv_weight, preferred_element_type=jnp.float32).astype(
        jnp.bfloat16
    )
    projected = projected.reshape(images, SEQ, head_count, 3, DH)
    queries = projected[:, :, :, 0]
    keys_b = projected[:, :, :, 1]
    values_b = projected[:, :, :, 2]
    scores = jnp.einsum(
        "bqhd,bkhd->bhqk", queries, keys_b, preferred_element_type=jnp.float32
    ) * DH ** (-0.5)
    row_top = jnp.max(scores, axis=3, keepdims=True)
    log_total = row_top + jnp.log(jnp.sum(jnp.exp(scores - row_top), axis=3, keepdims=True))
    attn_b = jnp.exp(scores - log_total).astype(jnp.bfloat16)
    context = jnp.einsum("bhqk,bkhd->bqhd", attn_b, values_b, preferred_element_type=jnp.float32)
    context_b = context.astype(jnp.bfloat16).reshape(tok_count, head_count * DH)
    return (queries, keys_b, values_b, log_total, context_b, projected)


def attend_back(queries, keys_b, values_b, log_total, context_b, context_grad, images):
    tok_count = context_b.shape[0]
    head_count = queries.shape[2]
    factor = DH ** (-0.5)
    scores = (
        jnp.einsum("bqhd,bkhd->bhqk", queries, keys_b, preferred_element_type=jnp.float32) * factor
    )
    attention = jnp.exp(scores - log_total)
    attn_b = attention.astype(jnp.bfloat16)
    grad_ctx = context_grad.reshape(images, SEQ, head_count, DH)
    context_four = context_b.reshape(images, SEQ, head_count, DH)
    value_grad = jnp.einsum("bhqk,bqhd->bkhd", attn_b, grad_ctx, preferred_element_type=jnp.float32)
    attn_grad = jnp.einsum(
        "bqhd,bkhd->bhqk", grad_ctx, values_b, preferred_element_type=jnp.float32
    )
    row_dot = jnp.sum(grad_ctx.astype(jnp.float32) * context_four.astype(jnp.float32), axis=3)
    row_dot = jnp.transpose(row_dot, (0, 2, 1))[:, :, :, None]
    score_grad = (attention * (attn_grad - row_dot) * factor).astype(jnp.bfloat16)
    query_grad = jnp.einsum(
        "bhqk,bkhd->bqhd", score_grad, keys_b, preferred_element_type=jnp.float32
    )
    key_grad = jnp.einsum(
        "bhqk,bqhd->bkhd", score_grad, queries, preferred_element_type=jnp.float32
    )
    stacked = jnp.stack([query_grad, key_grad, value_grad], axis=3)
    return stacked.astype(jnp.bfloat16).reshape(tok_count, head_count * 3 * DH)


def plain_device(
    tokens,
    norm1_gain,
    norm1_shift,
    qkv_weight,
    proj_weight,
    proj_shift,
    norm2_gain,
    norm2_shift,
    router_weight,
    expand_weight,
    expand_shift,
    shrink_weight,
    shrink_shift,
    route_expert,
    route_slot,
    cotangent,
):
    experts = lax.axis_size("expert")
    tensor_count = lax.axis_size("tensor")
    tok_count = tokens.shape[0]
    images = tok_count // SEQ
    capacity = tensor_count * (5 * tok_count // (2 * experts * tensor_count) + 1)
    width = tokens.shape[1]
    token_f = tokens.astype(jnp.float32)
    normed, scaled1, inverse1 = normalize(token_f, norm1_gain, norm1_shift)
    normed_b = normed.astype(jnp.bfloat16)
    queries, keys_b, values_b, log_total, context_b, _ = attend_front(normed_b, qkv_weight, images)
    attn_part = jnp.dot(context_b, proj_weight, preferred_element_type=jnp.float32)
    hidden = token_f + heads_total(attn_part) + proj_shift
    normed2, scaled2, inverse2 = normalize(hidden, norm2_gain, norm2_shift)
    mixed_b = normed2.astype(jnp.bfloat16)
    logits = jnp.dot(mixed_b, router_weight, preferred_element_type=jnp.float32)
    pick_mask = (
        lax.broadcasted_iota(jnp.int32, (tok_count, 2, experts), 2) == route_expert[:, :, None]
    ).astype(jnp.float32)
    chosen = jnp.sum(logits[:, None, :] * pick_mask, axis=2)
    gate_top = jnp.max(chosen, axis=1, keepdims=True)
    lifted = jnp.exp(chosen - gate_top)
    gate_weights = lifted / jnp.sum(lifted, axis=1, keepdims=True)
    targets, owners = route_tables(route_expert, route_slot, experts, capacity)
    buffer = jnp.take(mixed_b, owners // 2, axis=0, mode="fill", fill_value=0).reshape(
        experts, capacity, width
    )
    received = send_rows(buffer).reshape(experts * capacity, width)
    preact = (
        jnp.dot(received, expand_weight[0], preferred_element_type=jnp.float32) + expand_shift[0]
    )
    activ_b = gelu_exact(preact).astype(jnp.bfloat16)
    out_part = jnp.dot(activ_b, shrink_weight[0], preferred_element_type=jnp.float32).reshape(
        experts, capacity, width
    )
    returned = return_rows(out_part, shrink_shift[0]).reshape(experts * capacity, width)
    picked = (
        jnp.take(returned, targets, axis=0, mode="fill", fill_value=0)
        .reshape(tok_count, 2, width)
        .astype(jnp.float32)
    )
    output = hidden + jnp.sum(gate_weights[:, :, None] * picked, axis=1)
    upstream = cotangent.astype(jnp.float32)
    gate_grad = jnp.sum(upstream[:, None, :] * picked, axis=2)
    weighted = (
        (gate_weights[:, :, None] * upstream[:, None, :])
        .astype(jnp.bfloat16)
        .reshape(2 * tok_count, width)
    )
    grad_buffer = jnp.take(weighted, owners, axis=0, mode="fill", fill_value=0).reshape(
        experts, capacity, width
    )
    grad_recv = send_rows(grad_buffer).reshape(experts * capacity, width)
    shrink_g = inner_rows(activ_b, grad_recv)
    sshift_g = jnp.sum(grad_recv.astype(jnp.float32), axis=0)
    pre_grad = outer_cols(grad_recv, shrink_weight[0]) * gelu_slope(preact)
    pre_gradb = pre_grad.astype(jnp.bfloat16)
    expand_g = inner_rows(received, pre_gradb)
    eshift_g = jnp.sum(pre_grad, axis=0)
    rows_part = outer_cols(pre_gradb, expand_weight[0]).reshape(experts, capacity, width)
    back_rows = return_rows(rows_part, 0.0).reshape(experts * capacity, width)
    common = jnp.sum(gate_weights * gate_grad, axis=1, keepdims=True)
    chosen_grad = gate_weights * (gate_grad - common)
    logit_grad = jnp.sum(pick_mask * chosen_grad[:, :, None], axis=1).astype(jnp.bfloat16)
    router_g = inner_rows(mixed_b, logit_grad)
    back_pick = (
        jnp.take(back_rows, targets, axis=0, mode="fill", fill_value=0)
        .reshape(tok_count, 2, width)
        .astype(jnp.float32)
    )
    mixed_grad = jnp.sum(back_pick, axis=1) + outer_cols(logit_grad, router_weight)
    gain2_g = jnp.sum(mixed_grad * scaled2, axis=0)
    shift2_g = jnp.sum(mixed_grad, axis=0)
    hidden_grad = upstream + norm_back(mixed_grad, scaled2, inverse2, norm2_gain)
    pshift_g = jnp.sum(hidden_grad, axis=0)
    hidden_gradb = hidden_grad.astype(jnp.bfloat16)
    proj_g = inner_rows(context_b, hidden_gradb)
    context_grad = outer_cols(hidden_gradb, proj_weight).astype(jnp.bfloat16)
    qkv_gradb = attend_back(queries, keys_b, values_b, log_total, context_b, context_grad, images)
    qkv_g = inner_rows(normed_b, qkv_gradb)
    normed_grad = heads_total(outer_cols(qkv_gradb, qkv_weight))
    gain1_g = jnp.sum(normed_grad * scaled1, axis=0)
    shift1_g = jnp.sum(normed_grad, axis=0)
    tokens_grad = hidden_grad + norm_back(normed_grad, scaled1, inverse1, norm1_gain)
    summed = lax.psum(
        (gain1_g, shift1_g, qkv_g, proj_g, pshift_g, gain2_g, shift2_g, router_g), "expert"
    )
    return (
        output,
        tokens_grad,
        summed[0],
        summed[1],
        summed[2],
        summed[3],
        summed[4],
        summed[5],
        summed[6],
        summed[7],
        expand_g[None],
        eshift_g[None],
        shrink_g[None],
        sshift_g[None],
    )

MESH = pl.DeviceIdType.MESH
F32 = jnp.float32
LIMIT = 28
FRONT = 28
BF16 = jnp.bfloat16


def place():
    e = lax.axis_index("expert")
    t = lax.axis_index("tensor")
    a = t // 2
    c = t % 2
    return e, t, a, c, (e, 2 * a + 1 - c), (e, 2 * (1 - a) + c)


def greet(devices):
    barrier = pltpu.get_barrier_semaphore()
    for device in devices:
        pl.semaphore_signal(barrier, inc=1, device_id=device, device_id_type=MESH)
    pl.semaphore_wait(barrier, len(devices))


def remote(src, dst, send, recv, device):
    return pltpu.make_async_remote_copy(
        src_ref=src, dst_ref=dst, send_sem=send, recv_sem=recv, device_id=device, device_id_type=MESH
    )


def turns(count):
    far = list(range(count // 2, count))
    near = list(range(1, count // 2))
    order = []
    for i, step in enumerate(far):
        order.append(step)
        if i < len(near):
            order.append(near[i])
    return order


def lanes(index, width):
    return pl.ds(pl.multiple_of(index * width, 128), width)


def call(kernel, outs, scratch, number, args, outside=False, limit=28):
    vmem = pl.BlockSpec(memory_space=pltpu.VMEM)
    hbm = pl.BlockSpec(memory_space=pltpu.HBM)
    return pl.pallas_call(
        kernel,
        out_shape=outs,
        in_specs=[hbm if outside else vmem] * len(args),
        out_specs=jax.tree.map(lambda _: vmem, outs),
        scratch_shapes=scratch,
        compiler_params=pltpu.CompilerParams(
            collective_id=number, has_side_effects=True, vmem_limit_bytes=limit * 1024 * 1024
        ),
    )(*args)


def front_kernel(
    tok_h, cot_h, experts_h, slots_h, gain1_h, shift1_h, qkv_h, proj_h, proj_shift_h, gain2_h,
    shift2_h, router_h,
    hid, mixed, normed, heads, ctx, cols, marks, rows_out, gate_rows, gains, taken,
    tok, cot, experts_t, slots_t, gain1_v, shift1_v, qkv_t, proj_w, proj_shift_v, gain2_v, shift2_v,
    router_t,
    csend, turned, xsum, xgot1, xpart, xgot2, xdone, xgot3,
    send_far, send_across, send_core, recv, xsem, local, load,
):
    loads = [
        pltpu.make_async_copy(src, dst, load.at[i])
        for i, (src, dst) in enumerate(
            (
                (experts_h, experts_t),
                (slots_h, slots_t),
                (cot_h, cot),
                (tok_h, tok),
                (gain1_h, gain1_v),
                (shift1_h, shift1_v),
                (qkv_h, qkv_t),
                (proj_h, proj_w),
                (proj_shift_h, proj_shift_v),
                (gain2_h, gain2_v),
                (shift2_h, shift2_v),
                (router_h, router_t),
            )
        )
    ]
    for copy in loads:
        copy.start()
    e, t, a, c, core, across = place()
    count, quarter, width = csend.shape
    rows = tok.shape[0]
    tall = xsum.shape[0]
    half = width // 2
    padded = 4 * quarter
    greet([(e ^ d, t) for d in range(1, count)] + [core, across])
    cmine, cother = lanes(c, half), lanes(1 - c, half)
    far, near, cross = 2 * (1 - a) + c, 2 * a + 1 - c, 2 * (1 - a) + 1 - c

    def far_copy(dst):
        return remote(csend.at[dst], taken.at[e, t], send_far.at[dst], recv.at[e, t], (dst, t))

    def across_copy(origin):
        spot = taken.at[origin, t]
        return remote(spot, spot, send_across.at[origin], recv.at[origin, t], across)

    def core_copy(origin, piece):
        spot = taken.at[origin, piece]
        return remote(spot, spot, send_core.at[origin, piece], recv.at[origin, piece], core)

    def forward(d):
        origin = e ^ d
        if d:
            core_copy(origin, t).wait_recv()
        across_copy(origin).start()
        core_copy(origin, t).start()

    for copy in loads[:3]:
        copy.wait()
    spots = [
        jnp.where(slots_t[j : j + 1] >= 0, experts_t[j : j + 1] * padded + slots_t[j : j + 1], -1)
        for j in range(2)
    ]
    ids = lax.broadcasted_iota(jnp.int32, (count * quarter, 1), 0)
    ids = ids // quarter * padded + ids % quarter + t * quarter
    chooser = jnp.where((ids == spots[0]) | (ids == spots[1]), 1.0, 0.0).astype(BF16)
    csend[...] = (
        jnp.dot(chooser, cot[...], preferred_element_type=F32)
        .astype(BF16)
        .reshape(count, quarter, width)
    )
    for d in turns(count):
        far_copy(e ^ d).start()
    keep = pltpu.make_async_copy(csend.at[e], taken.at[e, t], local)
    keep.start()
    for copy in loads[3:]:
        copy.wait()
    gain1, shift1, proj_shift, gain2, shift2 = [
        ref[...].reshape(1, width)
        for ref in (gain1_v, shift1_v, proj_shift_v, gain2_v, shift2_v)
    ]
    token_f = tok[...].astype(F32)
    normed_f, _, _ = normalize(token_f, gain1, shift1)
    normed_b = normed_f.astype(BF16)
    normed[...] = normed_b
    keep.wait()
    forward(0)
    projected = outer_cols(normed_b, qkv_t[...]).astype(BF16)
    head_count = heads.shape[0]
    for i in range(head_count):
        for j in range(3):
            start = DH * (3 * i + j)
            heads[i, j, tall - 16 :] = jnp.zeros((16, DH), BF16)
            heads[i, j, :rows] = projected[:, start : start + DH]
    turned[...] = jnp.zeros_like(turned)
    for j in range(2):
        turned[j : j + 1, :rows] = experts_t[j : j + 1].astype(F32)
        turned[2 + j : 3 + j, :rows] = spots[j].astype(F32)
    table = jnp.transpose(turned[...])[:rows]
    span = -(-rows // 32) * 16
    early = (1, 2)
    for i in range(head_count):
        for image in range(rows // SEQ):
            base = image * SEQ // 16 * 16
            area = pl.ds(base, span)
            spot_q = lax.broadcasted_iota(jnp.int32, (span, 1), 0) + base
            spot_k = lax.broadcasted_iota(jnp.int32, (1, span), 1) + base
            low, high = image * SEQ, (image + 1) * SEQ
            good_q = (spot_q >= low) & (spot_q < high)
            good_k = (spot_k >= low) & (spot_k < high)
            scores = outer_cols(heads[i, 0, area], heads[i, 1, area]) * DH ** (-0.5)
            scores = jnp.where(good_k, scores, -1e30)
            weight = jnp.exp(scores - jnp.max(scores, axis=1, keepdims=True))
            share = jnp.where(good_q, 1.0 / jnp.sum(weight, axis=1, keepdims=True), 0.0)
            value = jnp.dot(
                (weight * share).astype(BF16), heads[i, 2, area], preferred_element_type=F32
            ).astype(BF16)
            columns = pl.ds(DH * i, DH)
            if image == 0:
                ctx[base : base + span, columns] = value
            else:
                over = (image - 1) * SEQ // 16 * 16 + span - base
                ctx[base : base + over, columns] += value[:over]
                ctx[base + over : base + span, columns] = value[over:]
        if i:
            forward(early[i - 1])
    xsum[...] = jnp.dot(ctx[...], proj_w[...], preferred_element_type=F32).astype(BF16)
    x1 = remote(xsum.at[:, cother], xgot1, xsem.at[0], xsem.at[1], core)
    x1.start()
    slots = lax.broadcasted_iota(jnp.int32, (rows, count * padded), 1)
    for j in range(2):
        hit = slots == table[:, 2 + j : 3 + j].astype(jnp.int32)
        marks[j] = jnp.where(hit, 1.0, 0.0).astype(BF16)
    x1.wait_recv()
    xpart[...] = (xsum[:, cmine].astype(F32) + xgot1[...].astype(F32)).astype(BF16)
    x2 = remote(xpart, xgot2, xsem.at[2], xsem.at[3], across)
    x2.start()
    for d in (3, 4, 5, 6, 7):
        forward(d)
    x2.wait_recv()
    xdone[...] = (xpart[...].astype(F32) + xgot2[...].astype(F32)).astype(BF16)
    x3 = remote(xdone, xgot3, xsem.at[4], xsem.at[5], core)
    x3.start()
    hid[:, cmine] = tok[:, cmine].astype(F32) + xdone[:rows].astype(F32)
    x3.wait_recv()
    hid[:, cother] = tok[:, cother].astype(F32) + xgot3[:rows].astype(F32)
    hidden = hid[...] + proj_shift
    hid[...] = hidden
    gains[0:1] = gain1
    gains[1:2] = gain2
    normed2, _, _ = normalize(hidden, gain2, shift2)
    mixed_b = normed2.astype(BF16)
    mixed[...] = mixed_b
    rows_out[...] = (
        jnp.dot(chooser, mixed_b, preferred_element_type=F32)
        .astype(BF16)
        .reshape(count, quarter, width)
    )
    for d in range(count):
        core_copy(e ^ d, far).wait_recv()
        core_copy(e ^ d, far).start()
    logits = outer_cols(mixed_b, router_t[...])
    names = lax.broadcasted_iota(jnp.int32, logits.shape, 1)
    chosen = [
        jnp.sum(
            jnp.where(names == table[:, j : j + 1].astype(jnp.int32), logits, 0.0),
            axis=1,
            keepdims=True,
        )
        for j in range(2)
    ]
    gate_top = jnp.maximum(chosen[0], chosen[1])
    lifted = [jnp.exp(value - gate_top) for value in chosen]
    gates = [value / (lifted[0] + lifted[1]) for value in lifted]
    lane = lax.broadcasted_iota(jnp.int32, (rows, 128), 1)
    cols[...] = jnp.where(lane == 2, gates[0], jnp.where(lane == 3, gates[1], table))
    for s in range(count):
        block = pl.ds(s * padded, padded)
        both = marks[0, :, block].astype(F32) * gates[0] + marks[1, :, block].astype(F32) * gates[1]
        gate_rows[s] = jnp.broadcast_to(jnp.sum(both, axis=0, keepdims=True), (8, padded))
    for d in range(count):
        origin = e ^ d
        core_copy(origin, near).wait_recv()
        core_copy(origin, cross).wait_recv()
        across_copy(origin).wait_send()
        core_copy(origin, t).wait_send()
        core_copy(origin, far).wait_send()
        if d:
            far_copy(origin).wait_send()
    for copy in (x1, x2, x3):
        copy.wait_send()


def run_front(args, count, quarter, head_count, number):
    rows, width = args[0].shape
    tall = -(-rows // 16) * 16
    half = width // 2
    padded = 4 * quarter
    dma = pltpu.SemaphoreType.DMA

    def shape(kind, *sizes):
        return jax.ShapeDtypeStruct(sizes, kind)

    piece = pltpu.VMEM((tall, half), BF16)
    return call(
        front_kernel,
        (
            shape(F32, rows, width),
            shape(BF16, rows, width),
            shape(BF16, rows, width),
            shape(BF16, head_count, 3, tall, DH),
            shape(BF16, tall, head_count * DH),
            shape(F32, rows, 128),
            shape(BF16, 2, rows, count * padded),
            shape(BF16, count, quarter, width),
            shape(F32, count, 8, padded),
            shape(F32, 8, width),
            shape(BF16, count, 4, quarter, width),
        ),
        [pltpu.VMEM(value.shape, value.dtype) for value in args]
        + [pltpu.VMEM((count, quarter, width), BF16), pltpu.VMEM((128, 512), F32)]
        + [pltpu.VMEM((tall, width), BF16)]
        + [piece] * 5
        + [dma((count,)), dma((count,)), dma((count, 4)), dma((count, 4)), dma((6,)), dma(()), dma((len(args),))],
        number,
        args,
        outside=True,
        limit=FRONT,
    )


def expert_kernel(
    first, raw, gate_rows, up_w, up_b, down_w, shift,
    rows_in, grads_out, activ, pre_b, bias_grad, shift_grad, out0, out1,
    part, got1, half1, got2, ready, gate_got,
    send_far, send_across, send_core, recv, gate_send, gate_recv,
    send1, recv1, send2, recv2, send3, recv3, send4, recv4, local,
):
    e, t, a, c, core, across = place()
    count = first.shape[0]
    greet([(e ^ d, t) for d in range(1, count)] + [core, across])
    outs = (out0, out1)
    far = 2 * (1 - a) + c
    near, cross = 2 * a + 1 - c, 2 * (1 - a) + 1 - c
    rows, width = part.shape[2] // 2, part.shape[3] // 2
    mine, other = pl.ds(c * rows, rows), pl.ds((1 - c) * rows, rows)
    left, right = lanes(a, width), lanes(1 - a, width)

    def origin_of(i):
        return e ^ (i // 2 + (i % 2) * (count // 2))

    def far_copy(dst):
        return remote(first.at[dst], rows_in.at[e, t], send_far.at[dst], recv.at[e, t], (dst, t))

    def gate_copy(dst):
        return remote(gate_rows.at[dst], gate_got.at[e], gate_send.at[dst], gate_recv.at[e], (dst, t))

    def across_copy(origin):
        spot = rows_in.at[origin, t]
        return remote(spot, spot, send_across.at[origin], recv.at[origin, t], across)

    def core_copy(origin, quarter):
        spot = rows_in.at[origin, quarter]
        return remote(spot, spot, send_core.at[origin, quarter], recv.at[origin, quarter], core)

    def one_copy(k, dst):
        return remote(part.at[k, dst, other], got1.at[k, dst], send1.at[k, dst], recv1.at[k, dst], core)

    def two_copy(k, dst):
        return remote(
            half1.at[k, dst, :, right], got2.at[k, dst], send2.at[k, dst], recv2.at[k, dst], across
        )

    def three_copy(k, dst):
        return remote(ready.at[k, dst], outs[k].at[e, c], send3.at[k, dst], recv3.at[k, e], (dst, t))

    def four_copy(k, origin, side):
        spot = outs[k].at[origin, side]
        return remote(spot, spot, send4.at[k, origin], recv4.at[k, origin], core)

    for d in turns(count):
        far_copy(e ^ d).start()
        gate_copy(e ^ d).start()
    keep = pltpu.make_async_copy(first.at[e], rows_in.at[e, t], local.at[0])
    keep.start()
    bias_grad[...] = jnp.zeros_like(bias_grad)
    shift_grad[...] = jnp.zeros_like(shift_grad)
    gate_got[e] = gate_rows[e]
    across_id = lax.broadcasted_iota(jnp.int32, (2 * rows, 2 * rows), 0)
    down_id = lax.broadcasted_iota(jnp.int32, (2 * rows, 2 * rows), 1)
    keep.wait()

    def step(i, carry):
        @pl.when(i < count)
        def _():
            origin = origin_of(i)

            @pl.when(i > 0)
            def _():
                core_copy(origin, t).wait_recv()

            across_copy(origin).start()
            core_copy(origin, t).start()

        @pl.when((i >= 1) & (i < count + 1))
        def _():
            origin = origin_of(i - 1)
            core_copy(origin, far).wait_recv()
            core_copy(origin, far).start()

        @pl.when((i >= 2) & (i < count + 2))
        def _():
            origin = origin_of(i - 2)

            @pl.when(i > 2)
            def _():
                here = gate_got.at[origin]
                remote(here, here, gate_send.at[origin], gate_recv.at[origin], across).wait_recv()

            core_copy(origin, near).wait_recv()
            core_copy(origin, cross).wait_recv()
            tokens = rows_in[origin].reshape(2 * rows, 2 * width)
            gate = jnp.sum(
                jnp.where(across_id == down_id, gate_got[origin, 0:1], 0.0), axis=1, keepdims=True
            )
            grads = (gate * raw[origin].reshape(2 * rows, 2 * width).astype(F32)).astype(BF16)
            grads_out[origin] = grads
            preact = jnp.dot(tokens, up_w[...], preferred_element_type=F32) + up_b[...]
            bell = 0.5 * (1.0 + lax.erf(preact * half_root))
            active = (preact * bell).astype(BF16)
            activ[origin] = active
            part[0, origin] = jnp.dot(active, down_w[...], preferred_element_type=F32).astype(BF16)
            one_copy(0, origin).start()
            slope = bell + preact * jnp.exp(-0.5 * preact * preact) * gauss_peak
            pre_grad = outer_cols(grads, down_w[...]) * slope
            bias_grad[...] += jnp.sum(pre_grad, axis=0, keepdims=True)
            shift_grad[...] += jnp.sum(grads.astype(F32), axis=0, keepdims=True)
            pre_low = pre_grad.astype(BF16)
            pre_b[origin] = pre_low
            part[1, origin] = outer_cols(pre_low, up_w[...]).astype(BF16)
            one_copy(1, origin).start()

        @pl.when((i >= 3) & (i < count + 3))
        def _():
            dst = origin_of(i - 3)
            for k in range(2):
                one_copy(k, dst).wait_recv()
                half1[k, dst] = (
                    part[k, dst, mine].astype(F32) + got1[k, dst].astype(F32)
                ).astype(BF16)
                two_copy(k, dst).start()

        @pl.when(i >= 4)
        def _():
            dst = origin_of(i - 4)
            for k in range(2):
                two_copy(k, dst).wait_recv()
                total = half1[k, dst, :, left].astype(F32) + got2[k, dst].astype(F32)
                if k == 0:
                    total = total + shift[:, left]
                ready[k, dst] = total.astype(BF16)

                @pl.when(i == 4)
                def _():
                    keep = pltpu.make_async_copy(ready.at[k, dst], outs[k].at[e, c], local.at[k])
                    keep.start()
                    keep.wait()
                    four_copy(k, e, c).start()

                @pl.when(i > 4)
                def _():
                    three_copy(k, dst).start()

        return carry

    lax.fori_loop(0, count + 4, step, 0)
    for d in turns(count):
        origin = e ^ d
        for k in range(2):
            spot = outs[k].at[origin, c]
            remote(spot, spot, send4.at[k, origin], recv3.at[k, origin], core).wait_recv()
            four_copy(k, origin, c).start()

    def finish(d, carry):
        origin = e ^ d
        across_copy(origin).wait_send()
        core_copy(origin, t).wait_send()
        core_copy(origin, far).wait_send()

        @pl.when(d > 0)
        def _():
            far_copy(origin).wait_send()
            gate_copy(origin).wait_send()

        for k in range(2):
            four_copy(k, origin, 1 - c).wait_recv()
            one_copy(k, origin).wait_send()
            two_copy(k, origin).wait_send()
            four_copy(k, origin, c).wait_send()

            @pl.when(d > 0)
            def _():
                three_copy(k, origin).wait_send()

        return carry

    lax.fori_loop(0, count, finish, 0)


def run_experts(first, raw, gate_rows, up_w, up_b, down_w, shift, number):
    count, rows, width = first.shape
    hidden = up_w.shape[1]
    taken = jax.ShapeDtypeStruct((count, 4, rows, width), BF16)
    inner = jax.ShapeDtypeStruct((count, 4 * rows, hidden), BF16)
    out = jax.ShapeDtypeStruct((count, 2, 2 * rows, width // 2), BF16)
    dma = pltpu.SemaphoreType.DMA
    full = pltpu.VMEM((2, count, 2 * rows, width), BF16)
    half = pltpu.VMEM((2, count, 2 * rows, width // 2), BF16)
    return call(
        expert_kernel,
        (
            taken,
            jax.ShapeDtypeStruct((count, 4 * rows, width), BF16),
            inner,
            inner,
            jax.ShapeDtypeStruct((1, hidden), F32),
            jax.ShapeDtypeStruct((1, width), F32),
            out,
            out,
        ),
        [pltpu.VMEM((2, count, 4 * rows, width), BF16), full, full, half, half]
        + [pltpu.VMEM((count, 8, 4 * rows), F32)]
        + [dma((count,)), dma((count,)), dma((count, 4)), dma((count, 4)), dma((count,)), dma((count,))]
        + [dma((2, count))] * 8
        + [dma((2,))],
        number,
        (first, raw, gate_rows, up_w, up_b, down_w, shift),
    )


def split(index):
    return index * 192


def back_kernel(
    ret, bak, marks, cols, cot, hid, mixed, router, gains, tok, normed, heads, ctx,
    proj_w, qkv_w, received, grad_recv, activ, pre_b,
    out, tok_g, fin, sums, shrink_g, expand_g,
    back_s, back_r, added_s, added_r, gate_s, gate_r, wide_b, hid_g,
    upper, turned, gsrc, got1, part, got2,
    xsum, xgot1, xpart, xgot2, xdone, xgot3, sm, sgot, sq, sgy, sgz,
    bsem, asem, gsem, s1, r1, s2, r2, s3, r3, s4, r4, xsem, tsem, ysem, zsend, zrecv, osem,
):
    e, t, a, c, core, across = place()
    z, y = e // 2, e % 2
    diag = (e, 2 * (1 - a) + 1 - c)
    beside = (2 * z + 1 - y, t)
    deep = got2.shape[1]
    rows, width = tok.shape
    tall = wide_b.shape[0]
    half = width // 2
    block = back_s.shape[1]
    chunks = gsrc.shape[0]
    factor = DH ** (-0.5)
    greet([core, across, diag, beside] + [(2 * lax.rem(z + d, deep) + y, t) for d in range(1, deep)])
    left, right = lanes(a, half), lanes(1 - a, half)
    ymine, yother = lanes(y, half), lanes(1 - y, half)
    cmine, cother = lanes(c, half), lanes(1 - c, half)

    def peers(order=(2, 1, 3)):
        return [lax.rem(z + d, deep) for d in order]

    total_slots = ret.shape[0] * ret.shape[1] * ret.shape[2]
    ret_all = ret[...].reshape(total_slots, half)
    bak_all = bak[...].reshape(total_slots, half)
    back_here = jnp.dot(marks[0] + marks[1], bak_all, preferred_element_type=F32).astype(BF16)
    picked = [jnp.dot(marks[j], ret_all, preferred_element_type=F32) for j in range(2)]
    route = cols[:, 0:2].astype(jnp.int32)
    g = [cols[:, 2:3], cols[:, 3:4]]
    back_s[1, block - 32 :, :] = jnp.zeros((32, half), BF16)
    added_s[1, block - 32 :, :] = jnp.zeros((32, half), BF16)
    back_s[0] = back_here[:block]
    back_s[1, : rows - block] = back_here[block:]
    back_across = remote(back_s.at[c], back_r.at[c], bsem.at[0], bsem.at[1], across)
    back_across.start()
    cot_half = cot[:, left].astype(F32)
    lane = lax.broadcasted_iota(jnp.int32, (rows, 128), 1)
    dots = [jnp.sum(cot_half * value, axis=1, keepdims=True) for value in picked]
    turned[...] = jnp.zeros_like(turned)
    turned[:rows] = jnp.where(lane == 0, dots[0], jnp.where(lane == 1, dots[1], 0.0))
    gate_s[...] = jnp.transpose(turned[...])[:8]
    gate_across = remote(gate_s, gate_r, gsem.at[0], gsem.at[1], across)
    gate_across.start()
    added_here = (g[0] * picked[0] + g[1] * picked[1]).astype(BF16)
    added_s[0] = added_here[:block]
    added_s[1, : rows - block] = added_here[block:]
    added_across = remote(added_s.at[c], added_r.at[c], asem.at[0], asem.at[1], across)
    added_across.start()
    mixed_row = mixed[...]
    hidden = hid[...]
    centered = hidden - jnp.mean(hidden, axis=1, keepdims=True)
    inverse2 = lax.rsqrt(jnp.mean(centered * centered, axis=1, keepdims=True) + norm_eps)
    scaled2 = centered * inverse2
    wide_b[:rows, left] = back_here
    for i in range(3):
        upper[i, tall - 16 :] = jnp.zeros((16, DH), BF16)

    @pl.loop(0, 3)
    def _(i):
        spot = lanes(i, width // 3)
        expand_g[pl.ds(pl.multiple_of(i * (width // 3), 8), width // 3)] = inner_rows(
            received[:, spot], pre_b[...]
        )

    back_across.wait_recv()
    back_core = remote(back_r.at[c], back_r.at[c], bsem.at[2], bsem.at[3], core)
    back_core.start()
    gate_across.wait_recv()
    gate_sum = gate_s[...] + gate_r[...]
    gate_cols = jnp.transpose(jnp.concatenate([gate_sum] * 16, axis=0))[:rows]
    gate_grad = [gate_cols[:, 0:1], gate_cols[:, 1:2]]
    common = g[0] * gate_grad[0] + g[1] * gate_grad[1]
    experts = lax.broadcasted_iota(jnp.int32, (rows, router.shape[0]), 1)
    logit_grad = (
        jnp.where(experts == route[:, 0:1], g[0] * (gate_grad[0] - common), 0.0)
        + jnp.where(experts == route[:, 1:2], g[1] * (gate_grad[1] - common), 0.0)
    ).astype(BF16)
    sm[1] = inner_rows(logit_grad, mixed_row) * 0.25
    from_router = jnp.dot(logit_grad, router[...], preferred_element_type=F32)
    back_other = remote(back_r.at[1 - c], back_r.at[1 - c], bsem.at[2], bsem.at[3], core)
    back_other.wait_recv()
    wide_b[:block, right] = back_r[0]
    wide_b[block:rows, right] = back_r[1, : rows - block]
    mixed_grad = wide_b[:rows].astype(F32) + from_router
    hidden_grad = cot[...].astype(F32) + norm_back(mixed_grad, scaled2, inverse2, gains[1:2])
    hid_g[...] = hidden_grad
    hidden_low = hidden_grad.astype(BF16)
    gsrc[0] = inner_rows(ctx[:rows], hidden_low).astype(BF16).reshape(gsrc.shape[1:])

    def y_copy(k):
        return remote(gsrc.at[k, :, :, yother], got1.at[k], s1.at[k], r1.at[k], beside)

    def z_copy(k, zz):
        return remote(part.at[k, zz], got2.at[k, z], s2.at[k, zz], r2.at[k, z], (2 * zz + y, t))

    def spread_copy(k, zz):
        spot = fin.at[k, z, :, ymine]
        return remote(spot, spot, s3.at[k, zz], r3.at[k, z], (2 * zz + y, t))

    def pass_copy(k, zz):
        spot = fin.at[k, zz, :, ymine]
        return remote(spot, spot, s4.at[k, zz], r4.at[k, zz], beside)

    def step_two(k):
        y_copy(k).wait_recv()
        part[k] = (gsrc[k, :, :, ymine].astype(F32) + got1[k].astype(F32)).astype(BF16)
        for zz in peers():
            z_copy(k, zz).start()

    def step_three(k):
        value = part[k, z].astype(F32)
        for zz in peers((1, 3, 2)):
            spot = got2.at[k, zz]
            remote(spot, spot, s2.at[k, zz], r2.at[k, zz], beside).wait_recv()
            value = value + got2[k, zz].astype(F32)
        fin[k, z, :, ymine] = value.astype(BF16)
        for zz in peers():
            spread_copy(k, zz).start()
        pass_copy(k, z).start()

    def step_four(k):
        for zz in peers((1, 3, 2)):
            spot = fin.at[k, zz, :, ymine]
            remote(spot, spot, s3.at[k, zz], r3.at[k, zz], beside).wait_recv()
            pass_copy(k, zz).start()

    y_copy(0).start()
    context_grad = outer_cols(hidden_low, proj_w[...]).astype(BF16)
    for i in range(3):
        upper[i, :rows] = context_grad[:, DH * i : DH * (i + 1)]
    sm[0, 2:3] = jnp.sum(hidden_grad, axis=0, keepdims=True) * 0.25
    sm[0, 3:4] = jnp.sum(mixed_grad * scaled2, axis=0, keepdims=True) * 0.25
    sm[0, 4:5] = jnp.sum(mixed_grad, axis=0, keepdims=True) * 0.25
    sm[0, 5:8] = jnp.zeros((3, width), F32)

    span = block
    for i in range(3):
        for image in range(rows // SEQ):
            base = image * SEQ // 16 * 16
            area = pl.ds(base, span)
            spot_k = lax.broadcasted_iota(jnp.int32, (span, 1), 0) + base
            spot_q = lax.broadcasted_iota(jnp.int32, (1, span), 1) + base
            low, high = image * SEQ, (image + 1) * SEQ
            good_k = (spot_k >= low) & (spot_k < high)
            good_q = (spot_q >= low) & (spot_q < high)
            queries, keys_b, values_b = heads[i, 0, area], heads[i, 1, area], heads[i, 2, area]
            up = upper[i, area]
            scores = outer_cols(keys_b, queries) * factor
            scores = jnp.where(good_k, scores, -1e30)
            top = jnp.max(scores, axis=0, keepdims=True)
            weight = jnp.exp(scores - top)
            share = jnp.where(good_q, 1.0 / jnp.sum(weight, axis=0, keepdims=True), 0.0)
            attention = weight * share
            attn_b = attention.astype(BF16)
            value_grad = jnp.dot(attn_b, up, preferred_element_type=F32)
            attn_grad = outer_cols(values_b, up)
            row_dot = jnp.sum(attention * attn_grad, axis=0, keepdims=True)
            score_grad = (attention * (attn_grad - row_dot) * factor).astype(BF16)
            key_grad = jnp.dot(score_grad, queries, preferred_element_type=F32)
            query_grad = inner_rows(score_grad, keys_b)
            for j, value in enumerate((query_grad, key_grad, value_grad)):
                columns = pl.ds(split(i) + DH * j, DH)
                if image == 0:
                    xsum_low = value.astype(BF16)
                    wide_b[base : base + span, columns] = xsum_low
                else:
                    over = (image - 1) * SEQ // 16 * 16 + span - base
                    xsum_low = value.astype(BF16)
                    wide_b[base : base + over, columns] += xsum_low[:over]
                    wide_b[base + over : base + span, columns] = xsum_low[over:]
        mine = wide_b[:rows, split(i) : split(i + 1)]
        gsrc[1 + i] = inner_rows(mine, normed[...]).astype(BF16).reshape(gsrc.shape[1:])
        y_copy(1 + i).start()
        step_two(i)
        if i >= 1:
            step_three(i - 1)
        if i >= 2:
            step_four(i - 2)
    qkv_low = wide_b[:rows, : qkv_w.shape[0]]
    normed_part = jnp.dot(qkv_low, qkv_w[...], preferred_element_type=F32)
    xsum[tall - 16 :] = jnp.zeros((16, width), BF16)
    xsum[:rows] = normed_part.astype(BF16)
    x1 = remote(xsum.at[:, cother], xgot1, xsem.at[0], xsem.at[1], core)
    x1.start()
    token_f = tok[...].astype(F32)
    centered1 = token_f - jnp.mean(token_f, axis=1, keepdims=True)
    inverse1 = lax.rsqrt(jnp.mean(centered1 * centered1, axis=1, keepdims=True) + norm_eps)
    scaled1 = centered1 * inverse1
    sm[0, 0:1] = jnp.sum(normed_part * scaled1, axis=0, keepdims=True)
    sm[0, 1:2] = jnp.sum(normed_part, axis=0, keepdims=True)

    def quarter(aa, cc):
        return sm.at[aa, :, lanes(cc, half)]

    trade = [
        remote(quarter(a, 1 - c), sgot.at[0], tsem.at[0, 0], tsem.at[1, 0], core),
        remote(quarter(1 - a, c), sgot.at[1], tsem.at[0, 1], tsem.at[1, 1], across),
        remote(quarter(1 - a, 1 - c), sgot.at[2], tsem.at[0, 2], tsem.at[1, 2], diag),
    ]
    for copy in trade:
        copy.start()
    x1.wait_recv()
    xpart[...] = (xsum[:, cmine].astype(F32) + xgot1[...].astype(F32)).astype(BF16)
    x2 = remote(xpart, xgot2, xsem.at[2], xsem.at[3], across)
    x2.start()
    step_two(3)
    step_three(2)
    step_four(1)
    for copy in trade:
        copy.wait_recv()
    sq[0] = (sm[a, :, cmine] + sgot[0]) + (sgot[1] + sgot[2])
    small_y = remote(sq.at[0], sgy, ysem.at[0], ysem.at[1], beside)
    small_y.start()

    @pl.loop(0, 3)
    def _(i):
        spot = lanes(i, width // 3)
        shrink_g[pl.ds(pl.multiple_of(i * (width // 3), 8), width // 3)] = inner_rows(
            activ[:, spot], grad_recv[...]
        )

    step_three(3)
    step_four(2)
    small_y.wait_recv()
    sq[1] = sq[0] + sgy[...]
    small_z = [
        remote(sq.at[1], sgz.at[z], zsend.at[zz], zrecv.at[z], (2 * zz + y, t)) for zz in peers()
    ]
    for copy in small_z:
        copy.start()
    sgz[z] = sq[1]
    step_four(3)
    for zz in peers((1, 3, 2)):
        spot = sgz.at[zz]
        remote(spot, spot, zsend.at[zz], zrecv.at[zz], beside).wait_recv()
    sums[a, :, cmine] = (sgz[0] + sgz[1]) + (sgz[2] + sgz[3])
    here = sums.at[a, :, cmine]
    tell = [
        remote(here, here, osem.at[0, i], osem.at[1, i], device)
        for i, device in enumerate((core, across, diag))
    ]
    for copy in tell:
        copy.start()
    added_across.wait_recv()
    added_core = remote(added_r.at[c], added_r.at[c], asem.at[2], asem.at[3], core)
    added_core.start()
    x2.wait_recv()
    xpart_sum = (xpart[...].astype(F32) + xgot2[...].astype(F32)).astype(BF16)
    xdone[...] = xpart_sum
    x3 = remote(xdone, xgot3, xsem.at[4], xsem.at[5], core)
    x3.start()
    wide_b[:, cmine] = xpart_sum
    added_other = remote(added_r.at[1 - c], added_r.at[1 - c], asem.at[2], asem.at[3], core)
    added_other.wait_recv()
    out[:, left] = hid[:, left] + jnp.concatenate([added_s[0], added_s[1, : rows - block]], 0).astype(F32)
    out[:, right] = hid[:, right] + jnp.concatenate([added_r[0], added_r[1, : rows - block]], 0).astype(F32)
    x3.wait_recv()
    wide_b[:, cother] = xgot3[...]
    normed_grad = wide_b[:rows].astype(F32)
    tok_g[...] = hid_g[...] + norm_back(normed_grad, scaled1, inverse1, gains[0:1])
    for k in range(chunks):
        for zz in range(deep):
            spot = fin.at[k, zz, :, yother]
            remote(spot, spot, s4.at[k, zz], r4.at[k, zz], beside).wait_recv()
    for copy, (aa, cc) in zip(tell, ((a, 1 - c), (1 - a, c), (1 - a, 1 - c))):
        copy.wait_recv()
    for copy in trade + tell + small_z:
        copy.wait_send()
    for copy in (
        back_across, back_core, gate_across, added_across, added_core, x1, x2, x3, small_y,
    ):
        copy.wait_send()
    for k in range(chunks):
        y_copy(k).wait_send()
        pass_copy(k, z).wait_send()
        for zz in peers():
            z_copy(k, zz).wait_send()
            spread_copy(k, zz).wait_send()
            pass_copy(k, zz).wait_send()


def run_back(args, number):
    ret, tok = args[0], args[9]
    rows, width = tok.shape
    half = width // 2
    tall = -(-rows // 16) * 16
    block = -(-rows // 32) * 16
    deep = ret.shape[0] // 2
    chunks = 4
    depth = width // chunks // deep
    dma = pltpu.SemaphoreType.DMA

    def low(*shape):
        return pltpu.VMEM(shape, BF16)

    def wide(*shape):
        return pltpu.VMEM(shape, F32)

    token_like = jax.ShapeDtypeStruct((rows, width), F32)
    square = jax.ShapeDtypeStruct((width, width), F32)
    pair = low(2, block, half)
    line = wide(8, 512)
    stage = low(chunks, deep, depth, half)
    quarter = wide(8, half)
    return call(
        back_kernel,
        (
            token_like,
            token_like,
            jax.ShapeDtypeStruct((chunks, deep, depth, width), BF16),
            jax.ShapeDtypeStruct((2, 8, width), F32),
            square,
            square,
        ),
        [pair, pair, pair, pair, line, line, low(tall, width), wide(rows, width)]
        + [low(3, tall, DH), wide(512, 128)]
        + [low(chunks, deep, depth, width), stage, stage, stage]
        + [low(tall, width)] + [low(tall, half)] * 5
        + [wide(2, 8, width), wide(3, 8, half), wide(2, 8, half), quarter, wide(deep, 8, half)]
        + [dma((4,)), dma((4,)), dma((2,)), dma((chunks,)), dma((chunks,))]
        + [dma((chunks, deep))] * 6
        + [dma((6,)), dma((2, 3)), dma((2,)), dma((deep,)), dma((deep,)), dma((2, 3))],
        number,
        args,
    )


def last_kernel(
    out, tok_g, fin, expand_g, shrink_g, eshift, sshift, sums,
    out_h, tok_h, qkv_h, proj_h, expand_h, shrink_h, eshift_h, sshift_h, router_h, *rest,
):
    lines_h, (full, *lines, sem) = rest[:5], rest[5:]
    chunks, deep, depth, width = fin.shape
    cut = deep * depth
    copies = []

    def send(src, dst):
        copy = pltpu.make_async_copy(src, dst, sem.at[len(copies)])
        copy.start()
        copies.append(copy)

    send(expand_g, expand_h)
    send(shrink_g, shrink_h)
    send(out, out_h)
    send(tok_g, tok_h)
    send(eshift, eshift_h)
    send(sshift, sshift_h)
    send(sums.at[1], router_h)
    for i in range(5):
        lines[i][...] = sums[0, i : i + 1].reshape(width)
        send(lines[i], lines_h[i])
    full[...] = fin[...].astype(F32).reshape(chunks * cut, width)
    send(full.at[pl.ds(0, cut)], proj_h)
    send(full.at[pl.ds(cut, (chunks - 1) * cut)], qkv_h)
    for copy in copies:
        copy.wait()


def run_last(args):
    big = args[2]
    chunks, deep, depth, width = big.shape
    cut = deep * depth
    vmem = pl.BlockSpec(memory_space=pltpu.VMEM)
    hbm = pl.BlockSpec(memory_space=pltpu.HBM)

    def shape(*sizes):
        return jax.ShapeDtypeStruct(sizes, F32)

    outs = (
        args[0],
        args[1],
        shape((chunks - 1) * cut, width),
        shape(cut, width),
        args[3],
        args[4],
        args[5],
        args[6],
        shape(8, width),
    ) + (shape(width),) * 5
    outs = tuple(jax.ShapeDtypeStruct(value.shape, F32) for value in outs)
    return pl.pallas_call(
        last_kernel,
        out_shape=outs,
        in_specs=[vmem] * len(args),
        out_specs=(hbm,) * len(outs),
        scratch_shapes=[pltpu.VMEM((chunks * cut, width), F32)]
        + [pltpu.VMEM((width,), F32)] * 5
        + [pltpu.SemaphoreType.DMA((len(outs),))],
        compiler_params=pltpu.CompilerParams(vmem_limit_bytes=LIMIT * 1024 * 1024),
    )(*args)


def fast_device(
    tokens,
    norm1_gain,
    norm1_shift,
    qkv_weight,
    proj_weight,
    proj_shift,
    norm2_gain,
    norm2_shift,
    router_weight,
    expand_weight,
    expand_shift,
    shrink_weight,
    shrink_shift,
    route_expert,
    route_slot,
    cotangent,
):
    experts = lax.axis_size("expert")
    tensor_count = lax.axis_size("tensor")
    tok_count = tokens.shape[0]
    capacity = tensor_count * (5 * tok_count // (2 * experts * tensor_count) + 1)
    quarter = -(-capacity // (16 * tensor_count)) * 16
    padded = quarter * tensor_count
    width = tokens.shape[1]
    qkv_t = qkv_weight.T
    router_t = router_weight.T
    hidden, mixed_b, normed_b, heads, context_b, cols, marks, rows_out, gate_rows, gains, raw = run_front(
        (
            tokens,
            cotangent,
            route_expert.T,
            route_slot.T,
            norm1_gain,
            norm1_shift,
            qkv_t,
            proj_weight,
            proj_shift,
            norm2_gain,
            norm2_shift,
            router_t,
        ),
        experts,
        quarter,
        proj_weight.shape[0] // DH,
        1,
    )
    received, grad_recv, activ_b, pre_gradb, eshift_g, sshift_g, returned, back_rows = run_experts(
        rows_out,
        raw,
        gate_rows,
        expand_weight[0],
        expand_shift,
        shrink_weight[0],
        shrink_shift,
        2,
    )
    output, tokens_grad, big, small, shrink_g, expand_g = run_back(
        (
            returned,
            back_rows,
            marks,
            cols,
            cotangent,
            hidden,
            mixed_b,
            router_t,
            gains,
            tokens,
            normed_b,
            heads,
            context_b,
            proj_weight,
            qkv_t,
            received.reshape(experts * padded, width),
            grad_recv.reshape(experts * padded, width),
            activ_b.reshape(experts * padded, -1),
            pre_gradb.reshape(experts * padded, -1),
        ),
        4,
    )
    (
        output,
        tokens_grad,
        qkv_g,
        proj_g,
        expand_g,
        shrink_g,
        eshift_g,
        sshift_g,
        router_g,
        gain1_g,
        shift1_g,
        pshift_g,
        gain2_g,
        shift2_g,
    ) = run_last((output, tokens_grad, big, expand_g, shrink_g, eshift_g, sshift_g, small))
    return (
        output,
        tokens_grad,
        gain1_g,
        shift1_g,
        qkv_g.T,
        proj_g,
        pshift_g,
        gain2_g,
        shift2_g,
        router_g.T,
        expand_g[None],
        eshift_g,
        shrink_g[None],
        sshift_g,
    )


def solution(mesh):
    small_mesh = mesh.shape["expert"] == 8 and mesh.shape["tensor"] == 4
    on_device = fast_device if small_mesh else plain_device
    return jax.shard_map(
        on_device,
        mesh=mesh,
        in_specs=(
            P("expert", None),
            P(),
            P(),
            P(None, "tensor"),
            P("tensor", None),
            P(),
            P(),
            P(),
            P(),
            P("expert", None, "tensor"),
            P("expert", "tensor"),
            P("expert", "tensor", None),
            P("expert", None),
            P("expert", None),
            P("expert", None),
            P("expert", None),
        ),
        out_specs=(
            P("expert", None),
            P("expert", None),
            P(),
            P(),
            P(None, "tensor"),
            P("tensor", None),
            P(),
            P(),
            P(),
            P(),
            P("expert", None, "tensor"),
            P("expert", "tensor"),
            P("expert", "tensor", None),
            P("expert", None),
        ),
        check_vma=False,
    )
```

```python
import functools

import jax
import jax.numpy as jnp
from jax import lax
from jax.experimental import pallas as pl
from jax.experimental.pallas import tpu as pltpu
from jax.sharding import PartitionSpec as P

DH = 64
SEQ = 197


norm_eps = 1e-06
half_root = 0.7071067811865476
gauss_peak = 0.3989422804014327


def normalize(values, norm_gain, norm_shift):
    row_mean = jnp.mean(values, axis=1, keepdims=True)
    centered = values - row_mean
    variance = jnp.mean(centered * centered, axis=1, keepdims=True)
    inverse = lax.rsqrt(variance + norm_eps)
    scaled = centered * inverse
    return (scaled * norm_gain + norm_shift, scaled, inverse)


def norm_back(upstream, scaled, inverse, norm_gain):
    weighted = upstream * norm_gain
    first_mean = jnp.mean(weighted, axis=1, keepdims=True)
    second_mean = jnp.mean(weighted * scaled, axis=1, keepdims=True)
    return inverse * (weighted - first_mean - scaled * second_mean)


def gelu_exact(preact):
    return 0.5 * preact * (1.0 + lax.erf(preact * half_root))


def gelu_slope(preact):
    return (
        0.5 * (1.0 + lax.erf(preact * half_root))
        + preact * jnp.exp(-0.5 * preact * preact) * gauss_peak
    )


def inner_rows(left_b, right_b):
    return lax.dot_general(
        left_b, right_b, (((0,), (0,)), ((), ())), preferred_element_type=jnp.float32
    )


def outer_cols(left_b, right_b):
    return lax.dot_general(
        left_b, right_b, (((1,), (1,)), ((), ())), preferred_element_type=jnp.float32
    )


def route_tables(route_expert, route_slot, experts, capacity):
    tok_count = route_expert.shape[0]
    kept = route_slot >= 0
    targets = jnp.where(kept, route_expert * capacity + route_slot, experts * capacity).reshape(-1)
    numbers = jnp.arange(2 * tok_count, dtype=jnp.int32)
    owners = (
        jnp.full((experts * capacity,), 2 * tok_count, jnp.int32)
        .at[targets]
        .set(numbers, mode="drop")
    )
    return (targets, owners)


def heads_total(partial_value):
    return lax.psum(partial_value.astype(jnp.bfloat16), "tensor").astype(jnp.float32)


def send_rows(buffer):
    return lax.all_to_all(buffer, "expert", split_axis=0, concat_axis=0, tiled=True)


def return_rows(partial_value, offset):
    summed = lax.psum(partial_value.astype(jnp.bfloat16), "tensor").astype(jnp.float32)
    ready = (summed + offset).astype(jnp.bfloat16)
    return lax.all_to_all(ready, "expert", split_axis=0, concat_axis=0, tiled=True)


def attend_front(normed_b, qkv_weight, images):
    tok_count = normed_b.shape[0]
    head_count = qkv_weight.shape[1] // (3 * DH)
    projected = jnp.dot(normed_b, qkv_weight, preferred_element_type=jnp.float32).astype(
        jnp.bfloat16
    )
    projected = projected.reshape(images, SEQ, head_count, 3, DH)
    queries = projected[:, :, :, 0]
    keys_b = projected[:, :, :, 1]
    values_b = projected[:, :, :, 2]
    scores = jnp.einsum(
        "bqhd,bkhd->bhqk", queries, keys_b, preferred_element_type=jnp.float32
    ) * DH ** (-0.5)
    row_top = jnp.max(scores, axis=3, keepdims=True)
    log_total = row_top + jnp.log(jnp.sum(jnp.exp(scores - row_top), axis=3, keepdims=True))
    attn_b = jnp.exp(scores - log_total).astype(jnp.bfloat16)
    context = jnp.einsum("bhqk,bkhd->bqhd", attn_b, values_b, preferred_element_type=jnp.float32)
    context_b = context.astype(jnp.bfloat16).reshape(tok_count, head_count * DH)
    return (queries, keys_b, values_b, log_total, context_b, projected)


def attend_back(queries, keys_b, values_b, log_total, context_b, context_grad, images):
    tok_count = context_b.shape[0]
    head_count = queries.shape[2]
    factor = DH ** (-0.5)
    scores = (
        jnp.einsum("bqhd,bkhd->bhqk", queries, keys_b, preferred_element_type=jnp.float32) * factor
    )
    attention = jnp.exp(scores - log_total)
    attn_b = attention.astype(jnp.bfloat16)
    grad_ctx = context_grad.reshape(images, SEQ, head_count, DH)
    context_four = context_b.reshape(images, SEQ, head_count, DH)
    value_grad = jnp.einsum("bhqk,bqhd->bkhd", attn_b, grad_ctx, preferred_element_type=jnp.float32)
    attn_grad = jnp.einsum(
        "bqhd,bkhd->bhqk", grad_ctx, values_b, preferred_element_type=jnp.float32
    )
    row_dot = jnp.sum(grad_ctx.astype(jnp.float32) * context_four.astype(jnp.float32), axis=3)
    row_dot = jnp.transpose(row_dot, (0, 2, 1))[:, :, :, None]
    score_grad = (attention * (attn_grad - row_dot) * factor).astype(jnp.bfloat16)
    query_grad = jnp.einsum(
        "bhqk,bkhd->bqhd", score_grad, keys_b, preferred_element_type=jnp.float32
    )
    key_grad = jnp.einsum(
        "bhqk,bqhd->bkhd", score_grad, queries, preferred_element_type=jnp.float32
    )
    stacked = jnp.stack([query_grad, key_grad, value_grad], axis=3)
    return stacked.astype(jnp.bfloat16).reshape(tok_count, head_count * 3 * DH)


def plain_device(
    tokens,
    norm1_gain,
    norm1_shift,
    qkv_weight,
    proj_weight,
    proj_shift,
    norm2_gain,
    norm2_shift,
    router_weight,
    expand_weight,
    expand_shift,
    shrink_weight,
    shrink_shift,
    route_expert,
    route_slot,
    cotangent,
):
    experts = lax.axis_size("expert")
    tensor_count = lax.axis_size("tensor")
    tok_count = tokens.shape[0]
    images = tok_count // SEQ
    capacity = tensor_count * (5 * tok_count // (2 * experts * tensor_count) + 1)
    width = tokens.shape[1]
    token_f = tokens.astype(jnp.float32)
    normed, scaled1, inverse1 = normalize(token_f, norm1_gain, norm1_shift)
    normed_b = normed.astype(jnp.bfloat16)
    queries, keys_b, values_b, log_total, context_b, _ = attend_front(normed_b, qkv_weight, images)
    attn_part = jnp.dot(context_b, proj_weight, preferred_element_type=jnp.float32)
    hidden = token_f + heads_total(attn_part) + proj_shift
    normed2, scaled2, inverse2 = normalize(hidden, norm2_gain, norm2_shift)
    mixed_b = normed2.astype(jnp.bfloat16)
    logits = jnp.dot(mixed_b, router_weight, preferred_element_type=jnp.float32)
    pick_mask = (
        lax.broadcasted_iota(jnp.int32, (tok_count, 2, experts), 2) == route_expert[:, :, None]
    ).astype(jnp.float32)
    chosen = jnp.sum(logits[:, None, :] * pick_mask, axis=2)
    gate_top = jnp.max(chosen, axis=1, keepdims=True)
    lifted = jnp.exp(chosen - gate_top)
    gate_weights = lifted / jnp.sum(lifted, axis=1, keepdims=True)
    targets, owners = route_tables(route_expert, route_slot, experts, capacity)
    buffer = jnp.take(mixed_b, owners // 2, axis=0, mode="fill", fill_value=0).reshape(
        experts, capacity, width
    )
    received = send_rows(buffer).reshape(experts * capacity, width)
    preact = (
        jnp.dot(received, expand_weight[0], preferred_element_type=jnp.float32) + expand_shift[0]
    )
    activ_b = gelu_exact(preact).astype(jnp.bfloat16)
    out_part = jnp.dot(activ_b, shrink_weight[0], preferred_element_type=jnp.float32).reshape(
        experts, capacity, width
    )
    returned = return_rows(out_part, shrink_shift[0]).reshape(experts * capacity, width)
    picked = (
        jnp.take(returned, targets, axis=0, mode="fill", fill_value=0)
        .reshape(tok_count, 2, width)
        .astype(jnp.float32)
    )
    output = hidden + jnp.sum(gate_weights[:, :, None] * picked, axis=1)
    upstream = cotangent.astype(jnp.float32)
    gate_grad = jnp.sum(upstream[:, None, :] * picked, axis=2)
    weighted = (
        (gate_weights[:, :, None] * upstream[:, None, :])
        .astype(jnp.bfloat16)
        .reshape(2 * tok_count, width)
    )
    grad_buffer = jnp.take(weighted, owners, axis=0, mode="fill", fill_value=0).reshape(
        experts, capacity, width
    )
    grad_recv = send_rows(grad_buffer).reshape(experts * capacity, width)
    shrink_g = inner_rows(activ_b, grad_recv)
    sshift_g = jnp.sum(grad_recv.astype(jnp.float32), axis=0)
    pre_grad = outer_cols(grad_recv, shrink_weight[0]) * gelu_slope(preact)
    pre_gradb = pre_grad.astype(jnp.bfloat16)
    expand_g = inner_rows(received, pre_gradb)
    eshift_g = jnp.sum(pre_grad, axis=0)
    rows_part = outer_cols(pre_gradb, expand_weight[0]).reshape(experts, capacity, width)
    back_rows = return_rows(rows_part, 0.0).reshape(experts * capacity, width)
    common = jnp.sum(gate_weights * gate_grad, axis=1, keepdims=True)
    chosen_grad = gate_weights * (gate_grad - common)
    logit_grad = jnp.sum(pick_mask * chosen_grad[:, :, None], axis=1).astype(jnp.bfloat16)
    router_g = inner_rows(mixed_b, logit_grad)
    back_pick = (
        jnp.take(back_rows, targets, axis=0, mode="fill", fill_value=0)
        .reshape(tok_count, 2, width)
        .astype(jnp.float32)
    )
    mixed_grad = jnp.sum(back_pick, axis=1) + outer_cols(logit_grad, router_weight)
    gain2_g = jnp.sum(mixed_grad * scaled2, axis=0)
    shift2_g = jnp.sum(mixed_grad, axis=0)
    hidden_grad = upstream + norm_back(mixed_grad, scaled2, inverse2, norm2_gain)
    pshift_g = jnp.sum(hidden_grad, axis=0)
    hidden_gradb = hidden_grad.astype(jnp.bfloat16)
    proj_g = inner_rows(context_b, hidden_gradb)
    context_grad = outer_cols(hidden_gradb, proj_weight).astype(jnp.bfloat16)
    qkv_gradb = attend_back(queries, keys_b, values_b, log_total, context_b, context_grad, images)
    qkv_g = inner_rows(normed_b, qkv_gradb)
    normed_grad = heads_total(outer_cols(qkv_gradb, qkv_weight))
    gain1_g = jnp.sum(normed_grad * scaled1, axis=0)
    shift1_g = jnp.sum(normed_grad, axis=0)
    tokens_grad = hidden_grad + norm_back(normed_grad, scaled1, inverse1, norm1_gain)
    summed = lax.psum(
        (gain1_g, shift1_g, qkv_g, proj_g, pshift_g, gain2_g, shift2_g, router_g), "expert"
    )
    return (
        output,
        tokens_grad,
        summed[0],
        summed[1],
        summed[2],
        summed[3],
        summed[4],
        summed[5],
        summed[6],
        summed[7],
        expand_g[None],
        eshift_g[None],
        shrink_g[None],
        sshift_g[None],
    )

MESH = pl.DeviceIdType.MESH
F32 = jnp.float32
LIMIT = 57
BF16 = jnp.bfloat16


def place():
    e = lax.axis_index("expert")
    t = lax.axis_index("tensor")
    a = t // 2
    c = t % 2
    return e, t, a, c, (e, 2 * a + 1 - c), (e, 2 * (1 - a) + c)


def greet(devices):
    barrier = pltpu.get_barrier_semaphore()
    for device in devices:
        pl.semaphore_signal(barrier, inc=1, device_id=device, device_id_type=MESH)
    pl.semaphore_wait(barrier, len(devices))


def remote(src, dst, send, recv, device):
    return pltpu.make_async_remote_copy(
        src_ref=src, dst_ref=dst, send_sem=send, recv_sem=recv, device_id=device, device_id_type=MESH
    )


def turns(count):
    far = list(range(count // 2, count))
    near = list(range(1, count // 2))
    order = []
    for i, step in enumerate(far):
        order.append(step)
        if i < len(near):
            order.append(near[i])
    return order


def lanes(index, width):
    return pl.ds(pl.multiple_of(index * width, 128), width)


def front_kernel(
    loads,
    hid, mixed, normed, heads, ctx, cols, marks, rows_out, gate_rows, gains, taken,
    tok, cot, experts_t, slots_t, gain1_v, shift1_v, qkv_t, proj_w, proj_shift_v, gain2_v, shift2_v,
    router_t,
    csend, turned, xsum, xgot1, xpart, xgot2, xdone, xgot3,
    send_far, send_across, send_core, recv, xsem, local,
):
    e, t, a, c, core, across = place()
    count, quarter, width = csend.shape
    rows = tok.shape[0]
    tall = xsum.shape[0]
    half = width // 2
    padded = 4 * quarter
    cmine, cother = lanes(c, half), lanes(1 - c, half)
    far, near, cross = 2 * (1 - a) + c, 2 * a + 1 - c, 2 * (1 - a) + 1 - c

    def far_copy(dst):
        return remote(csend.at[dst], taken.at[e, t], send_far.at[dst], recv.at[e, t], (dst, t))

    def across_copy(origin):
        spot = taken.at[origin, t]
        return remote(spot, spot, send_across.at[origin], recv.at[origin, t], across)

    def core_copy(origin, piece):
        spot = taken.at[origin, piece]
        return remote(spot, spot, send_core.at[origin, piece], recv.at[origin, piece], core)

    def forward(d):
        origin = e ^ d
        if d:
            core_copy(origin, t).wait_recv()
        across_copy(origin).start()
        core_copy(origin, t).start()

    for copy in loads[:3]:
        copy.wait()
    spots = [
        jnp.where(slots_t[j : j + 1] >= 0, experts_t[j : j + 1] * padded + slots_t[j : j + 1], -1)
        for j in range(2)
    ]
    ids = lax.broadcasted_iota(jnp.int32, (count * quarter, 1), 0)
    ids = ids // quarter * padded + ids % quarter + t * quarter
    chooser = jnp.where((ids == spots[0]) | (ids == spots[1]), 1.0, 0.0).astype(BF16)
    csend[...] = (
        jnp.dot(chooser, cot[...], preferred_element_type=F32)
        .astype(BF16)
        .reshape(count, quarter, width)
    )
    for d in turns(count):
        far_copy(e ^ d).start()
    keep = pltpu.make_async_copy(csend.at[e], taken.at[e, t], local)
    keep.start()
    for copy in loads[3:12]:
        copy.wait()
    gain1, shift1, proj_shift, gain2, shift2 = [
        ref[...].reshape(1, width)
        for ref in (gain1_v, shift1_v, proj_shift_v, gain2_v, shift2_v)
    ]
    token_f = tok[...].astype(F32)
    normed_f, _, _ = normalize(token_f, gain1, shift1)
    normed_b = normed_f.astype(BF16)
    normed[...] = normed_b
    keep.wait()
    forward(0)
    projected = outer_cols(normed_b, qkv_t[...]).astype(BF16)
    head_count = heads.shape[0]
    for i in range(head_count):
        for j in range(3):
            start = DH * (3 * i + j)
            heads[i, j, tall - 16 :] = jnp.zeros((16, DH), BF16)
            heads[i, j, :rows] = projected[:, start : start + DH]
    turned[...] = jnp.zeros_like(turned)
    for j in range(2):
        turned[j : j + 1, :rows] = experts_t[j : j + 1].astype(F32)
        turned[2 + j : 3 + j, :rows] = spots[j].astype(F32)
    table = jnp.transpose(turned[...])[:rows]
    span = -(-rows // 32) * 16
    early = (1, 2)
    for i in range(head_count):
        for image in range(rows // SEQ):
            base = image * SEQ // 16 * 16
            area = pl.ds(base, span)
            spot_q = lax.broadcasted_iota(jnp.int32, (span, 1), 0) + base
            spot_k = lax.broadcasted_iota(jnp.int32, (1, span), 1) + base
            low, high = image * SEQ, (image + 1) * SEQ
            good_q = (spot_q >= low) & (spot_q < high)
            good_k = (spot_k >= low) & (spot_k < high)
            scores = outer_cols(heads[i, 0, area], heads[i, 1, area]) * DH ** (-0.5)
            scores = jnp.where(good_k, scores, -1e30)
            weight = jnp.exp(scores - jnp.max(scores, axis=1, keepdims=True))
            share = jnp.where(good_q, 1.0 / jnp.sum(weight, axis=1, keepdims=True), 0.0)
            value = jnp.dot(
                (weight * share).astype(BF16), heads[i, 2, area], preferred_element_type=F32
            ).astype(BF16)
            columns = pl.ds(DH * i, DH)
            if image == 0:
                ctx[base : base + span, columns] = value
            else:
                over = (image - 1) * SEQ // 16 * 16 + span - base
                ctx[base : base + over, columns] += value[:over]
                ctx[base + over : base + span, columns] = value[over:]
        if i:
            forward(early[i - 1])
    xsum[...] = jnp.dot(ctx[...], proj_w[...], preferred_element_type=F32).astype(BF16)
    x1 = remote(xsum.at[:, cother], xgot1, xsem.at[0], xsem.at[1], core)
    x1.start()
    slots = lax.broadcasted_iota(jnp.int32, (rows, count * padded), 1)
    for j in range(2):
        hit = slots == table[:, 2 + j : 3 + j].astype(jnp.int32)
        marks[j] = jnp.where(hit, 1.0, 0.0).astype(BF16)
    x1.wait_recv()
    xpart[...] = (xsum[:, cmine].astype(F32) + xgot1[...].astype(F32)).astype(BF16)
    x2 = remote(xpart, xgot2, xsem.at[2], xsem.at[3], across)
    x2.start()
    for d in (3, 4, 5, 6, 7):
        forward(d)
    x2.wait_recv()
    xdone[...] = (xpart[...].astype(F32) + xgot2[...].astype(F32)).astype(BF16)
    x3 = remote(xdone, xgot3, xsem.at[4], xsem.at[5], core)
    x3.start()
    hid[:, cmine] = tok[:, cmine].astype(F32) + xdone[:rows].astype(F32)
    x3.wait_recv()
    hid[:, cother] = tok[:, cother].astype(F32) + xgot3[:rows].astype(F32)
    hidden = hid[...] + proj_shift
    hid[...] = hidden
    gains[0:1] = gain1
    gains[1:2] = gain2
    normed2, _, _ = normalize(hidden, gain2, shift2)
    mixed_b = normed2.astype(BF16)
    mixed[...] = mixed_b
    rows_out[...] = (
        jnp.dot(chooser, mixed_b, preferred_element_type=F32)
        .astype(BF16)
        .reshape(count, quarter, width)
    )
    for d in range(count):
        core_copy(e ^ d, far).wait_recv()
        core_copy(e ^ d, far).start()
    logits = outer_cols(mixed_b, router_t[...])
    names = lax.broadcasted_iota(jnp.int32, logits.shape, 1)
    chosen = [
        jnp.sum(
            jnp.where(names == table[:, j : j + 1].astype(jnp.int32), logits, 0.0),
            axis=1,
            keepdims=True,
        )
        for j in range(2)
    ]
    gate_top = jnp.maximum(chosen[0], chosen[1])
    lifted = [jnp.exp(value - gate_top) for value in chosen]
    gates = [value / (lifted[0] + lifted[1]) for value in lifted]
    lane = lax.broadcasted_iota(jnp.int32, (rows, 128), 1)
    cols[...] = jnp.where(lane == 2, gates[0], jnp.where(lane == 3, gates[1], table))
    for s in range(count):
        block = pl.ds(s * padded, padded)
        both = marks[0, :, block].astype(F32) * gates[0] + marks[1, :, block].astype(F32) * gates[1]
        gate_rows[s] = jnp.broadcast_to(jnp.sum(both, axis=0, keepdims=True), (8, padded))
    for d in range(count):
        origin = e ^ d
        core_copy(origin, near).wait_recv()
        core_copy(origin, cross).wait_recv()
        across_copy(origin).wait_send()
        core_copy(origin, t).wait_send()
        core_copy(origin, far).wait_send()
        if d:
            far_copy(origin).wait_send()
    for copy in (x1, x2, x3):
        copy.wait_send()


def front_parts(rows, width, count, quarter, head_count):
    tall = -(-rows // 16) * 16
    half = width // 2
    padded = 4 * quarter
    dma = pltpu.SemaphoreType.DMA
    piece = pltpu.VMEM((tall, half), BF16)
    outs = [
        pltpu.VMEM((rows, width), F32),
        pltpu.VMEM((rows, width), BF16),
        pltpu.VMEM((rows, width), BF16),
        pltpu.VMEM((head_count, 3, tall, DH), BF16),
        pltpu.VMEM((tall, head_count * DH), BF16),
        pltpu.VMEM((rows, 128), F32),
        pltpu.VMEM((2, rows, count * padded), BF16),
        pltpu.VMEM((count, quarter, width), BF16),
        pltpu.VMEM((count, 8, padded), F32),
        pltpu.VMEM((8, width), F32),
        pltpu.VMEM((count, 4, quarter, width), BF16),
    ]
    scratch = (
        [pltpu.VMEM((count, quarter, width), BF16), pltpu.VMEM((128, 512), F32)]
        + [pltpu.VMEM((tall, width), BF16)]
        + [piece] * 5
        + [dma((count,)), dma((count,)), dma((count, 4)), dma((count, 4)), dma((6,)), dma(())]
    )
    return outs, scratch


def expert_kernel(
    first, raw, gate_rows, up_w, up_b, down_w, shift,
    rows_in, grads_out, activ, pre_b, bias_grad, shift_grad, out0, out1,
    part, got1, half1, got2, ready, gate_got,
    send_far, send_across, send_core, recv, gate_send, gate_recv,
    send1, recv1, send2, recv2, send3, recv3, send4, recv4, local,
):
    e, t, a, c, core, across = place()
    count = first.shape[0]
    outs = (out0, out1)
    far = 2 * (1 - a) + c
    near, cross = 2 * a + 1 - c, 2 * (1 - a) + 1 - c
    rows, width = part.shape[2] // 2, part.shape[3] // 2
    mine, other = pl.ds(c * rows, rows), pl.ds((1 - c) * rows, rows)
    left, right = lanes(a, width), lanes(1 - a, width)

    def origin_of(i):
        return e ^ (4 * (i // 2 % 2) + 2 * (i // 4) + i % 2)

    def far_copy(dst):
        return remote(first.at[dst], rows_in.at[e, t], send_far.at[dst], recv.at[e, t], (dst, t))

    def gate_copy(dst):
        return remote(gate_rows.at[dst], gate_got.at[e], gate_send.at[dst], gate_recv.at[e], (dst, t))

    def across_copy(origin):
        spot = rows_in.at[origin, t]
        return remote(spot, spot, send_across.at[origin], recv.at[origin, t], across)

    def core_copy(origin, quarter):
        spot = rows_in.at[origin, quarter]
        return remote(spot, spot, send_core.at[origin, quarter], recv.at[origin, quarter], core)

    def one_copy(k, dst):
        return remote(part.at[k, dst, other], got1.at[k, dst], send1.at[k, dst], recv1.at[k, dst], core)

    def two_copy(k, dst):
        return remote(
            half1.at[k, dst, :, right], got2.at[k, dst], send2.at[k, dst], recv2.at[k, dst], across
        )

    def three_copy(k, dst):
        return remote(ready.at[k, dst], outs[k].at[e, c], send3.at[k, dst], recv3.at[k, e], (dst, t))

    def four_copy(k, origin, side):
        spot = outs[k].at[origin, side]
        return remote(spot, spot, send4.at[k, origin], recv4.at[k, origin], core)

    for d in turns(count):
        far_copy(e ^ d).start()
        gate_copy(e ^ d).start()
    keep = pltpu.make_async_copy(first.at[e], rows_in.at[e, t], local.at[0])
    keep.start()
    bias_grad[...] = jnp.zeros_like(bias_grad)
    shift_grad[...] = jnp.zeros_like(shift_grad)
    gate_got[e] = gate_rows[e]
    across_id = lax.broadcasted_iota(jnp.int32, (2 * rows, 2 * rows), 0)
    down_id = lax.broadcasted_iota(jnp.int32, (2 * rows, 2 * rows), 1)
    keep.wait()

    def step(i, carry):
        for j in range(2):

            @pl.when(i < count // 2)
            def _():
                origin = origin_of(2 * i + j)
                if j == 0:

                    @pl.when(i > 0)
                    def _():
                        core_copy(origin, t).wait_recv()

                else:
                    core_copy(origin, t).wait_recv()
                across_copy(origin).start()
                core_copy(origin, t).start()

            @pl.when((i >= 1) & (i < count // 2 + 1))
            def _():
                origin = origin_of(2 * i - 2 + j)
                core_copy(origin, far).wait_recv()
                core_copy(origin, far).start()

        @pl.when((i >= 2) & (i < count + 2))
        def _():
            origin = origin_of(i - 2)

            @pl.when(i > 2)
            def _():
                here = gate_got.at[origin]
                remote(here, here, gate_send.at[origin], gate_recv.at[origin], across).wait_recv()

            core_copy(origin, near).wait_recv()
            core_copy(origin, cross).wait_recv()
            tokens = rows_in[origin].reshape(2 * rows, 2 * width)
            gate = jnp.sum(
                jnp.where(across_id == down_id, gate_got[origin, 0:1], 0.0), axis=1, keepdims=True
            )
            grads = (gate * raw[origin].reshape(2 * rows, 2 * width).astype(F32)).astype(BF16)
            grads_out[origin] = grads
            preact = jnp.dot(tokens, up_w[...], preferred_element_type=F32) + up_b[...]
            bell = 0.5 * (1.0 + lax.erf(preact * half_root))
            active = (preact * bell).astype(BF16)
            activ[origin] = active
            part[0, origin] = jnp.dot(active, down_w[...], preferred_element_type=F32).astype(BF16)
            one_copy(0, origin).start()
            slope = bell + preact * jnp.exp(-0.5 * preact * preact) * gauss_peak
            pre_grad = outer_cols(grads, down_w[...]) * slope
            bias_grad[...] += jnp.sum(pre_grad, axis=0, keepdims=True)
            shift_grad[...] += jnp.sum(grads.astype(F32), axis=0, keepdims=True)
            pre_low = pre_grad.astype(BF16)
            pre_b[origin] = pre_low
            part[1, origin] = outer_cols(pre_low, up_w[...]).astype(BF16)
            one_copy(1, origin).start()

        @pl.when((i >= 3) & (i < count + 3))
        def _():
            dst = origin_of(i - 3)
            for k in range(2):
                one_copy(k, dst).wait_recv()
                half1[k, dst] = (
                    part[k, dst, mine].astype(F32) + got1[k, dst].astype(F32)
                ).astype(BF16)
                two_copy(k, dst).start()

        @pl.when(i >= 5)
        def _():
            dst = origin_of(i - 5)
            for k in range(2):
                two_copy(k, dst).wait_recv()
                total = half1[k, dst, :, left].astype(F32) + got2[k, dst].astype(F32)
                if k == 0:
                    total = total + shift[:, left]
                ready[k, dst] = total.astype(BF16)

                @pl.when(i == 5)
                def _():
                    keep = pltpu.make_async_copy(ready.at[k, dst], outs[k].at[e, c], local.at[k])
                    keep.start()
                    keep.wait()
                    four_copy(k, e, c).start()

                @pl.when(i > 5)
                def _():
                    three_copy(k, dst).start()

        return carry

    lax.fori_loop(0, count + 5, step, 0)
    for d in turns(count):
        origin = e ^ d
        for k in range(2):
            spot = outs[k].at[origin, c]
            remote(spot, spot, send4.at[k, origin], recv3.at[k, origin], core).wait_recv()
            four_copy(k, origin, c).start()

    def finish(d, carry):
        origin = e ^ d
        across_copy(origin).wait_send()
        core_copy(origin, t).wait_send()
        core_copy(origin, far).wait_send()

        @pl.when(d > 0)
        def _():
            far_copy(origin).wait_send()
            gate_copy(origin).wait_send()

        for k in range(2):
            four_copy(k, origin, 1 - c).wait_recv()
            one_copy(k, origin).wait_send()
            two_copy(k, origin).wait_send()
            four_copy(k, origin, c).wait_send()

            @pl.when(d > 0)
            def _():
                three_copy(k, origin).wait_send()

        return carry

    lax.fori_loop(0, count, finish, 0)


def expert_parts(count, rows, width, hidden):
    dma = pltpu.SemaphoreType.DMA
    inner = pltpu.VMEM((count, 4 * rows, hidden), BF16)
    out = pltpu.VMEM((count, 2, 2 * rows, width // 2), BF16)
    full = pltpu.VMEM((2, count, 2 * rows, width), BF16)
    half = pltpu.VMEM((2, count, 2 * rows, width // 2), BF16)
    outs = [
        pltpu.VMEM((count, 4, rows, width), BF16),
        pltpu.VMEM((count, 4 * rows, width), BF16),
        inner,
        inner,
    ]
    scratch = (
        [pltpu.VMEM((2, count, 4 * rows, width), BF16), full, full, half, half]
        + [pltpu.VMEM((count, 8, 4 * rows), F32)]
        + [dma((count,)), dma((count,)), dma((count, 4)), dma((count, 4)), dma((count,)), dma((count,))]
        + [dma((2, count))] * 8
        + [dma((2,))]
    )
    return outs, [out, out], scratch


def split(index):
    return index * 192


def back_kernel(
    ret, bak, marks, cols, cot, hid, mixed, router, gains, tok, normed, heads, ctx,
    proj_w, qkv_w, received, grad_recv, activ, pre_b, leave,
    out, tok_g, fin, sums, shrink_g, expand_g,
    back_s, back_r, added_s, added_r, gate_s, gate_r, wide_b, hid_g,
    upper, turned, gsrc, got1, part, got2,
    xsum, xgot1, xpart, xgot2, xdone, xgot3, sm, sgot, sq, sgy, sgz,
    bsem, asem, gsem, s1, r1, s2, r2, s3, r3, s4, r4, xsem, tsem, ysem, zsend, zrecv, osem,
):
    e, t, a, c, core, across = place()
    z, y = e // 2, e % 2
    diag = (e, 2 * (1 - a) + 1 - c)
    beside = (2 * z + 1 - y, t)
    deep = got2.shape[1]
    rows, width = tok.shape
    tall = wide_b.shape[0]
    half = width // 2
    block = back_s.shape[1]
    chunks = gsrc.shape[0]
    factor = DH ** (-0.5)
    left, right = lanes(a, half), lanes(1 - a, half)
    ymine, yother = lanes(y, half), lanes(1 - y, half)
    cmine, cother = lanes(c, half), lanes(1 - c, half)

    def peers(order=(2, 1, 3)):
        return [lax.rem(z + d, deep) for d in order]

    total_slots = ret.shape[0] * ret.shape[1] * ret.shape[2]
    ret_all = ret[...].reshape(total_slots, half)
    bak_all = bak[...].reshape(total_slots, half)
    back_here = jnp.dot(marks[0] + marks[1], bak_all, preferred_element_type=F32).astype(BF16)
    picked = [jnp.dot(marks[j], ret_all, preferred_element_type=F32) for j in range(2)]
    route = cols[:, 0:2].astype(jnp.int32)
    g = [cols[:, 2:3], cols[:, 3:4]]
    back_s[1, block - 32 :, :] = jnp.zeros((32, half), BF16)
    added_s[1, block - 32 :, :] = jnp.zeros((32, half), BF16)
    back_s[0] = back_here[:block]
    back_s[1, : rows - block] = back_here[block:]
    back_across = remote(back_s.at[c], back_r.at[c], bsem.at[0], bsem.at[1], across)
    back_across.start()
    cot_half = cot[:, left].astype(F32)
    lane = lax.broadcasted_iota(jnp.int32, (rows, 128), 1)
    dots = [jnp.sum(cot_half * value, axis=1, keepdims=True) for value in picked]
    turned[...] = jnp.zeros_like(turned)
    turned[:rows] = jnp.where(lane == 0, dots[0], jnp.where(lane == 1, dots[1], 0.0))
    gate_s[...] = jnp.transpose(turned[...])[:8]
    gate_across = remote(gate_s, gate_r, gsem.at[0], gsem.at[1], across)
    gate_across.start()
    added_here = (g[0] * picked[0] + g[1] * picked[1]).astype(BF16)
    added_s[0] = added_here[:block]
    added_s[1, : rows - block] = added_here[block:]
    added_across = remote(added_s.at[c], added_r.at[c], asem.at[0], asem.at[1], across)
    added_across.start()
    mixed_row = mixed[...]
    hidden = hid[...]
    centered = hidden - jnp.mean(hidden, axis=1, keepdims=True)
    inverse2 = lax.rsqrt(jnp.mean(centered * centered, axis=1, keepdims=True) + norm_eps)
    scaled2 = centered * inverse2
    wide_b[:rows, left] = back_here
    for i in range(3):
        upper[i, tall - 16 :] = jnp.zeros((16, DH), BF16)

    @pl.loop(0, 3)
    def _(i):
        spot = lanes(i, width // 3)
        expand_g[pl.ds(pl.multiple_of(i * (width // 3), 8), width // 3)] = inner_rows(
            received[:, :, :, spot].reshape(total_slots, width // 3),
            pre_b[...].reshape(total_slots, -1),
        )

    leave[0].start()

    back_across.wait_recv()
    back_core = remote(back_r.at[c], back_r.at[c], bsem.at[2], bsem.at[3], core)
    back_core.start()
    gate_across.wait_recv()
    gate_sum = gate_s[...] + gate_r[...]
    gate_cols = jnp.transpose(jnp.concatenate([gate_sum] * 16, axis=0))[:rows]
    gate_grad = [gate_cols[:, 0:1], gate_cols[:, 1:2]]
    common = g[0] * gate_grad[0] + g[1] * gate_grad[1]
    experts = lax.broadcasted_iota(jnp.int32, (rows, router.shape[0]), 1)
    logit_grad = (
        jnp.where(experts == route[:, 0:1], g[0] * (gate_grad[0] - common), 0.0)
        + jnp.where(experts == route[:, 1:2], g[1] * (gate_grad[1] - common), 0.0)
    ).astype(BF16)
    sm[1] = inner_rows(logit_grad, mixed_row) * 0.25
    from_router = jnp.dot(logit_grad, router[...], preferred_element_type=F32)
    back_other = remote(back_r.at[1 - c], back_r.at[1 - c], bsem.at[2], bsem.at[3], core)
    back_other.wait_recv()
    wide_b[:block, right] = back_r[0]
    wide_b[block:rows, right] = back_r[1, : rows - block]
    mixed_grad = wide_b[:rows].astype(F32) + from_router
    hidden_grad = cot[...].astype(F32) + norm_back(mixed_grad, scaled2, inverse2, gains[1:2])
    hid_g[...] = hidden_grad
    hidden_low = hidden_grad.astype(BF16)
    gsrc[0] = inner_rows(ctx[:rows], hidden_low).astype(BF16).reshape(gsrc.shape[1:])

    def y_copy(k):
        return remote(gsrc.at[k, :, :, yother], got1.at[k], s1.at[k], r1.at[k], beside)

    def z_copy(k, zz):
        return remote(part.at[k, zz], got2.at[k, z], s2.at[k, zz], r2.at[k, z], (2 * zz + y, t))

    def spread_copy(k, zz):
        spot = fin.at[k, z, :, ymine]
        return remote(spot, spot, s3.at[k, zz], r3.at[k, z], (2 * zz + y, t))

    def pass_copy(k, zz):
        spot = fin.at[k, zz, :, ymine]
        return remote(spot, spot, s4.at[k, zz], r4.at[k, zz], beside)

    def step_two(k):
        y_copy(k).wait_recv()
        part[k] = (gsrc[k, :, :, ymine].astype(F32) + got1[k].astype(F32)).astype(BF16)
        for zz in peers():
            z_copy(k, zz).start()

    def step_three(k):
        value = part[k, z].astype(F32)
        for zz in peers((1, 3, 2)):
            spot = got2.at[k, zz]
            remote(spot, spot, s2.at[k, zz], r2.at[k, zz], beside).wait_recv()
            value = value + got2[k, zz].astype(F32)
        fin[k, z, :, ymine] = value.astype(BF16)
        for zz in peers():
            spread_copy(k, zz).start()
        pass_copy(k, z).start()

    def step_four(k):
        for zz in peers((1, 3, 2)):
            spot = fin.at[k, zz, :, ymine]
            remote(spot, spot, s3.at[k, zz], r3.at[k, zz], beside).wait_recv()
            pass_copy(k, zz).start()

    y_copy(0).start()
    context_grad = outer_cols(hidden_low, proj_w[...]).astype(BF16)
    for i in range(3):
        upper[i, :rows] = context_grad[:, DH * i : DH * (i + 1)]
    sm[0, 2:3] = jnp.sum(hidden_grad, axis=0, keepdims=True) * 0.25
    sm[0, 3:4] = jnp.sum(mixed_grad * scaled2, axis=0, keepdims=True) * 0.25
    sm[0, 4:5] = jnp.sum(mixed_grad, axis=0, keepdims=True) * 0.25
    sm[0, 5:8] = jnp.zeros((3, width), F32)

    span = block
    for i in range(3):
        for image in range(rows // SEQ):
            base = image * SEQ // 16 * 16
            area = pl.ds(base, span)
            spot_k = lax.broadcasted_iota(jnp.int32, (span, 1), 0) + base
            spot_q = lax.broadcasted_iota(jnp.int32, (1, span), 1) + base
            low, high = image * SEQ, (image + 1) * SEQ
            good_k = (spot_k >= low) & (spot_k < high)
            good_q = (spot_q >= low) & (spot_q < high)
            queries, keys_b, values_b = heads[i, 0, area], heads[i, 1, area], heads[i, 2, area]
            up = upper[i, area]
            scores = outer_cols(keys_b, queries) * factor
            scores = jnp.where(good_k, scores, -1e30)
            top = jnp.max(scores, axis=0, keepdims=True)
            weight = jnp.exp(scores - top)
            share = jnp.where(good_q, 1.0 / jnp.sum(weight, axis=0, keepdims=True), 0.0)
            attention = weight * share
            attn_b = attention.astype(BF16)
            value_grad = jnp.dot(attn_b, up, preferred_element_type=F32)
            attn_grad = outer_cols(values_b, up)
            row_dot = jnp.sum(attention * attn_grad, axis=0, keepdims=True)
            score_grad = (attention * (attn_grad - row_dot) * factor).astype(BF16)
            key_grad = jnp.dot(score_grad, queries, preferred_element_type=F32)
            query_grad = inner_rows(score_grad, keys_b)
            for j, value in enumerate((query_grad, key_grad, value_grad)):
                columns = pl.ds(split(i) + DH * j, DH)
                if image == 0:
                    xsum_low = value.astype(BF16)
                    wide_b[base : base + span, columns] = xsum_low
                else:
                    over = (image - 1) * SEQ // 16 * 16 + span - base
                    xsum_low = value.astype(BF16)
                    wide_b[base : base + over, columns] += xsum_low[:over]
                    wide_b[base + over : base + span, columns] = xsum_low[over:]
        mine = wide_b[:rows, split(i) : split(i + 1)]
        gsrc[1 + i] = inner_rows(mine, normed[...]).astype(BF16).reshape(gsrc.shape[1:])
        y_copy(1 + i).start()
        step_two(i)
        if i >= 1:
            step_three(i - 1)
        if i >= 2:
            step_four(i - 2)
    qkv_low = wide_b[:rows, : qkv_w.shape[0]]
    normed_part = jnp.dot(qkv_low, qkv_w[...], preferred_element_type=F32)
    xsum[tall - 16 :] = jnp.zeros((16, width), BF16)
    xsum[:rows] = normed_part.astype(BF16)
    x1 = remote(xsum.at[:, cother], xgot1, xsem.at[0], xsem.at[1], core)
    x1.start()
    token_f = tok[...].astype(F32)
    centered1 = token_f - jnp.mean(token_f, axis=1, keepdims=True)
    inverse1 = lax.rsqrt(jnp.mean(centered1 * centered1, axis=1, keepdims=True) + norm_eps)
    scaled1 = centered1 * inverse1
    sm[0, 0:1] = jnp.sum(normed_part * scaled1, axis=0, keepdims=True)
    sm[0, 1:2] = jnp.sum(normed_part, axis=0, keepdims=True)

    def quarter(aa, cc):
        return sm.at[aa, :, lanes(cc, half)]

    trade = [
        remote(quarter(a, 1 - c), sgot.at[0], tsem.at[0, 0], tsem.at[1, 0], core),
        remote(quarter(1 - a, c), sgot.at[1], tsem.at[0, 1], tsem.at[1, 1], across),
        remote(quarter(1 - a, 1 - c), sgot.at[2], tsem.at[0, 2], tsem.at[1, 2], diag),
    ]
    for copy in trade:
        copy.start()
    x1.wait_recv()
    xpart[...] = (xsum[:, cmine].astype(F32) + xgot1[...].astype(F32)).astype(BF16)
    x2 = remote(xpart, xgot2, xsem.at[2], xsem.at[3], across)
    x2.start()
    step_two(3)
    step_three(2)
    step_four(1)
    for copy in trade:
        copy.wait_recv()
    sq[0] = (sm[a, :, cmine] + sgot[0]) + (sgot[1] + sgot[2])
    small_y = remote(sq.at[0], sgy, ysem.at[0], ysem.at[1], beside)
    small_y.start()

    @pl.loop(0, 3)
    def _(i):
        spot = lanes(i, width // 3)
        shrink_g[pl.ds(pl.multiple_of(i * (width // 3), 8), width // 3)] = inner_rows(
            activ[:, :, spot].reshape(total_slots, width // 3),
            grad_recv[...].reshape(total_slots, width),
        )

    leave[1].start()

    step_three(3)
    step_four(2)
    small_y.wait_recv()
    sq[1] = sq[0] + sgy[...]
    small_z = [
        remote(sq.at[1], sgz.at[z], zsend.at[zz], zrecv.at[z], (2 * zz + y, t)) for zz in peers()
    ]
    for copy in small_z:
        copy.start()
    sgz[z] = sq[1]
    step_four(3)
    for zz in peers((1, 3, 2)):
        spot = sgz.at[zz]
        remote(spot, spot, zsend.at[zz], zrecv.at[zz], beside).wait_recv()
    sums[a, :, cmine] = (sgz[0] + sgz[1]) + (sgz[2] + sgz[3])
    here = sums.at[a, :, cmine]
    tell = [
        remote(here, here, osem.at[0, i], osem.at[1, i], device)
        for i, device in enumerate((core, across, diag))
    ]
    for copy in tell:
        copy.start()
    added_across.wait_recv()
    added_core = remote(added_r.at[c], added_r.at[c], asem.at[2], asem.at[3], core)
    added_core.start()
    x2.wait_recv()
    xpart_sum = (xpart[...].astype(F32) + xgot2[...].astype(F32)).astype(BF16)
    xdone[...] = xpart_sum
    x3 = remote(xdone, xgot3, xsem.at[4], xsem.at[5], core)
    x3.start()
    wide_b[:, cmine] = xpart_sum
    added_other = remote(added_r.at[1 - c], added_r.at[1 - c], asem.at[2], asem.at[3], core)
    added_other.wait_recv()
    out[:, left] = hid[:, left] + jnp.concatenate([added_s[0], added_s[1, : rows - block]], 0).astype(F32)
    out[:, right] = hid[:, right] + jnp.concatenate([added_r[0], added_r[1, : rows - block]], 0).astype(F32)
    leave[2].start()
    x3.wait_recv()
    wide_b[:, cother] = xgot3[...]
    normed_grad = wide_b[:rows].astype(F32)
    tok_g[...] = hid_g[...] + norm_back(normed_grad, scaled1, inverse1, gains[0:1])
    leave[3].start()
    for k in range(chunks):
        for zz in range(deep):
            spot = fin.at[k, zz, :, yother]
            remote(spot, spot, s4.at[k, zz], r4.at[k, zz], beside).wait_recv()
    for copy, (aa, cc) in zip(tell, ((a, 1 - c), (1 - a, c), (1 - a, 1 - c))):
        copy.wait_recv()
    for copy in trade + tell + small_z:
        copy.wait_send()
    for copy in (
        back_across, back_core, gate_across, added_across, added_core, x1, x2, x3, small_y,
    ):
        copy.wait_send()
    for k in range(chunks):
        y_copy(k).wait_send()
        pass_copy(k, z).wait_send()
        for zz in peers():
            z_copy(k, zz).wait_send()
            spread_copy(k, zz).wait_send()
            pass_copy(k, zz).wait_send()


def back_parts(rows, width, count):
    half = width // 2
    tall = -(-rows // 16) * 16
    block = -(-rows // 32) * 16
    deep = count // 2
    chunks = 4
    depth = width // chunks // deep
    dma = pltpu.SemaphoreType.DMA

    def low(*shape):
        return pltpu.VMEM(shape, BF16)

    def wide(*shape):
        return pltpu.VMEM(shape, F32)

    pair = low(2, block, half)
    line = wide(8, 512)
    stage = low(chunks, deep, depth, half)
    quarter = wide(8, half)
    outs = [wide(rows, width), wide(rows, width), wide(width, width), wide(width, width)]
    scratch = (
        [pair, pair, pair, pair, line, line, low(tall, width), wide(rows, width)]
        + [low(3, tall, DH), wide(512, 128)]
        + [low(chunks, deep, depth, width), stage, stage, stage]
        + [low(tall, width)]
        + [low(tall, half)] * 5
        + [wide(2, 8, width), wide(3, 8, half), wide(2, 8, half), quarter, wide(deep, 8, half)]
        + [dma((4,)), dma((4,)), dma((2,)), dma((chunks,)), dma((chunks,))]
        + [dma((chunks, deep))] * 6
        + [dma((6,)), dma((2, 3)), dma((2,)), dma((deep,)), dma((deep,)), dma((2, 3))]
    )
    return outs, scratch, (chunks, deep, depth, width)


def whole_kernel(counts, *refs):
    groups = []
    at = 0
    for number in counts:
        groups.append(refs[at : at + number])
        at += number
    (
        ins, (out_h, tok_h, shrink_h, expand_h, fin, sums, bias_grad, shift_grad),
        held, front_outs, front_scratch, rows_outs, results, expert_scratch, back_outs,
        back_scratch, (load, save),
    ) = groups
    e, t, a, c, core, across = place()
    loads = [pltpu.make_async_copy(src, dst, load.at[i]) for i, (src, dst) in enumerate(zip(ins, held))]
    for copy in loads:
        copy.start()
    experts = front_outs[8].shape[0]
    greet([(e ^ d, t) for d in range(1, experts)] + [core, across, (e, 2 * (1 - a) + 1 - c)])
    (
        experts_t, slots_t, cot, tok, gain1_v, shift1_v, qkv_t, proj_w, proj_shift_v, gain2_v,
        shift2_v, router_t, up_w, up_b, down_w, shift,
    ) = held
    front_kernel(
        loads, *front_outs,
        tok, cot, experts_t, slots_t, gain1_v, shift1_v, qkv_t, proj_w, proj_shift_v, gain2_v,
        shift2_v, router_t,
        *front_scratch,
    )
    hid, mixed, normed, heads, ctx, cols, marks, rows_out, gate_rows, gains, raw = front_outs
    for copy in loads[12:]:
        copy.wait()
    expert_kernel(
        rows_out, raw, gate_rows, up_w, up_b, down_w, shift,
        *rows_outs, bias_grad, shift_grad, *results, *expert_scratch,
    )
    out, tok_g, shrink_g, expand_g = back_outs
    pairs = ((expand_g, expand_h), (shrink_g, shrink_h), (out, out_h), (tok_g, tok_h))
    leave = [pltpu.make_async_copy(src, dst, save.at[i]) for i, (src, dst) in enumerate(pairs)]
    back_kernel(
        *results, marks, cols, cot, hid, mixed, router_t, gains, tok, normed, heads, ctx,
        proj_w, qkv_t, *rows_outs, leave,
        out, tok_g, fin, sums, shrink_g, expand_g,
        *back_scratch,
    )
    for copy in leave:
        copy.wait()


def run_whole(args, experts, quarter):
    tok = args[3]
    rows, width = tok.shape
    hidden = args[12].shape[1]
    head_count = args[7].shape[0] // DH
    vmem = pl.BlockSpec(memory_space=pltpu.VMEM)
    hbm = pl.BlockSpec(memory_space=pltpu.HBM)
    dma = pltpu.SemaphoreType.DMA
    front_outs, front_scratch = front_parts(rows, width, experts, quarter, head_count)
    rows_outs, results, expert_scratch = expert_parts(experts, quarter, width, hidden)
    back_outs, back_scratch, big = back_parts(rows, width, experts)
    held = [pltpu.VMEM(value.shape, value.dtype) for value in args]
    outs = [jax.ShapeDtypeStruct(value.shape, F32) for value in back_outs]
    outs = outs + [
        jax.ShapeDtypeStruct(big, BF16),
        jax.ShapeDtypeStruct((2, 8, width), F32),
        jax.ShapeDtypeStruct((1, hidden), F32),
        jax.ShapeDtypeStruct((1, width), F32),
    ]
    parts = [
        held, front_outs, front_scratch, rows_outs, results, expert_scratch, back_outs,
        back_scratch, [dma((len(args),)), dma((4,))],
    ]
    counts = [len(args), len(outs)] + [len(part) for part in parts]
    return pl.pallas_call(
        functools.partial(whole_kernel, counts),
        out_shape=tuple(outs),
        in_specs=[hbm] * len(args),
        out_specs=(hbm,) * 4 + (vmem,) * 4,
        scratch_shapes=sum(parts, []),
        compiler_params=pltpu.CompilerParams(
            collective_id=1, has_side_effects=True, vmem_limit_bytes=LIMIT * 1024 * 1024
        ),
    )(*args)


def last_kernel(
    out, tok_g, big, expand_g, shrink_g, eshift, sshift, small,
    out_h, tok_h, qkv_h, proj_h, expand_h, shrink_h, eshift_h, sshift_h, router_h, *rest,
):
    lines_h, (full, fin, sums, *rest) = rest[:5], rest[5:]
    lines, held, (load, sem) = rest[:5], rest[5:11], rest[11:]
    chunks, deep, depth, width = fin.shape
    cut = deep * depth
    plain = (expand_g, shrink_g, out, tok_g, eshift, sshift)
    plain_h = (expand_h, shrink_h, out_h, tok_h, eshift_h, sshift_h)
    takes = [
        pltpu.make_async_copy(src, dst, load.at[i])
        for i, (src, dst) in enumerate(zip((small, big) + plain, (sums, fin) + tuple(held)))
    ]
    for copy in takes:
        copy.start()
    copies = []

    def send(src, dst):
        copy = pltpu.make_async_copy(src, dst, sem.at[len(copies)])
        copy.start()
        copies.append(copy)

    takes[0].wait()
    send(sums.at[1], router_h)
    for i in range(5):
        lines[i][...] = sums[0, i : i + 1].reshape(width)
        send(lines[i], lines_h[i])
    takes[1].wait()
    full[...] = fin[...].astype(F32).reshape(chunks * cut, width)
    send(full.at[pl.ds(0, cut)], proj_h)
    send(full.at[pl.ds(cut, (chunks - 1) * cut)], qkv_h)
    for i, dst in enumerate(plain_h):
        takes[2 + i].wait()
        send(held[i], dst)
    for copy in copies:
        copy.wait()


def run_last(args):
    big = args[2]
    chunks, deep, depth, width = big.shape
    cut = deep * depth
    hbm = pl.BlockSpec(memory_space=pltpu.HBM)

    def shape(*sizes):
        return jax.ShapeDtypeStruct(sizes, F32)

    outs = (
        args[0],
        args[1],
        shape((chunks - 1) * cut, width),
        shape(cut, width),
        args[3],
        args[4],
        args[5],
        args[6],
        shape(8, width),
    ) + (shape(width),) * 5
    outs = tuple(jax.ShapeDtypeStruct(value.shape, F32) for value in outs)
    return pl.pallas_call(
        last_kernel,
        out_shape=outs,
        in_specs=[hbm] * len(args),
        out_specs=(hbm,) * len(outs),
        scratch_shapes=[
            pltpu.VMEM((chunks * cut, width), F32),
            pltpu.VMEM(big.shape, BF16),
            pltpu.VMEM(args[7].shape, F32),
        ]
        + [pltpu.VMEM((width,), F32)] * 5
        + [pltpu.VMEM(args[i].shape, F32) for i in (3, 4, 0, 1, 5, 6)]
        + [pltpu.SemaphoreType.DMA((len(args),))]
        + [pltpu.SemaphoreType.DMA((len(outs),))],
        compiler_params=pltpu.CompilerParams(vmem_limit_bytes=LIMIT * 1024 * 1024),
    )(*args)


def fast_device(
    tokens,
    norm1_gain,
    norm1_shift,
    qkv_weight,
    proj_weight,
    proj_shift,
    norm2_gain,
    norm2_shift,
    router_weight,
    expand_weight,
    expand_shift,
    shrink_weight,
    shrink_shift,
    route_expert,
    route_slot,
    cotangent,
):
    experts = lax.axis_size("expert")
    tensor_count = lax.axis_size("tensor")
    tok_count = tokens.shape[0]
    capacity = tensor_count * (5 * tok_count // (2 * experts * tensor_count) + 1)
    quarter = -(-capacity // (16 * tensor_count)) * 16
    qkv_t = qkv_weight.T
    router_t = router_weight.T
    output, tokens_grad, shrink_g, expand_g, big, small, eshift_g, sshift_g = run_whole(
        (
            route_expert.T,
            route_slot.T,
            cotangent,
            tokens,
            norm1_gain,
            norm1_shift,
            qkv_t,
            proj_weight,
            proj_shift,
            norm2_gain,
            norm2_shift,
            router_t,
            expand_weight[0],
            expand_shift,
            shrink_weight[0],
            shrink_shift,
        ),
        experts,
        quarter,
    )
    (
        output,
        tokens_grad,
        qkv_g,
        proj_g,
        expand_g,
        shrink_g,
        eshift_g,
        sshift_g,
        router_g,
        gain1_g,
        shift1_g,
        pshift_g,
        gain2_g,
        shift2_g,
    ) = run_last((output, tokens_grad, big, expand_g, shrink_g, eshift_g, sshift_g, small))
    return (
        output,
        tokens_grad,
        gain1_g,
        shift1_g,
        qkv_g.T,
        proj_g,
        pshift_g,
        gain2_g,
        shift2_g,
        router_g.T,
        expand_g[None],
        eshift_g,
        shrink_g[None],
        sshift_g,
    )


def solution(mesh):
    small_mesh = mesh.shape["expert"] == 8 and mesh.shape["tensor"] == 4
    on_device = fast_device if small_mesh else plain_device
    return jax.shard_map(
        on_device,
        mesh=mesh,
        in_specs=(
            P("expert", None),
            P(),
            P(),
            P(None, "tensor"),
            P("tensor", None),
            P(),
            P(),
            P(),
            P(),
            P("expert", None, "tensor"),
            P("expert", "tensor"),
            P("expert", "tensor", None),
            P("expert", None),
            P("expert", None),
            P("expert", None),
            P("expert", None),
        ),
        out_specs=(
            P("expert", None),
            P("expert", None),
            P(),
            P(),
            P(None, "tensor"),
            P("tensor", None),
            P(),
            P(),
            P(),
            P(),
            P("expert", None, "tensor"),
            P("expert", "tensor"),
            P("expert", "tensor", None),
            P("expert", None),
        ),
        check_vma=False,
    )
```

```python
import functools

import jax
import jax.numpy as jnp
from jax import lax
from jax.experimental import pallas as pl
from jax.experimental.pallas import tpu as pltpu
from jax.sharding import PartitionSpec as P

DH = 64
SEQ = 197


norm_eps = 1e-06
half_root = 0.7071067811865476
gauss_peak = 0.3989422804014327


def normalize(values, norm_gain, norm_shift):
    row_mean = jnp.mean(values, axis=1, keepdims=True)
    centered = values - row_mean
    variance = jnp.mean(centered * centered, axis=1, keepdims=True)
    inverse = lax.rsqrt(variance + norm_eps)
    scaled = centered * inverse
    return (scaled * norm_gain + norm_shift, scaled, inverse)


def norm_back(upstream, scaled, inverse, norm_gain):
    weighted = upstream * norm_gain
    first_mean = jnp.mean(weighted, axis=1, keepdims=True)
    second_mean = jnp.mean(weighted * scaled, axis=1, keepdims=True)
    return inverse * (weighted - first_mean - scaled * second_mean)


def gelu_exact(preact):
    return 0.5 * preact * (1.0 + lax.erf(preact * half_root))


def gelu_slope(preact):
    return (
        0.5 * (1.0 + lax.erf(preact * half_root))
        + preact * jnp.exp(-0.5 * preact * preact) * gauss_peak
    )


def inner_rows(left_b, right_b):
    return lax.dot_general(
        left_b, right_b, (((0,), (0,)), ((), ())), preferred_element_type=jnp.float32
    )


def outer_cols(left_b, right_b):
    return lax.dot_general(
        left_b, right_b, (((1,), (1,)), ((), ())), preferred_element_type=jnp.float32
    )


def route_tables(route_expert, route_slot, experts, capacity):
    tok_count = route_expert.shape[0]
    kept = route_slot >= 0
    targets = jnp.where(kept, route_expert * capacity + route_slot, experts * capacity).reshape(-1)
    numbers = jnp.arange(2 * tok_count, dtype=jnp.int32)
    owners = (
        jnp.full((experts * capacity,), 2 * tok_count, jnp.int32)
        .at[targets]
        .set(numbers, mode="drop")
    )
    return (targets, owners)


def heads_total(partial_value):
    return lax.psum(partial_value.astype(jnp.bfloat16), "tensor").astype(jnp.float32)


def send_rows(buffer):
    return lax.all_to_all(buffer, "expert", split_axis=0, concat_axis=0, tiled=True)


def return_rows(partial_value, offset):
    summed = lax.psum(partial_value.astype(jnp.bfloat16), "tensor").astype(jnp.float32)
    ready = (summed + offset).astype(jnp.bfloat16)
    return lax.all_to_all(ready, "expert", split_axis=0, concat_axis=0, tiled=True)


def attend_front(normed_b, qkv_weight, images):
    tok_count = normed_b.shape[0]
    head_count = qkv_weight.shape[1] // (3 * DH)
    projected = jnp.dot(normed_b, qkv_weight, preferred_element_type=jnp.float32).astype(
        jnp.bfloat16
    )
    projected = projected.reshape(images, SEQ, head_count, 3, DH)
    queries = projected[:, :, :, 0]
    keys_b = projected[:, :, :, 1]
    values_b = projected[:, :, :, 2]
    scores = jnp.einsum(
        "bqhd,bkhd->bhqk", queries, keys_b, preferred_element_type=jnp.float32
    ) * DH ** (-0.5)
    row_top = jnp.max(scores, axis=3, keepdims=True)
    log_total = row_top + jnp.log(jnp.sum(jnp.exp(scores - row_top), axis=3, keepdims=True))
    attn_b = jnp.exp(scores - log_total).astype(jnp.bfloat16)
    context = jnp.einsum("bhqk,bkhd->bqhd", attn_b, values_b, preferred_element_type=jnp.float32)
    context_b = context.astype(jnp.bfloat16).reshape(tok_count, head_count * DH)
    return (queries, keys_b, values_b, log_total, context_b, projected)


def attend_back(queries, keys_b, values_b, log_total, context_b, context_grad, images):
    tok_count = context_b.shape[0]
    head_count = queries.shape[2]
    factor = DH ** (-0.5)
    scores = (
        jnp.einsum("bqhd,bkhd->bhqk", queries, keys_b, preferred_element_type=jnp.float32) * factor
    )
    attention = jnp.exp(scores - log_total)
    attn_b = attention.astype(jnp.bfloat16)
    grad_ctx = context_grad.reshape(images, SEQ, head_count, DH)
    context_four = context_b.reshape(images, SEQ, head_count, DH)
    value_grad = jnp.einsum("bhqk,bqhd->bkhd", attn_b, grad_ctx, preferred_element_type=jnp.float32)
    attn_grad = jnp.einsum(
        "bqhd,bkhd->bhqk", grad_ctx, values_b, preferred_element_type=jnp.float32
    )
    row_dot = jnp.sum(grad_ctx.astype(jnp.float32) * context_four.astype(jnp.float32), axis=3)
    row_dot = jnp.transpose(row_dot, (0, 2, 1))[:, :, :, None]
    score_grad = (attention * (attn_grad - row_dot) * factor).astype(jnp.bfloat16)
    query_grad = jnp.einsum(
        "bhqk,bkhd->bqhd", score_grad, keys_b, preferred_element_type=jnp.float32
    )
    key_grad = jnp.einsum(
        "bhqk,bqhd->bkhd", score_grad, queries, preferred_element_type=jnp.float32
    )
    stacked = jnp.stack([query_grad, key_grad, value_grad], axis=3)
    return stacked.astype(jnp.bfloat16).reshape(tok_count, head_count * 3 * DH)


def plain_device(
    tokens,
    norm1_gain,
    norm1_shift,
    qkv_weight,
    proj_weight,
    proj_shift,
    norm2_gain,
    norm2_shift,
    router_weight,
    expand_weight,
    expand_shift,
    shrink_weight,
    shrink_shift,
    route_expert,
    route_slot,
    cotangent,
):
    experts = lax.axis_size("expert")
    tensor_count = lax.axis_size("tensor")
    tok_count = tokens.shape[0]
    images = tok_count // SEQ
    capacity = tensor_count * (5 * tok_count // (2 * experts * tensor_count) + 1)
    width = tokens.shape[1]
    token_f = tokens.astype(jnp.float32)
    normed, scaled1, inverse1 = normalize(token_f, norm1_gain, norm1_shift)
    normed_b = normed.astype(jnp.bfloat16)
    queries, keys_b, values_b, log_total, context_b, _ = attend_front(normed_b, qkv_weight, images)
    attn_part = jnp.dot(context_b, proj_weight, preferred_element_type=jnp.float32)
    hidden = token_f + heads_total(attn_part) + proj_shift
    normed2, scaled2, inverse2 = normalize(hidden, norm2_gain, norm2_shift)
    mixed_b = normed2.astype(jnp.bfloat16)
    logits = jnp.dot(mixed_b, router_weight, preferred_element_type=jnp.float32)
    pick_mask = (
        lax.broadcasted_iota(jnp.int32, (tok_count, 2, experts), 2) == route_expert[:, :, None]
    ).astype(jnp.float32)
    chosen = jnp.sum(logits[:, None, :] * pick_mask, axis=2)
    gate_top = jnp.max(chosen, axis=1, keepdims=True)
    lifted = jnp.exp(chosen - gate_top)
    gate_weights = lifted / jnp.sum(lifted, axis=1, keepdims=True)
    targets, owners = route_tables(route_expert, route_slot, experts, capacity)
    buffer = jnp.take(mixed_b, owners // 2, axis=0, mode="fill", fill_value=0).reshape(
        experts, capacity, width
    )
    received = send_rows(buffer).reshape(experts * capacity, width)
    preact = (
        jnp.dot(received, expand_weight[0], preferred_element_type=jnp.float32) + expand_shift[0]
    )
    activ_b = gelu_exact(preact).astype(jnp.bfloat16)
    out_part = jnp.dot(activ_b, shrink_weight[0], preferred_element_type=jnp.float32).reshape(
        experts, capacity, width
    )
    returned = return_rows(out_part, shrink_shift[0]).reshape(experts * capacity, width)
    picked = (
        jnp.take(returned, targets, axis=0, mode="fill", fill_value=0)
        .reshape(tok_count, 2, width)
        .astype(jnp.float32)
    )
    output = hidden + jnp.sum(gate_weights[:, :, None] * picked, axis=1)
    upstream = cotangent.astype(jnp.float32)
    gate_grad = jnp.sum(upstream[:, None, :] * picked, axis=2)
    weighted = (
        (gate_weights[:, :, None] * upstream[:, None, :])
        .astype(jnp.bfloat16)
        .reshape(2 * tok_count, width)
    )
    grad_buffer = jnp.take(weighted, owners, axis=0, mode="fill", fill_value=0).reshape(
        experts, capacity, width
    )
    grad_recv = send_rows(grad_buffer).reshape(experts * capacity, width)
    shrink_g = inner_rows(activ_b, grad_recv)
    sshift_g = jnp.sum(grad_recv.astype(jnp.float32), axis=0)
    pre_grad = outer_cols(grad_recv, shrink_weight[0]) * gelu_slope(preact)
    pre_gradb = pre_grad.astype(jnp.bfloat16)
    expand_g = inner_rows(received, pre_gradb)
    eshift_g = jnp.sum(pre_grad, axis=0)
    rows_part = outer_cols(pre_gradb, expand_weight[0]).reshape(experts, capacity, width)
    back_rows = return_rows(rows_part, 0.0).reshape(experts * capacity, width)
    common = jnp.sum(gate_weights * gate_grad, axis=1, keepdims=True)
    chosen_grad = gate_weights * (gate_grad - common)
    logit_grad = jnp.sum(pick_mask * chosen_grad[:, :, None], axis=1).astype(jnp.bfloat16)
    router_g = inner_rows(mixed_b, logit_grad)
    back_pick = (
        jnp.take(back_rows, targets, axis=0, mode="fill", fill_value=0)
        .reshape(tok_count, 2, width)
        .astype(jnp.float32)
    )
    mixed_grad = jnp.sum(back_pick, axis=1) + outer_cols(logit_grad, router_weight)
    gain2_g = jnp.sum(mixed_grad * scaled2, axis=0)
    shift2_g = jnp.sum(mixed_grad, axis=0)
    hidden_grad = upstream + norm_back(mixed_grad, scaled2, inverse2, norm2_gain)
    pshift_g = jnp.sum(hidden_grad, axis=0)
    hidden_gradb = hidden_grad.astype(jnp.bfloat16)
    proj_g = inner_rows(context_b, hidden_gradb)
    context_grad = outer_cols(hidden_gradb, proj_weight).astype(jnp.bfloat16)
    qkv_gradb = attend_back(queries, keys_b, values_b, log_total, context_b, context_grad, images)
    qkv_g = inner_rows(normed_b, qkv_gradb)
    normed_grad = heads_total(outer_cols(qkv_gradb, qkv_weight))
    gain1_g = jnp.sum(normed_grad * scaled1, axis=0)
    shift1_g = jnp.sum(normed_grad, axis=0)
    tokens_grad = hidden_grad + norm_back(normed_grad, scaled1, inverse1, norm1_gain)
    summed = lax.psum(
        (gain1_g, shift1_g, qkv_g, proj_g, pshift_g, gain2_g, shift2_g, router_g), "expert"
    )
    return (
        output,
        tokens_grad,
        summed[0],
        summed[1],
        summed[2],
        summed[3],
        summed[4],
        summed[5],
        summed[6],
        summed[7],
        expand_g[None],
        eshift_g[None],
        shrink_g[None],
        sshift_g[None],
    )

MESH = pl.DeviceIdType.MESH
F32 = jnp.float32
LIMIT = 57
BF16 = jnp.bfloat16


def place():
    e = lax.axis_index("expert")
    t = lax.axis_index("tensor")
    a = t // 2
    c = t % 2
    return e, t, a, c, (e, 2 * a + 1 - c), (e, 2 * (1 - a) + c)


def greet(devices):
    barrier = pltpu.get_barrier_semaphore()
    for device in devices:
        pl.semaphore_signal(barrier, inc=1, device_id=device, device_id_type=MESH)
    pl.semaphore_wait(barrier, len(devices))


def remote(src, dst, send, recv, device):
    return pltpu.make_async_remote_copy(
        src_ref=src, dst_ref=dst, send_sem=send, recv_sem=recv, device_id=device, device_id_type=MESH
    )


def turns(count):
    far = list(range(count // 2, count))
    near = list(range(1, count // 2))
    order = []
    for i, step in enumerate(far):
        order.append(step)
        if i < len(near):
            order.append(near[i])
    return order


def lanes(index, width):
    return pl.ds(pl.multiple_of(index * width, 128), width)


class Rows:
    def __init__(self, two, one, dest, send_far, send_across, send_core, recv):
        self.two, self.one, self.dest = two, one, dest
        self.send_far, self.send_across = send_far, send_across
        self.send_core, self.recv = send_core, recv
        self.e, self.t, self.a, self.c, self.core, self.across = place()
        self.count = dest.shape[0]
        self.far = 2 * (1 - self.a) + self.c
        self.near, self.cross = 2 * self.a + 1 - self.c, 2 * (1 - self.a) + 1 - self.c

    def half(self, origin):
        return self.dest.at[origin, pl.ds(2 * self.c, 2)]

    def send(self, d):
        to = (self.e ^ d, self.t)
        if d < self.count // 2:
            spot, sem = self.half(self.e), self.recv.at[self.e, 0]
            return remote(self.two.at[d], spot, self.send_far.at[d], sem, to)
        spot, sem = self.dest.at[self.e, self.t], self.recv.at[self.e, self.t]
        return remote(self.one.at[d - self.count // 2], spot, self.send_far.at[d], sem, to)

    def keep(self, sem):
        return pltpu.make_async_copy(self.two.at[0], self.half(self.e), sem)

    def begin(self):
        for d in turns(self.count):
            self.send(d).start()

    def wait_two(self, origin):
        spot = self.half(origin)
        remote(spot, spot, self.send_far.at[0], self.recv.at[origin, 0], self.core).wait_recv()

    def core_two(self, origin):
        spot = self.half(origin)
        return remote(spot, spot, self.send_core.at[origin, 0], self.recv.at[origin, 1], self.core)

    def across_copy(self, origin):
        spot, sem = self.dest.at[origin, self.t], self.recv.at[origin, self.t]
        return remote(spot, spot, self.send_across.at[origin], sem, self.across)

    def core_copy(self, origin, piece):
        spot, sem = self.dest.at[origin, piece], self.recv.at[origin, piece]
        return remote(spot, spot, self.send_core.at[origin, piece], sem, self.core)

    def pass_one(self, origin):
        self.core_copy(origin, self.t).wait_recv()
        self.across_copy(origin).start()
        self.core_copy(origin, self.t).start()

    def hop_one(self, origin):
        self.core_copy(origin, self.far).wait_recv()
        self.core_copy(origin, self.far).start()

    def ready_two(self, origin):
        self.core_two(origin).wait_recv()

    def ready_one(self, origin):
        self.core_copy(origin, self.near).wait_recv()
        self.core_copy(origin, self.cross).wait_recv()

    def close(self):
        for d in range(self.count):
            origin = self.e ^ d
            if d:
                self.send(d).wait_send()
            if d < self.count // 2:
                self.core_two(origin).wait_send()
            else:
                self.across_copy(origin).wait_send()
                self.core_copy(origin, self.t).wait_send()
                self.core_copy(origin, self.far).wait_send()


def front_kernel(
    loads, begin_rows, begin_gates,
    hid, mixed, normed, heads, ctx, cols, marks, rows_two, rows_one, gate_rows, gains, taken,
    tok, cot, experts_t, slots_t, gain1_v, shift1_v, qkv_t, proj_w, proj_shift_v, gain2_v, shift2_v,
    router_t,
    cot_two, cot_one, turned, xsum, xgot1, xpart, xgot2, xdone, xgot3,
    send_far, send_across, send_core, recv, xsem, local,
):
    e, t, a, c, core, across = place()
    count, _, quarter, width = taken.shape
    rows = tok.shape[0]
    tall = xsum.shape[0]
    half = width // 2
    padded = 4 * quarter
    cmine, cother = lanes(c, half), lanes(1 - c, half)
    raw = Rows(cot_two, cot_one, taken, send_far, send_across, send_core, recv)

    def forward(d):
        origin = e ^ d
        if d < count // 2:
            if d:
                raw.wait_two(origin)
            raw.core_two(origin).start()
        else:
            raw.pass_one(origin)

    def place_rows(values, two, one):
        cut = count * quarter
        two[...] = values[:cut].reshape(two.shape)
        one[...] = values[cut:].reshape(one.shape)

    for copy in loads[:3]:
        copy.wait()
    spots = [
        jnp.where(slots_t[j : j + 1] >= 0, experts_t[j : j + 1] * padded + slots_t[j : j + 1], -1)
        for j in range(2)
    ]
    many = lax.broadcasted_iota(jnp.int32, (count * quarter, 1), 0)
    few = lax.broadcasted_iota(jnp.int32, (count // 2 * quarter, 1), 0)
    ids = jnp.concatenate(
        [
            (e ^ (many // (2 * quarter))) * padded + many % (2 * quarter) + 2 * c * quarter,
            (e ^ (count // 2 + few // quarter)) * padded + few % quarter + t * quarter,
        ],
        axis=0,
    )
    chooser = jnp.where((ids == spots[0]) | (ids == spots[1]), 1.0, 0.0).astype(BF16)
    place_rows(jnp.dot(chooser, cot[...], preferred_element_type=F32).astype(BF16), cot_two, cot_one)
    raw.begin()
    keep = raw.keep(local)
    keep.start()
    for copy in loads[3:12]:
        copy.wait()
    gain1, shift1, proj_shift, gain2, shift2 = [
        ref[...].reshape(1, width)
        for ref in (gain1_v, shift1_v, proj_shift_v, gain2_v, shift2_v)
    ]
    token_f = tok[...].astype(F32)
    normed_f, _, _ = normalize(token_f, gain1, shift1)
    normed_b = normed_f.astype(BF16)
    normed[...] = normed_b
    keep.wait()
    forward(0)
    projected = outer_cols(normed_b, qkv_t[...]).astype(BF16)
    head_count = heads.shape[0]
    for i in range(head_count):
        for j in range(3):
            start = DH * (3 * i + j)
            heads[i, j, tall - 16 :] = jnp.zeros((16, DH), BF16)
            heads[i, j, :rows] = projected[:, start : start + DH]
    turned[...] = jnp.zeros_like(turned)
    for j in range(2):
        turned[j : j + 1, :rows] = experts_t[j : j + 1].astype(F32)
        turned[2 + j : 3 + j, :rows] = spots[j].astype(F32)
    table = jnp.transpose(turned[...])[:rows]
    span = -(-rows // 32) * 16
    edge = SEQ // 16 * 16
    limits = ((0, edge), (edge, tall))
    areas = [pl.ds(low, high - low) for low, high in limits]

    def one(p):
        src = xsum.at[areas[p], cother]
        return remote(src, xgot1.at[areas[p]], xsem.at[6 * p], xsem.at[6 * p + 1], core)

    def two(p):
        src, dst = xpart.at[areas[p]], xgot2.at[areas[p]]
        return remote(src, dst, xsem.at[6 * p + 2], xsem.at[6 * p + 3], across)

    def three(p):
        src, dst = xdone.at[areas[p]], xgot3.at[areas[p]]
        return remote(src, dst, xsem.at[6 * p + 4], xsem.at[6 * p + 5], core)

    def start_two(p):
        one(p).wait_recv()
        xpart[areas[p]] = (
            xsum[areas[p], cmine].astype(F32) + xgot1[areas[p]].astype(F32)
        ).astype(BF16)
        two(p).start()

    def start_three(p):
        two(p).wait_recv()
        xdone[areas[p]] = (
            xpart[areas[p]].astype(F32) + xgot2[areas[p]].astype(F32)
        ).astype(BF16)
        three(p).start()

    def finish(p):
        low, high = limits[p][0], min(limits[p][1], rows)
        span_p = pl.ds(low, high - low)
        three(p).wait_recv()
        hid[span_p, cmine] = tok[span_p, cmine].astype(F32) + xdone[span_p].astype(F32)
        hid[span_p, cother] = tok[span_p, cother].astype(F32) + xgot3[span_p].astype(F32)
        hidden = hid[span_p] + proj_shift
        hid[span_p] = hidden
        mixed[span_p] = normalize(hidden, gain2, shift2)[0].astype(BF16)

    for image in range(rows // SEQ):
        base = image * SEQ // 16 * 16
        area = pl.ds(base, span)
        spot_q = lax.broadcasted_iota(jnp.int32, (span, 1), 0) + base
        spot_k = lax.broadcasted_iota(jnp.int32, (1, span), 1) + base
        low, high = image * SEQ, (image + 1) * SEQ
        good_q = (spot_q >= low) & (spot_q < high)
        good_k = (spot_k >= low) & (spot_k < high)
        for i in range(head_count):
            scores = outer_cols(heads[i, 0, area], heads[i, 1, area]) * DH ** (-0.5)
            scores = jnp.where(good_k, scores, -1e30)
            weight = jnp.exp(scores - jnp.max(scores, axis=1, keepdims=True))
            share = jnp.where(good_q, 1.0 / jnp.sum(weight, axis=1, keepdims=True), 0.0)
            value = jnp.dot(
                (weight * share).astype(BF16), heads[i, 2, area], preferred_element_type=F32
            ).astype(BF16)
            columns = pl.ds(DH * i, DH)
            if image == 0:
                ctx[base : base + span, columns] = value
            else:
                over = (image - 1) * SEQ // 16 * 16 + span - base
                ctx[base : base + over, columns] += value[:over]
                ctx[base + over : base + span, columns] = value[over:]
                if i == 0:
                    start_two(0)
                else:
                    forward(i)
        xsum[areas[image]] = jnp.dot(
            ctx[areas[image]], proj_w[...], preferred_element_type=F32
        ).astype(BF16)
        one(image).start()
    slots = lax.broadcasted_iota(jnp.int32, (rows, count * padded), 1)
    for j in range(2):
        hit = slots == table[:, 2 + j : 3 + j].astype(jnp.int32)
        marks[j] = jnp.where(hit, 1.0, 0.0).astype(BF16)
    start_two(1)
    for d in (3, 4, 5, 6, 7):
        forward(d)
    gains[0:1] = gain1
    gains[1:2] = gain2
    start_three(0)
    finish(0)
    start_three(1)
    finish(1)
    mixed_b = mixed[...]
    place_rows(jnp.dot(chooser, mixed_b, preferred_element_type=F32).astype(BF16), rows_two, rows_one)
    begin_rows()
    for d in range(count // 2, count):
        raw.hop_one(e ^ d)
    logits = outer_cols(mixed_b, router_t[...])
    names = lax.broadcasted_iota(jnp.int32, logits.shape, 1)
    chosen = [
        jnp.sum(
            jnp.where(names == table[:, j : j + 1].astype(jnp.int32), logits, 0.0),
            axis=1,
            keepdims=True,
        )
        for j in range(2)
    ]
    gate_top = jnp.maximum(chosen[0], chosen[1])
    lifted = [jnp.exp(value - gate_top) for value in chosen]
    gates = [value / (lifted[0] + lifted[1]) for value in lifted]
    lane = lax.broadcasted_iota(jnp.int32, (rows, 128), 1)
    cols[...] = jnp.where(lane == 2, gates[0], jnp.where(lane == 3, gates[1], table))
    for s in range(count):
        block = pl.ds(s * padded, padded)
        both = marks[0, :, block].astype(F32) * gates[0] + marks[1, :, block].astype(F32) * gates[1]
        gate_rows[s] = jnp.broadcast_to(jnp.sum(both, axis=0, keepdims=True), (8, padded))
    begin_gates()

    def close():
        raw.close()
        for p in range(2):
            one(p).wait_send()
            two(p).wait_send()
            three(p).wait_send()

    return raw, close


def front_parts(rows, width, count, quarter, head_count):
    tall = -(-rows // 16) * 16
    half = width // 2
    padded = 4 * quarter
    dma = pltpu.SemaphoreType.DMA
    piece = pltpu.VMEM((tall, half), BF16)
    outs = [
        pltpu.VMEM((rows, width), F32),
        pltpu.VMEM((rows, width), BF16),
        pltpu.VMEM((rows, width), BF16),
        pltpu.VMEM((head_count, 3, tall, DH), BF16),
        pltpu.VMEM((tall, head_count * DH), BF16),
        pltpu.VMEM((rows, 128), F32),
        pltpu.VMEM((2, rows, count * padded), BF16),
        pltpu.VMEM((count // 2, 2, quarter, width), BF16),
        pltpu.VMEM((count // 2, quarter, width), BF16),
        pltpu.VMEM((count, 8, padded), F32),
        pltpu.VMEM((8, width), F32),
        pltpu.VMEM((count, 4, quarter, width), BF16),
    ]
    scratch = (
        [pltpu.VMEM((count // 2, 2, quarter, width), BF16)]
        + [pltpu.VMEM((count // 2, quarter, width), BF16), pltpu.VMEM((128, 512), F32)]
        + [pltpu.VMEM((tall, width), BF16)]
        + [piece] * 5
        + [dma((count,)), dma((count,)), dma((count, 4)), dma((count, 4)), dma((12,)), dma(())]
    )
    return outs, scratch


def gates_copy(gate_rows, gate_got, send, recv, dst):
    e, t = lax.axis_index("expert"), lax.axis_index("tensor")
    return remote(gate_rows.at[dst], gate_got.at[e], send.at[dst], recv.at[e], (dst, t))


def expert_kernel(
    sent, rows, idle, keep,
    raw, gate_rows, up_w, up_b, down_w, shift,
    rows_in, grads_out, activ, pre_b, bias_grad, shift_grad, out0, out1,
    part, got1, half1, got2, ready, gate_got,
    send_far, send_across, send_core, recv, gate_send, gate_recv,
    send1, recv1, send2, recv2, send3, recv3, send4, recv4, local,
):
    e, t, a, c, core, across = place()
    count = raw.shape[0]
    outs = (out0, out1)
    high, width = part.shape[2] // 2, part.shape[3] // 2
    mine, other = pl.ds(c * high, high), pl.ds((1 - c) * high, high)
    left, right = lanes(a, width), lanes(1 - a, width)

    def origin_of(i):
        return e ^ (4 * (i // 2 % 2) + 2 * (i // 4) + i % 2)

    def gate_copy(dst):
        return gates_copy(gate_rows, gate_got, gate_send, gate_recv, dst)

    def one_copy(k, dst):
        return remote(part.at[k, dst, other], got1.at[k, dst], send1.at[k, dst], recv1.at[k, dst], core)

    def two_copy(k, dst):
        return remote(
            half1.at[k, dst, :, right], got2.at[k, dst], send2.at[k, dst], recv2.at[k, dst], across
        )

    def three_copy(k, dst):
        return remote(ready.at[k, dst], outs[k].at[e, c], send3.at[k, dst], recv3.at[k, e], (dst, t))

    def four_copy(k, origin, side):
        spot = outs[k].at[origin, side]
        return remote(spot, spot, send4.at[k, origin], recv4.at[k, origin], core)

    bias_grad[...] = jnp.zeros_like(bias_grad)
    shift_grad[...] = jnp.zeros_like(shift_grad)
    gate_got[e] = gate_rows[e]
    across_id = lax.broadcasted_iota(jnp.int32, (2 * high, 2 * high), 0)
    down_id = lax.broadcasted_iota(jnp.int32, (2 * high, 2 * high), 1)
    keep.wait()

    def step(i, carry):
        for j in range(2):

            @pl.when((i < count // 2) & (i % 2 == 0))
            def _():
                origin = origin_of(2 * i + j)
                if j == 0:

                    @pl.when(i > 0)
                    def _():
                        rows.wait_two(origin)

                else:
                    rows.wait_two(origin)
                rows.core_two(origin).start()

            @pl.when((i < count // 2) & (i % 2 == 1))
            def _():
                rows.pass_one(origin_of(2 * i + j))

            @pl.when((i >= 1) & (i < count // 2 + 1) & (i % 2 == 0))
            def _():
                rows.hop_one(origin_of(2 * i - 2 + j))

        @pl.when((i >= 2) & (i < count + 2))
        def _():
            origin = origin_of(i - 2)

            @pl.when(i > 2)
            def _():
                here = gate_got.at[origin]
                remote(here, here, gate_send.at[origin], gate_recv.at[origin], across).wait_recv()

            @pl.when(i // 2 % 2 == 1)
            def _():
                rows.ready_two(origin)
                sent.ready_two(origin)

            @pl.when(i // 2 % 2 == 0)
            def _():
                rows.ready_one(origin)
                sent.ready_one(origin)

            tokens = rows_in[origin].reshape(2 * high, 2 * width)
            gate = jnp.sum(
                jnp.where(across_id == down_id, gate_got[origin, 0:1], 0.0), axis=1, keepdims=True
            )
            grads = (gate * raw[origin].reshape(2 * high, 2 * width).astype(F32)).astype(BF16)
            grads_out[origin] = grads
            preact = jnp.dot(tokens, up_w[...], preferred_element_type=F32) + up_b[...]
            bell = 0.5 * (1.0 + lax.erf(preact * half_root))
            active = (preact * bell).astype(BF16)
            activ[origin] = active
            part[0, origin] = jnp.dot(active, down_w[...], preferred_element_type=F32).astype(BF16)
            one_copy(0, origin).start()
            slope = bell + preact * jnp.exp(-0.5 * preact * preact) * gauss_peak
            pre_grad = outer_cols(grads, down_w[...]) * slope
            bias_grad[...] += jnp.sum(pre_grad, axis=0, keepdims=True)
            shift_grad[...] += jnp.sum(grads.astype(F32), axis=0, keepdims=True)
            pre_low = pre_grad.astype(BF16)
            pre_b[origin] = pre_low
            part[1, origin] = outer_cols(pre_low, up_w[...]).astype(BF16)
            one_copy(1, origin).start()

        @pl.when((i >= 3) & (i < count + 3))
        def _():
            dst = origin_of(i - 3)
            for k in range(2):
                one_copy(k, dst).wait_recv()
                half1[k, dst] = (
                    part[k, dst, mine].astype(F32) + got1[k, dst].astype(F32)
                ).astype(BF16)
                two_copy(k, dst).start()

        @pl.when(i >= 5)
        def _():
            dst = origin_of(i - 5)
            for k in range(2):
                two_copy(k, dst).wait_recv()
                total = half1[k, dst, :, left].astype(F32) + got2[k, dst].astype(F32)
                if k == 0:
                    total = total + shift[:, left]
                ready[k, dst] = total.astype(BF16)

                @pl.when(i == 5)
                def _():
                    keep = pltpu.make_async_copy(ready.at[k, dst], outs[k].at[e, c], local.at[k])
                    keep.start()
                    keep.wait()
                    four_copy(k, e, c).start()

                @pl.when(i > 5)
                def _():
                    three_copy(k, dst).start()

        return carry

    lax.fori_loop(0, count + 5, step, 0)
    idle()
    for d in turns(count):
        origin = e ^ d
        for k in range(2):
            spot = outs[k].at[origin, c]
            remote(spot, spot, send4.at[k, origin], recv3.at[k, origin], core).wait_recv()
            four_copy(k, origin, c).start()

    def finish(d, carry):
        origin = e ^ d

        @pl.when(d > 0)
        def _():
            gate_copy(origin).wait_send()

        for k in range(2):
            four_copy(k, origin, 1 - c).wait_recv()
            one_copy(k, origin).wait_send()
            two_copy(k, origin).wait_send()
            four_copy(k, origin, c).wait_send()

            @pl.when(d > 0)
            def _():
                three_copy(k, origin).wait_send()

        return carry

    lax.fori_loop(0, count, finish, 0)
    rows.close()


def expert_parts(count, rows, width, hidden):
    dma = pltpu.SemaphoreType.DMA
    inner = pltpu.VMEM((count, 4 * rows, hidden), BF16)
    out = pltpu.VMEM((count, 2, 2 * rows, width // 2), BF16)
    full = pltpu.VMEM((2, count, 2 * rows, width), BF16)
    half = pltpu.VMEM((2, count, 2 * rows, width // 2), BF16)
    outs = [
        pltpu.VMEM((count, 4, rows, width), BF16),
        pltpu.VMEM((count, 4 * rows, width), BF16),
        inner,
        inner,
    ]
    scratch = (
        [pltpu.VMEM((2, count, 4 * rows, width), BF16), full, full, half, half]
        + [pltpu.VMEM((count, 8, 4 * rows), F32)]
        + [dma((count,)), dma((count,)), dma((count, 4)), dma((count, 4)), dma((count,)), dma((count,))]
        + [dma((2, count))] * 8
        + [dma((2,))]
    )
    return outs, [out, out], scratch


def split(index):
    return index * 192


def weight_sums(left, right, out, leave):
    width = out.shape[0]
    part = width // 3
    right_all = right[...].reshape(-1, out.shape[1])

    @pl.loop(0, 3)
    def _(i):
        spot = lanes(i, part)
        left_part = left[..., spot].reshape(-1, part)
        out[pl.ds(pl.multiple_of(i * part, 8), part)] = inner_rows(left_part, right_all)

    leave.start()


def back_kernel(
    ret, bak, marks, cols, cot, hid, mixed, router, gains, tok, normed, heads, ctx,
    proj_w, qkv_w, received, grad_recv, activ, pre_b, leave,
    out, tok_g, fin, sums, shrink_g, expand_g,
    back_s, back_r, added_s, added_r, gate_s, gate_r, wide_b, hid_g,
    upper, turned, gsrc, got1, part, got2,
    xsum, xgot1, xpart, xgot2, xdone, xgot3, sm, sgot, sq, sgy, sgz,
    bsem, asem, gsem, s1, r1, s2, r2, s3, r3, s4, r4, xsem, tsem, ysem, zsend, zrecv, osem,
):
    e, t, a, c, core, across = place()
    z, y = e // 2, e % 2
    diag = (e, 2 * (1 - a) + 1 - c)
    beside = (2 * z + 1 - y, t)
    deep = got2.shape[1]
    rows, width = tok.shape
    tall = wide_b.shape[0]
    half = width // 2
    block = back_s.shape[1]
    chunks = gsrc.shape[0]
    factor = DH ** (-0.5)
    left, right = lanes(a, half), lanes(1 - a, half)
    ymine, yother = lanes(y, half), lanes(1 - y, half)
    cmine, cother = lanes(c, half), lanes(1 - c, half)

    def peers(order=(2, 1, 3)):
        return [lax.rem(z + d, deep) for d in order]

    total_slots = ret.shape[0] * ret.shape[1] * ret.shape[2]
    ret_all = ret[...].reshape(total_slots, half)
    bak_all = bak[...].reshape(total_slots, half)
    back_here = jnp.dot(marks[0] + marks[1], bak_all, preferred_element_type=F32).astype(BF16)
    picked = [jnp.dot(marks[j], ret_all, preferred_element_type=F32) for j in range(2)]
    route = cols[:, 0:2].astype(jnp.int32)
    g = [cols[:, 2:3], cols[:, 3:4]]
    back_s[1, block - 32 :, :] = jnp.zeros((32, half), BF16)
    added_s[1, block - 32 :, :] = jnp.zeros((32, half), BF16)
    back_s[0] = back_here[:block]
    back_s[1, : rows - block] = back_here[block:]
    back_across = remote(back_s.at[c], back_r.at[c], bsem.at[0], bsem.at[1], across)
    back_across.start()
    cot_half = cot[:, left].astype(F32)
    lane = lax.broadcasted_iota(jnp.int32, (rows, 128), 1)
    dots = [jnp.sum(cot_half * value, axis=1, keepdims=True) for value in picked]
    turned[...] = jnp.zeros_like(turned)
    turned[:rows] = jnp.where(lane == 0, dots[0], jnp.where(lane == 1, dots[1], 0.0))
    gate_s[...] = jnp.transpose(turned[...])[:8]
    gate_across = remote(gate_s, gate_r, gsem.at[0], gsem.at[1], across)
    gate_across.start()
    added_here = (g[0] * picked[0] + g[1] * picked[1]).astype(BF16)
    added_s[0] = added_here[:block]
    added_s[1, : rows - block] = added_here[block:]
    added_across = remote(added_s.at[c], added_r.at[c], asem.at[0], asem.at[1], across)
    added_across.start()
    mixed_row = mixed[...]
    hidden = hid[...]
    centered = hidden - jnp.mean(hidden, axis=1, keepdims=True)
    inverse2 = lax.rsqrt(jnp.mean(centered * centered, axis=1, keepdims=True) + norm_eps)
    scaled2 = centered * inverse2
    wide_b[:rows, left] = back_here
    for i in range(3):
        upper[i, tall - 16 :] = jnp.zeros((16, DH), BF16)

    weight_sums(activ, grad_recv, shrink_g, leave[1])
    back_across.wait_recv()
    back_core = remote(back_r.at[c], back_r.at[c], bsem.at[2], bsem.at[3], core)
    back_core.start()
    gate_across.wait_recv()
    gate_sum = gate_s[...] + gate_r[...]
    gate_cols = jnp.transpose(jnp.concatenate([gate_sum] * 16, axis=0))[:rows]
    gate_grad = [gate_cols[:, 0:1], gate_cols[:, 1:2]]
    common = g[0] * gate_grad[0] + g[1] * gate_grad[1]
    experts = lax.broadcasted_iota(jnp.int32, (rows, router.shape[0]), 1)
    logit_grad = (
        jnp.where(experts == route[:, 0:1], g[0] * (gate_grad[0] - common), 0.0)
        + jnp.where(experts == route[:, 1:2], g[1] * (gate_grad[1] - common), 0.0)
    ).astype(BF16)
    sm[1] = inner_rows(logit_grad, mixed_row) * 0.25
    from_router = jnp.dot(logit_grad, router[...], preferred_element_type=F32)
    back_other = remote(back_r.at[1 - c], back_r.at[1 - c], bsem.at[2], bsem.at[3], core)
    back_other.wait_recv()
    wide_b[:block, right] = back_r[0]
    wide_b[block:rows, right] = back_r[1, : rows - block]
    mixed_grad = wide_b[:rows].astype(F32) + from_router
    hidden_grad = cot[...].astype(F32) + norm_back(mixed_grad, scaled2, inverse2, gains[1:2])
    hid_g[...] = hidden_grad
    hidden_low = hidden_grad.astype(BF16)
    gsrc[0] = inner_rows(ctx[:rows], hidden_low).astype(BF16).reshape(gsrc.shape[1:])

    def y_copy(k):
        return remote(gsrc.at[k, :, :, yother], got1.at[k], s1.at[k], r1.at[k], beside)

    def z_copy(k, zz):
        return remote(part.at[k, zz], got2.at[k, z], s2.at[k, zz], r2.at[k, z], (2 * zz + y, t))

    def spread_copy(k, zz):
        spot = fin.at[k, z, :, ymine]
        return remote(spot, spot, s3.at[k, zz], r3.at[k, z], (2 * zz + y, t))

    def pass_copy(k, zz):
        spot = fin.at[k, zz, :, ymine]
        return remote(spot, spot, s4.at[k, zz], r4.at[k, zz], beside)

    def step_two(k):
        y_copy(k).wait_recv()
        part[k] = (gsrc[k, :, :, ymine].astype(F32) + got1[k].astype(F32)).astype(BF16)
        for zz in peers():
            z_copy(k, zz).start()

    def step_three(k):
        value = part[k, z].astype(F32)
        for zz in peers((1, 3, 2)):
            spot = got2.at[k, zz]
            remote(spot, spot, s2.at[k, zz], r2.at[k, zz], beside).wait_recv()
            value = value + got2[k, zz].astype(F32)
        fin[k, z, :, ymine] = value.astype(BF16)
        for zz in peers():
            spread_copy(k, zz).start()
        pass_copy(k, z).start()

    def step_four(k):
        for zz in peers((1, 3, 2)):
            spot = fin.at[k, zz, :, ymine]
            remote(spot, spot, s3.at[k, zz], r3.at[k, zz], beside).wait_recv()
            pass_copy(k, zz).start()

    y_copy(0).start()
    context_grad = outer_cols(hidden_low, proj_w[...]).astype(BF16)
    for i in range(3):
        upper[i, :rows] = context_grad[:, DH * i : DH * (i + 1)]
    sm[0, 2:3] = jnp.sum(hidden_grad, axis=0, keepdims=True) * 0.25
    sm[0, 3:4] = jnp.sum(mixed_grad * scaled2, axis=0, keepdims=True) * 0.25
    sm[0, 4:5] = jnp.sum(mixed_grad, axis=0, keepdims=True) * 0.25
    sm[0, 5:8] = jnp.zeros((3, width), F32)

    span = block
    for i in range(3):
        for image in range(rows // SEQ):
            base = image * SEQ // 16 * 16
            area = pl.ds(base, span)
            spot_k = lax.broadcasted_iota(jnp.int32, (span, 1), 0) + base
            spot_q = lax.broadcasted_iota(jnp.int32, (1, span), 1) + base
            low, high = image * SEQ, (image + 1) * SEQ
            good_k = (spot_k >= low) & (spot_k < high)
            good_q = (spot_q >= low) & (spot_q < high)
            queries, keys_b, values_b = heads[i, 0, area], heads[i, 1, area], heads[i, 2, area]
            up = upper[i, area]
            scores = outer_cols(keys_b, queries) * factor
            scores = jnp.where(good_k, scores, -1e30)
            top = jnp.max(scores, axis=0, keepdims=True)
            weight = jnp.exp(scores - top)
            share = jnp.where(good_q, 1.0 / jnp.sum(weight, axis=0, keepdims=True), 0.0)
            attention = weight * share
            attn_b = attention.astype(BF16)
            value_grad = jnp.dot(attn_b, up, preferred_element_type=F32)
            attn_grad = outer_cols(values_b, up)
            row_dot = jnp.sum(attention * attn_grad, axis=0, keepdims=True)
            score_grad = (attention * (attn_grad - row_dot) * factor).astype(BF16)
            key_grad = jnp.dot(score_grad, queries, preferred_element_type=F32)
            query_grad = inner_rows(score_grad, keys_b)
            for j, value in enumerate((query_grad, key_grad, value_grad)):
                columns = pl.ds(split(i) + DH * j, DH)
                if image == 0:
                    xsum_low = value.astype(BF16)
                    wide_b[base : base + span, columns] = xsum_low
                else:
                    over = (image - 1) * SEQ // 16 * 16 + span - base
                    xsum_low = value.astype(BF16)
                    wide_b[base : base + over, columns] += xsum_low[:over]
                    wide_b[base + over : base + span, columns] = xsum_low[over:]
        mine = wide_b[:rows, split(i) : split(i + 1)]
        gsrc[1 + i] = inner_rows(mine, normed[...]).astype(BF16).reshape(gsrc.shape[1:])
        y_copy(1 + i).start()
        step_two(i)
        if i >= 1:
            step_three(i - 1)
        if i >= 2:
            step_four(i - 2)
    qkv_low = wide_b[:rows, : qkv_w.shape[0]]
    normed_part = jnp.dot(qkv_low, qkv_w[...], preferred_element_type=F32)
    xsum[tall - 16 :] = jnp.zeros((16, width), BF16)
    xsum[:rows] = normed_part.astype(BF16)
    x1 = remote(xsum.at[:, cother], xgot1, xsem.at[0], xsem.at[1], core)
    x1.start()
    step_two(3)
    token_f = tok[...].astype(F32)
    centered1 = token_f - jnp.mean(token_f, axis=1, keepdims=True)
    inverse1 = lax.rsqrt(jnp.mean(centered1 * centered1, axis=1, keepdims=True) + norm_eps)
    scaled1 = centered1 * inverse1
    sm[0, 0:1] = jnp.sum(normed_part * scaled1, axis=0, keepdims=True)
    sm[0, 1:2] = jnp.sum(normed_part, axis=0, keepdims=True)

    def quarter(aa, cc):
        return sm.at[aa, :, lanes(cc, half)]

    trade = [
        remote(quarter(a, 1 - c), sgot.at[0], tsem.at[0, 0], tsem.at[1, 0], core),
        remote(quarter(1 - a, c), sgot.at[1], tsem.at[0, 1], tsem.at[1, 1], across),
        remote(quarter(1 - a, 1 - c), sgot.at[2], tsem.at[0, 2], tsem.at[1, 2], diag),
    ]
    for copy in trade:
        copy.start()
    x1.wait_recv()
    xpart[...] = (xsum[:, cmine].astype(F32) + xgot1[...].astype(F32)).astype(BF16)
    x2 = remote(xpart, xgot2, xsem.at[2], xsem.at[3], across)
    x2.start()
    step_three(2)
    step_four(1)
    for copy in trade:
        copy.wait_recv()
    sq[0] = (sm[a, :, cmine] + sgot[0]) + (sgot[1] + sgot[2])
    small_y = remote(sq.at[0], sgy, ysem.at[0], ysem.at[1], beside)
    small_y.start()

    step_three(3)
    step_four(2)
    small_y.wait_recv()
    sq[1] = sq[0] + sgy[...]
    small_z = [
        remote(sq.at[1], sgz.at[z], zsend.at[zz], zrecv.at[z], (2 * zz + y, t)) for zz in peers()
    ]
    for copy in small_z:
        copy.start()
    sgz[z] = sq[1]
    step_four(3)
    for zz in peers((1, 3, 2)):
        spot = sgz.at[zz]
        remote(spot, spot, zsend.at[zz], zrecv.at[zz], beside).wait_recv()
    sums[a, :, cmine] = (sgz[0] + sgz[1]) + (sgz[2] + sgz[3])
    here = sums.at[a, :, cmine]
    tell = [
        remote(here, here, osem.at[0, i], osem.at[1, i], device)
        for i, device in enumerate((core, across, diag))
    ]
    for copy in tell:
        copy.start()
    added_across.wait_recv()
    added_core = remote(added_r.at[c], added_r.at[c], asem.at[2], asem.at[3], core)
    added_core.start()
    x2.wait_recv()
    xpart_sum = (xpart[...].astype(F32) + xgot2[...].astype(F32)).astype(BF16)
    xdone[...] = xpart_sum
    x3 = remote(xdone, xgot3, xsem.at[4], xsem.at[5], core)
    x3.start()
    wide_b[:, cmine] = xpart_sum
    added_other = remote(added_r.at[1 - c], added_r.at[1 - c], asem.at[2], asem.at[3], core)
    added_other.wait_recv()
    out[:, left] = hid[:, left] + jnp.concatenate([added_s[0], added_s[1, : rows - block]], 0).astype(F32)
    out[:, right] = hid[:, right] + jnp.concatenate([added_r[0], added_r[1, : rows - block]], 0).astype(F32)
    leave[2].start()
    x3.wait_recv()
    wide_b[:, cother] = xgot3[...]
    normed_grad = wide_b[:rows].astype(F32)
    tok_g[...] = hid_g[...] + norm_back(normed_grad, scaled1, inverse1, gains[0:1])
    leave[3].start()
    for k in range(chunks):
        for zz in range(deep):
            spot = fin.at[k, zz, :, yother]
            remote(spot, spot, s4.at[k, zz], r4.at[k, zz], beside).wait_recv()
    for copy, (aa, cc) in zip(tell, ((a, 1 - c), (1 - a, c), (1 - a, 1 - c))):
        copy.wait_recv()
    for copy in trade + tell + small_z:
        copy.wait_send()
    for copy in (
        back_across, back_core, gate_across, added_across, added_core, x1, x2, x3, small_y,
    ):
        copy.wait_send()
    for k in range(chunks):
        y_copy(k).wait_send()
        pass_copy(k, z).wait_send()
        for zz in peers():
            z_copy(k, zz).wait_send()
            spread_copy(k, zz).wait_send()
            pass_copy(k, zz).wait_send()


def back_parts(rows, width, count):
    half = width // 2
    tall = -(-rows // 16) * 16
    block = -(-rows // 32) * 16
    deep = count // 2
    chunks = 4
    depth = width // chunks // deep
    dma = pltpu.SemaphoreType.DMA

    def low(*shape):
        return pltpu.VMEM(shape, BF16)

    def wide(*shape):
        return pltpu.VMEM(shape, F32)

    pair = low(2, block, half)
    line = wide(8, 512)
    stage = low(chunks, deep, depth, half)
    quarter = wide(8, half)
    outs = [wide(rows, width), wide(rows, width), wide(width, width), wide(width, width)]
    scratch = (
        [pair, pair, pair, pair, line, line, low(tall, width), wide(rows, width)]
        + [low(3, tall, DH), wide(512, 128)]
        + [low(chunks, deep, depth, width), stage, stage, stage]
        + [low(tall, width)]
        + [low(tall, half)] * 5
        + [wide(2, 8, width), wide(3, 8, half), wide(2, 8, half), quarter, wide(deep, 8, half)]
        + [dma((4,)), dma((4,)), dma((2,)), dma((chunks,)), dma((chunks,))]
        + [dma((chunks, deep))] * 6
        + [dma((6,)), dma((2, 3)), dma((2,)), dma((deep,)), dma((deep,)), dma((2, 3))]
    )
    return outs, scratch, (chunks, deep, depth, width)


def whole_kernel(counts, *refs):
    groups = []
    at = 0
    for number in counts:
        groups.append(refs[at : at + number])
        at += number
    (
        ins, (out_h, tok_h, shrink_h, expand_h, fin, sums, bias_grad, shift_grad),
        held, front_outs, front_scratch, rows_outs, results, expert_scratch, back_outs,
        back_scratch, (load, save),
    ) = groups
    e, t, a, c, core, across = place()
    loads = [pltpu.make_async_copy(src, dst, load.at[i]) for i, (src, dst) in enumerate(zip(ins, held))]
    for copy in loads:
        copy.start()
    experts = front_outs[-1].shape[0]
    greet([(e ^ d, t) for d in range(1, experts)] + [core, across, (e, 2 * (1 - a) + 1 - c)])
    (
        experts_t, slots_t, cot, tok, gain1_v, shift1_v, qkv_t, proj_w, proj_shift_v, gain2_v,
        shift2_v, router_t, up_w, up_b, down_w, shift,
    ) = held
    hid, mixed, normed, heads, ctx, cols, marks, rows_two, rows_one, gate_rows, gains, raw = front_outs
    rows_in = rows_outs[0]
    gate_got, send_far, send_across, send_core, recv, gate_send, gate_recv = expert_scratch[5:12]
    rows = Rows(rows_two, rows_one, rows_in, send_far, send_across, send_core, recv)
    keep = rows.keep(expert_scratch[-1].at[0])

    def begin_rows():
        rows.begin()
        keep.start()

    def begin_gates():
        for d in turns(experts):
            gates_copy(gate_rows, gate_got, gate_send, gate_recv, e ^ d).start()

    sent, close = front_kernel(
        loads, begin_rows, begin_gates, *front_outs,
        tok, cot, experts_t, slots_t, gain1_v, shift1_v, qkv_t, proj_w, proj_shift_v, gain2_v,
        shift2_v, router_t,
        *front_scratch,
    )
    for copy in loads[12:]:
        copy.wait()
    out, tok_g, shrink_g, expand_g = back_outs
    pairs = ((expand_g, expand_h), (shrink_g, shrink_h), (out, out_h), (tok_g, tok_h))
    leave = [pltpu.make_async_copy(src, dst, save.at[i]) for i, (src, dst) in enumerate(pairs)]
    expert_kernel(
        sent, rows, lambda: weight_sums(rows_in, rows_outs[3], expand_g, leave[0]), keep,
        raw, gate_rows, up_w, up_b, down_w, shift,
        *rows_outs, bias_grad, shift_grad, *results, *expert_scratch,
    )
    back_kernel(
        *results, marks, cols, cot, hid, mixed, router_t, gains, tok, normed, heads, ctx,
        proj_w, qkv_t, *rows_outs, leave,
        out, tok_g, fin, sums, shrink_g, expand_g,
        *back_scratch,
    )
    close()
    for copy in leave:
        copy.wait()


def run_whole(args, experts, quarter):
    tok = args[3]
    rows, width = tok.shape
    hidden = args[12].shape[1]
    head_count = args[7].shape[0] // DH
    vmem = pl.BlockSpec(memory_space=pltpu.VMEM)
    hbm = pl.BlockSpec(memory_space=pltpu.HBM)
    dma = pltpu.SemaphoreType.DMA
    front_outs, front_scratch = front_parts(rows, width, experts, quarter, head_count)
    rows_outs, results, expert_scratch = expert_parts(experts, quarter, width, hidden)
    back_outs, back_scratch, big = back_parts(rows, width, experts)
    held = [pltpu.VMEM(value.shape, value.dtype) for value in args]
    outs = [jax.ShapeDtypeStruct(value.shape, F32) for value in back_outs]
    outs = outs + [
        jax.ShapeDtypeStruct(big, BF16),
        jax.ShapeDtypeStruct((2, 8, width), F32),
        jax.ShapeDtypeStruct((1, hidden), F32),
        jax.ShapeDtypeStruct((1, width), F32),
    ]
    parts = [
        held, front_outs, front_scratch, rows_outs, results, expert_scratch, back_outs,
        back_scratch, [dma((len(args),)), dma((4,))],
    ]
    counts = [len(args), len(outs)] + [len(part) for part in parts]
    return pl.pallas_call(
        functools.partial(whole_kernel, counts),
        out_shape=tuple(outs),
        in_specs=[hbm] * len(args),
        out_specs=(hbm,) * 4 + (vmem,) * 4,
        scratch_shapes=sum(parts, []),
        compiler_params=pltpu.CompilerParams(
            collective_id=1, has_side_effects=True, vmem_limit_bytes=LIMIT * 1024 * 1024
        ),
    )(*args)


def last_kernel(
    out, tok_g, big, expand_g, shrink_g, eshift, sshift, small,
    out_h, tok_h, qkv_h, proj_h, expand_h, shrink_h, eshift_h, sshift_h, router_h, *rest,
):
    lines_h, (full, fin, sums, *rest) = rest[:5], rest[5:]
    lines, held, (load, sem) = rest[:5], rest[5:11], rest[11:]
    chunks, deep, depth, width = fin.shape
    cut = deep * depth
    plain = (expand_g, shrink_g, out, tok_g, eshift, sshift)
    plain_h = (expand_h, shrink_h, out_h, tok_h, eshift_h, sshift_h)
    takes = [
        pltpu.make_async_copy(src, dst, load.at[i])
        for i, (src, dst) in enumerate(zip((small, big) + plain, (sums, fin) + tuple(held)))
    ]
    for copy in takes:
        copy.start()
    copies = []

    def send(src, dst):
        copy = pltpu.make_async_copy(src, dst, sem.at[len(copies)])
        copy.start()
        copies.append(copy)

    takes[0].wait()
    send(sums.at[1], router_h)
    for i in range(5):
        lines[i][...] = sums[0, i : i + 1].reshape(width)
        send(lines[i], lines_h[i])
    takes[1].wait()
    full[...] = fin[...].astype(F32).reshape(chunks * cut, width)
    send(full.at[pl.ds(0, cut)], proj_h)
    send(full.at[pl.ds(cut, (chunks - 1) * cut)], qkv_h)
    for i, dst in enumerate(plain_h):
        takes[2 + i].wait()
        send(held[i], dst)
    for copy in copies:
        copy.wait()


def run_last(args):
    big = args[2]
    chunks, deep, depth, width = big.shape
    cut = deep * depth
    hbm = pl.BlockSpec(memory_space=pltpu.HBM)

    def shape(*sizes):
        return jax.ShapeDtypeStruct(sizes, F32)

    outs = (
        args[0],
        args[1],
        shape((chunks - 1) * cut, width),
        shape(cut, width),
        args[3],
        args[4],
        args[5],
        args[6],
        shape(8, width),
    ) + (shape(width),) * 5
    outs = tuple(jax.ShapeDtypeStruct(value.shape, F32) for value in outs)
    return pl.pallas_call(
        last_kernel,
        out_shape=outs,
        in_specs=[hbm] * len(args),
        out_specs=(hbm,) * len(outs),
        scratch_shapes=[
            pltpu.VMEM((chunks * cut, width), F32),
            pltpu.VMEM(big.shape, BF16),
            pltpu.VMEM(args[7].shape, F32),
        ]
        + [pltpu.VMEM((width,), F32)] * 5
        + [pltpu.VMEM(args[i].shape, F32) for i in (3, 4, 0, 1, 5, 6)]
        + [pltpu.SemaphoreType.DMA((len(args),))]
        + [pltpu.SemaphoreType.DMA((len(outs),))],
        compiler_params=pltpu.CompilerParams(vmem_limit_bytes=LIMIT * 1024 * 1024),
    )(*args)


def fast_device(
    tokens,
    norm1_gain,
    norm1_shift,
    qkv_weight,
    proj_weight,
    proj_shift,
    norm2_gain,
    norm2_shift,
    router_weight,
    expand_weight,
    expand_shift,
    shrink_weight,
    shrink_shift,
    route_expert,
    route_slot,
    cotangent,
):
    experts = lax.axis_size("expert")
    tensor_count = lax.axis_size("tensor")
    tok_count = tokens.shape[0]
    capacity = tensor_count * (5 * tok_count // (2 * experts * tensor_count) + 1)
    quarter = -(-capacity // (16 * tensor_count)) * 16
    qkv_t = qkv_weight.T
    router_t = router_weight.T
    output, tokens_grad, shrink_g, expand_g, big, small, eshift_g, sshift_g = run_whole(
        (
            route_expert.T,
            route_slot.T,
            cotangent,
            tokens,
            norm1_gain,
            norm1_shift,
            qkv_t,
            proj_weight,
            proj_shift,
            norm2_gain,
            norm2_shift,
            router_t,
            expand_weight[0],
            expand_shift,
            shrink_weight[0],
            shrink_shift,
        ),
        experts,
        quarter,
    )
    (
        output,
        tokens_grad,
        qkv_g,
        proj_g,
        expand_g,
        shrink_g,
        eshift_g,
        sshift_g,
        router_g,
        gain1_g,
        shift1_g,
        pshift_g,
        gain2_g,
        shift2_g,
    ) = run_last((output, tokens_grad, big, expand_g, shrink_g, eshift_g, sshift_g, small))
    return (
        output,
        tokens_grad,
        gain1_g,
        shift1_g,
        qkv_g.T,
        proj_g,
        pshift_g,
        gain2_g,
        shift2_g,
        router_g.T,
        expand_g[None],
        eshift_g,
        shrink_g[None],
        sshift_g,
    )


def solution(mesh):
    small_mesh = mesh.shape["expert"] == 8 and mesh.shape["tensor"] == 4
    on_device = fast_device if small_mesh else plain_device
    return jax.shard_map(
        on_device,
        mesh=mesh,
        in_specs=(
            P("expert", None),
            P(),
            P(),
            P(None, "tensor"),
            P("tensor", None),
            P(),
            P(),
            P(),
            P(),
            P("expert", None, "tensor"),
            P("expert", "tensor"),
            P("expert", "tensor", None),
            P("expert", None),
            P("expert", None),
            P("expert", None),
            P("expert", None),
        ),
        out_specs=(
            P("expert", None),
            P("expert", None),
            P(),
            P(),
            P(None, "tensor"),
            P("tensor", None),
            P(),
            P(),
            P(),
            P(),
            P("expert", None, "tensor"),
            P("expert", "tensor"),
            P("expert", "tensor", None),
            P("expert", None),
        ),
        check_vma=False,
    )
```

```python
import functools

import jax
import jax.numpy as jnp
from jax import lax
from jax.experimental import pallas as pl
from jax.experimental.pallas import tpu as pltpu
from jax.sharding import PartitionSpec as P

DH = 64
SEQ = 197


norm_eps = 1e-06
half_root = 0.7071067811865476
gauss_peak = 0.3989422804014327


def normalize(values, norm_gain, norm_shift):
    row_mean = jnp.mean(values, axis=1, keepdims=True)
    centered = values - row_mean
    variance = jnp.mean(centered * centered, axis=1, keepdims=True)
    inverse = lax.rsqrt(variance + norm_eps)
    scaled = centered * inverse
    return (scaled * norm_gain + norm_shift, scaled, inverse)


def norm_back(upstream, scaled, inverse, norm_gain):
    weighted = upstream * norm_gain
    first_mean = jnp.mean(weighted, axis=1, keepdims=True)
    second_mean = jnp.mean(weighted * scaled, axis=1, keepdims=True)
    return inverse * (weighted - first_mean - scaled * second_mean)


def gelu_exact(preact):
    return 0.5 * preact * (1.0 + lax.erf(preact * half_root))


def gelu_slope(preact):
    return (
        0.5 * (1.0 + lax.erf(preact * half_root))
        + preact * jnp.exp(-0.5 * preact * preact) * gauss_peak
    )


def inner_rows(left_b, right_b):
    return lax.dot_general(
        left_b, right_b, (((0,), (0,)), ((), ())), preferred_element_type=jnp.float32
    )


def outer_cols(left_b, right_b):
    return lax.dot_general(
        left_b, right_b, (((1,), (1,)), ((), ())), preferred_element_type=jnp.float32
    )


def route_tables(route_expert, route_slot, experts, capacity):
    tok_count = route_expert.shape[0]
    kept = route_slot >= 0
    targets = jnp.where(kept, route_expert * capacity + route_slot, experts * capacity).reshape(-1)
    numbers = jnp.arange(2 * tok_count, dtype=jnp.int32)
    owners = (
        jnp.full((experts * capacity,), 2 * tok_count, jnp.int32)
        .at[targets]
        .set(numbers, mode="drop")
    )
    return (targets, owners)


def heads_total(partial_value):
    return lax.psum(partial_value.astype(jnp.bfloat16), "tensor").astype(jnp.float32)


def send_rows(buffer):
    return lax.all_to_all(buffer, "expert", split_axis=0, concat_axis=0, tiled=True)


def return_rows(partial_value, offset):
    summed = lax.psum(partial_value.astype(jnp.bfloat16), "tensor").astype(jnp.float32)
    ready = (summed + offset).astype(jnp.bfloat16)
    return lax.all_to_all(ready, "expert", split_axis=0, concat_axis=0, tiled=True)


def attend_front(normed_b, qkv_weight, images):
    tok_count = normed_b.shape[0]
    head_count = qkv_weight.shape[1] // (3 * DH)
    projected = jnp.dot(normed_b, qkv_weight, preferred_element_type=jnp.float32).astype(
        jnp.bfloat16
    )
    projected = projected.reshape(images, SEQ, head_count, 3, DH)
    queries = projected[:, :, :, 0]
    keys_b = projected[:, :, :, 1]
    values_b = projected[:, :, :, 2]
    scores = jnp.einsum(
        "bqhd,bkhd->bhqk", queries, keys_b, preferred_element_type=jnp.float32
    ) * DH ** (-0.5)
    row_top = jnp.max(scores, axis=3, keepdims=True)
    log_total = row_top + jnp.log(jnp.sum(jnp.exp(scores - row_top), axis=3, keepdims=True))
    attn_b = jnp.exp(scores - log_total).astype(jnp.bfloat16)
    context = jnp.einsum("bhqk,bkhd->bqhd", attn_b, values_b, preferred_element_type=jnp.float32)
    context_b = context.astype(jnp.bfloat16).reshape(tok_count, head_count * DH)
    return (queries, keys_b, values_b, log_total, context_b, projected)


def attend_back(queries, keys_b, values_b, log_total, context_b, context_grad, images):
    tok_count = context_b.shape[0]
    head_count = queries.shape[2]
    factor = DH ** (-0.5)
    scores = (
        jnp.einsum("bqhd,bkhd->bhqk", queries, keys_b, preferred_element_type=jnp.float32) * factor
    )
    attention = jnp.exp(scores - log_total)
    attn_b = attention.astype(jnp.bfloat16)
    grad_ctx = context_grad.reshape(images, SEQ, head_count, DH)
    context_four = context_b.reshape(images, SEQ, head_count, DH)
    value_grad = jnp.einsum("bhqk,bqhd->bkhd", attn_b, grad_ctx, preferred_element_type=jnp.float32)
    attn_grad = jnp.einsum(
        "bqhd,bkhd->bhqk", grad_ctx, values_b, preferred_element_type=jnp.float32
    )
    row_dot = jnp.sum(grad_ctx.astype(jnp.float32) * context_four.astype(jnp.float32), axis=3)
    row_dot = jnp.transpose(row_dot, (0, 2, 1))[:, :, :, None]
    score_grad = (attention * (attn_grad - row_dot) * factor).astype(jnp.bfloat16)
    query_grad = jnp.einsum(
        "bhqk,bkhd->bqhd", score_grad, keys_b, preferred_element_type=jnp.float32
    )
    key_grad = jnp.einsum(
        "bhqk,bqhd->bkhd", score_grad, queries, preferred_element_type=jnp.float32
    )
    stacked = jnp.stack([query_grad, key_grad, value_grad], axis=3)
    return stacked.astype(jnp.bfloat16).reshape(tok_count, head_count * 3 * DH)


def plain_device(
    tokens,
    norm1_gain,
    norm1_shift,
    qkv_weight,
    proj_weight,
    proj_shift,
    norm2_gain,
    norm2_shift,
    router_weight,
    expand_weight,
    expand_shift,
    shrink_weight,
    shrink_shift,
    route_expert,
    route_slot,
    cotangent,
):
    experts = lax.axis_size("expert")
    tensor_count = lax.axis_size("tensor")
    tok_count = tokens.shape[0]
    images = tok_count // SEQ
    capacity = tensor_count * (5 * tok_count // (2 * experts * tensor_count) + 1)
    width = tokens.shape[1]
    token_f = tokens.astype(jnp.float32)
    normed, scaled1, inverse1 = normalize(token_f, norm1_gain, norm1_shift)
    normed_b = normed.astype(jnp.bfloat16)
    queries, keys_b, values_b, log_total, context_b, _ = attend_front(normed_b, qkv_weight, images)
    attn_part = jnp.dot(context_b, proj_weight, preferred_element_type=jnp.float32)
    hidden = token_f + heads_total(attn_part) + proj_shift
    normed2, scaled2, inverse2 = normalize(hidden, norm2_gain, norm2_shift)
    mixed_b = normed2.astype(jnp.bfloat16)
    logits = jnp.dot(mixed_b, router_weight, preferred_element_type=jnp.float32)
    pick_mask = (
        lax.broadcasted_iota(jnp.int32, (tok_count, 2, experts), 2) == route_expert[:, :, None]
    ).astype(jnp.float32)
    chosen = jnp.sum(logits[:, None, :] * pick_mask, axis=2)
    gate_top = jnp.max(chosen, axis=1, keepdims=True)
    lifted = jnp.exp(chosen - gate_top)
    gate_weights = lifted / jnp.sum(lifted, axis=1, keepdims=True)
    targets, owners = route_tables(route_expert, route_slot, experts, capacity)
    buffer = jnp.take(mixed_b, owners // 2, axis=0, mode="fill", fill_value=0).reshape(
        experts, capacity, width
    )
    received = send_rows(buffer).reshape(experts * capacity, width)
    preact = (
        jnp.dot(received, expand_weight[0], preferred_element_type=jnp.float32) + expand_shift[0]
    )
    activ_b = gelu_exact(preact).astype(jnp.bfloat16)
    out_part = jnp.dot(activ_b, shrink_weight[0], preferred_element_type=jnp.float32).reshape(
        experts, capacity, width
    )
    returned = return_rows(out_part, shrink_shift[0]).reshape(experts * capacity, width)
    picked = (
        jnp.take(returned, targets, axis=0, mode="fill", fill_value=0)
        .reshape(tok_count, 2, width)
        .astype(jnp.float32)
    )
    output = hidden + jnp.sum(gate_weights[:, :, None] * picked, axis=1)
    upstream = cotangent.astype(jnp.float32)
    gate_grad = jnp.sum(upstream[:, None, :] * picked, axis=2)
    weighted = (
        (gate_weights[:, :, None] * upstream[:, None, :])
        .astype(jnp.bfloat16)
        .reshape(2 * tok_count, width)
    )
    grad_buffer = jnp.take(weighted, owners, axis=0, mode="fill", fill_value=0).reshape(
        experts, capacity, width
    )
    grad_recv = send_rows(grad_buffer).reshape(experts * capacity, width)
    shrink_g = inner_rows(activ_b, grad_recv)
    sshift_g = jnp.sum(grad_recv.astype(jnp.float32), axis=0)
    pre_grad = outer_cols(grad_recv, shrink_weight[0]) * gelu_slope(preact)
    pre_gradb = pre_grad.astype(jnp.bfloat16)
    expand_g = inner_rows(received, pre_gradb)
    eshift_g = jnp.sum(pre_grad, axis=0)
    rows_part = outer_cols(pre_gradb, expand_weight[0]).reshape(experts, capacity, width)
    back_rows = return_rows(rows_part, 0.0).reshape(experts * capacity, width)
    common = jnp.sum(gate_weights * gate_grad, axis=1, keepdims=True)
    chosen_grad = gate_weights * (gate_grad - common)
    logit_grad = jnp.sum(pick_mask * chosen_grad[:, :, None], axis=1).astype(jnp.bfloat16)
    router_g = inner_rows(mixed_b, logit_grad)
    back_pick = (
        jnp.take(back_rows, targets, axis=0, mode="fill", fill_value=0)
        .reshape(tok_count, 2, width)
        .astype(jnp.float32)
    )
    mixed_grad = jnp.sum(back_pick, axis=1) + outer_cols(logit_grad, router_weight)
    gain2_g = jnp.sum(mixed_grad * scaled2, axis=0)
    shift2_g = jnp.sum(mixed_grad, axis=0)
    hidden_grad = upstream + norm_back(mixed_grad, scaled2, inverse2, norm2_gain)
    pshift_g = jnp.sum(hidden_grad, axis=0)
    hidden_gradb = hidden_grad.astype(jnp.bfloat16)
    proj_g = inner_rows(context_b, hidden_gradb)
    context_grad = outer_cols(hidden_gradb, proj_weight).astype(jnp.bfloat16)
    qkv_gradb = attend_back(queries, keys_b, values_b, log_total, context_b, context_grad, images)
    qkv_g = inner_rows(normed_b, qkv_gradb)
    normed_grad = heads_total(outer_cols(qkv_gradb, qkv_weight))
    gain1_g = jnp.sum(normed_grad * scaled1, axis=0)
    shift1_g = jnp.sum(normed_grad, axis=0)
    tokens_grad = hidden_grad + norm_back(normed_grad, scaled1, inverse1, norm1_gain)
    summed = lax.psum(
        (gain1_g, shift1_g, qkv_g, proj_g, pshift_g, gain2_g, shift2_g, router_g), "expert"
    )
    return (
        output,
        tokens_grad,
        summed[0],
        summed[1],
        summed[2],
        summed[3],
        summed[4],
        summed[5],
        summed[6],
        summed[7],
        expand_g[None],
        eshift_g[None],
        shrink_g[None],
        sshift_g[None],
    )

MESH = pl.DeviceIdType.MESH
F32 = jnp.float32
LIMIT = 57
BF16 = jnp.bfloat16


def place():
    e = lax.axis_index("expert")
    t = lax.axis_index("tensor")
    a = t // 2
    c = t % 2
    return e, t, a, c, (e, 2 * a + 1 - c), (e, 2 * (1 - a) + c)


def greet(devices):
    barrier = pltpu.get_barrier_semaphore()
    for device in devices:
        pl.semaphore_signal(barrier, inc=1, device_id=device, device_id_type=MESH)
    pl.semaphore_wait(barrier, len(devices))


def remote(src, dst, send, recv, device):
    return pltpu.make_async_remote_copy(
        src_ref=src, dst_ref=dst, send_sem=send, recv_sem=recv, device_id=device, device_id_type=MESH
    )


def turns(count):
    far = list(range(count // 2, count))
    near = list(range(1, count // 2))
    order = []
    for i, step in enumerate(far):
        order.append(step)
        if i < len(near):
            order.append(near[i])
    return order


def lanes(index, width):
    return pl.ds(pl.multiple_of(index * width, 128), width)


class Rows:
    def __init__(self, two, one, dest, send_far, send_across, send_core, recv):
        self.two, self.one, self.dest = two, one, dest
        self.send_far, self.send_across = send_far, send_across
        self.send_core, self.recv = send_core, recv
        self.e, self.t, self.a, self.c, self.core, self.across = place()
        self.count = dest.shape[0]
        self.far = 2 * (1 - self.a) + self.c
        self.near, self.cross = 2 * self.a + 1 - self.c, 2 * (1 - self.a) + 1 - self.c

    def half(self, origin):
        return self.dest.at[origin, pl.ds(2 * self.c, 2)]

    def send(self, d):
        to = (self.e ^ d, self.t)
        if d < self.count // 2:
            spot, sem = self.half(self.e), self.recv.at[self.e, 0]
            return remote(self.two.at[d], spot, self.send_far.at[d], sem, to)
        spot, sem = self.dest.at[self.e, self.t], self.recv.at[self.e, self.t]
        return remote(self.one.at[d - self.count // 2], spot, self.send_far.at[d], sem, to)

    def keep(self, sem):
        return pltpu.make_async_copy(self.two.at[0], self.half(self.e), sem)

    def begin(self):
        for d in turns(self.count):
            self.send(d).start()

    def wait_two(self, origin):
        spot = self.half(origin)
        remote(spot, spot, self.send_far.at[0], self.recv.at[origin, 0], self.core).wait_recv()

    def core_two(self, origin):
        spot = self.half(origin)
        return remote(spot, spot, self.send_core.at[origin, 0], self.recv.at[origin, 1], self.core)

    def across_copy(self, origin):
        spot, sem = self.dest.at[origin, self.t], self.recv.at[origin, self.t]
        return remote(spot, spot, self.send_across.at[origin], sem, self.across)

    def core_copy(self, origin, piece):
        spot, sem = self.dest.at[origin, piece], self.recv.at[origin, piece]
        return remote(spot, spot, self.send_core.at[origin, piece], sem, self.core)

    def pass_one(self, origin):
        self.core_copy(origin, self.t).wait_recv()
        self.across_copy(origin).start()
        self.core_copy(origin, self.t).start()

    def hop_one(self, origin):
        self.core_copy(origin, self.far).wait_recv()
        self.core_copy(origin, self.far).start()

    def ready_two(self, origin):
        self.core_two(origin).wait_recv()

    def ready_one(self, origin):
        self.core_copy(origin, self.near).wait_recv()
        self.core_copy(origin, self.cross).wait_recv()

    def close(self):
        for d in range(self.count):
            origin = self.e ^ d
            if d:
                self.send(d).wait_send()
            if d < self.count // 2:
                self.core_two(origin).wait_send()
            else:
                self.across_copy(origin).wait_send()
                self.core_copy(origin, self.t).wait_send()
                self.core_copy(origin, self.far).wait_send()


def front_kernel(
    loads, begin_rows, begin_gates,
    hid, mixed, normed, heads, ctx, cols, marks, rows_two, rows_one, gate_rows, gains, taken,
    tok, cot, experts_t, slots_t, gain1_v, shift1_v, qkv_t, proj_w, proj_shift_v, gain2_v, shift2_v,
    router_t,
    cot_two, cot_one, turned, xsum, xgot1, xpart, xgot2, xdone, xgot3,
    send_far, send_across, send_core, recv, xsem, local,
):
    e, t, a, c, core, across = place()
    count, _, quarter, width = taken.shape
    rows = tok.shape[0]
    tall = xsum.shape[0]
    half = width // 2
    padded = 4 * quarter
    cmine, cother = lanes(c, half), lanes(1 - c, half)
    raw = Rows(cot_two, cot_one, taken, send_far, send_across, send_core, recv)

    def forward(d):
        origin = e ^ d
        if d < count // 2:
            if d:
                raw.wait_two(origin)
            raw.core_two(origin).start()
        else:
            raw.pass_one(origin)

    def place_rows(values, two, one):
        cut = count * quarter
        two[...] = values[:cut].reshape(two.shape)
        one[...] = values[cut:].reshape(one.shape)

    for copy in loads[:3]:
        copy.wait()
    spots = [
        jnp.where(slots_t[j : j + 1] >= 0, experts_t[j : j + 1] * padded + slots_t[j : j + 1], -1)
        for j in range(2)
    ]
    many = lax.broadcasted_iota(jnp.int32, (count * quarter, 1), 0)
    few = lax.broadcasted_iota(jnp.int32, (count // 2 * quarter, 1), 0)
    ids = jnp.concatenate(
        [
            (e ^ (many // (2 * quarter))) * padded + many % (2 * quarter) + 2 * c * quarter,
            (e ^ (count // 2 + few // quarter)) * padded + few % quarter + t * quarter,
        ],
        axis=0,
    )
    chooser = jnp.where((ids == spots[0]) | (ids == spots[1]), 1.0, 0.0).astype(BF16)
    place_rows(jnp.dot(chooser, cot[...], preferred_element_type=F32).astype(BF16), cot_two, cot_one)
    raw.begin()
    keep = raw.keep(local)
    keep.start()
    for copy in loads[3:12]:
        copy.wait()
    gain1, shift1, proj_shift, gain2, shift2 = [
        ref[...].reshape(1, width)
        for ref in (gain1_v, shift1_v, proj_shift_v, gain2_v, shift2_v)
    ]
    token_f = tok[...].astype(F32)
    normed_f, _, _ = normalize(token_f, gain1, shift1)
    normed_b = normed_f.astype(BF16)
    normed[...] = normed_b
    keep.wait()
    forward(0)
    projected = outer_cols(normed_b, qkv_t[...]).astype(BF16)
    head_count = heads.shape[0]
    for i in range(head_count):
        for j in range(3):
            start = DH * (3 * i + j)
            heads[i, j, tall - 16 :] = jnp.zeros((16, DH), BF16)
            heads[i, j, :rows] = projected[:, start : start + DH]
    turned[...] = jnp.zeros_like(turned)
    for j in range(2):
        turned[j : j + 1, :rows] = experts_t[j : j + 1].astype(F32)
        turned[2 + j : 3 + j, :rows] = spots[j].astype(F32)
    table = jnp.transpose(turned[...])[:rows]
    span = -(-rows // 32) * 16
    edge = SEQ // 16 * 16
    limits = ((0, edge), (edge, tall))
    areas = [pl.ds(low, high - low) for low, high in limits]

    def one(p):
        src = xsum.at[areas[p], cother]
        return remote(src, xgot1.at[areas[p]], xsem.at[6 * p], xsem.at[6 * p + 1], core)

    def two(p):
        src, dst = xpart.at[areas[p]], xgot2.at[areas[p]]
        return remote(src, dst, xsem.at[6 * p + 2], xsem.at[6 * p + 3], across)

    def three(p):
        src, dst = xdone.at[areas[p]], xgot3.at[areas[p]]
        return remote(src, dst, xsem.at[6 * p + 4], xsem.at[6 * p + 5], core)

    def start_two(p):
        one(p).wait_recv()
        xpart[areas[p]] = (
            xsum[areas[p], cmine].astype(F32) + xgot1[areas[p]].astype(F32)
        ).astype(BF16)
        two(p).start()

    def start_three(p):
        two(p).wait_recv()
        xdone[areas[p]] = (
            xpart[areas[p]].astype(F32) + xgot2[areas[p]].astype(F32)
        ).astype(BF16)
        three(p).start()

    def finish(p):
        low, high = limits[p][0], min(limits[p][1], rows)
        span_p = pl.ds(low, high - low)
        three(p).wait_recv()
        hid[span_p, cmine] = tok[span_p, cmine].astype(F32) + xdone[span_p].astype(F32)
        hid[span_p, cother] = tok[span_p, cother].astype(F32) + xgot3[span_p].astype(F32)
        hidden = hid[span_p] + proj_shift
        hid[span_p] = hidden
        mixed[span_p] = normalize(hidden, gain2, shift2)[0].astype(BF16)

    for image in range(rows // SEQ):
        base = image * SEQ // 16 * 16
        area = pl.ds(base, span)
        spot_q = lax.broadcasted_iota(jnp.int32, (span, 1), 0) + base
        spot_k = lax.broadcasted_iota(jnp.int32, (1, span), 1) + base
        low, high = image * SEQ, (image + 1) * SEQ
        good_q = (spot_q >= low) & (spot_q < high)
        good_k = (spot_k >= low) & (spot_k < high)
        for i in range(head_count):
            scores = outer_cols(heads[i, 0, area], heads[i, 1, area]) * DH ** (-0.5)
            scores = jnp.where(good_k, scores, -1e30)
            weight = jnp.exp(scores - jnp.max(scores, axis=1, keepdims=True))
            share = jnp.where(good_q, 1.0 / jnp.sum(weight, axis=1, keepdims=True), 0.0)
            value = jnp.dot(
                (weight * share).astype(BF16), heads[i, 2, area], preferred_element_type=F32
            ).astype(BF16)
            columns = pl.ds(DH * i, DH)
            if image == 0:
                ctx[base : base + span, columns] = value
            else:
                over = (image - 1) * SEQ // 16 * 16 + span - base
                ctx[base : base + over, columns] += value[:over]
                ctx[base + over : base + span, columns] = value[over:]
                if i == 0:
                    start_two(0)
                else:
                    forward(i)
        xsum[areas[image]] = jnp.dot(
            ctx[areas[image]], proj_w[...], preferred_element_type=F32
        ).astype(BF16)
        one(image).start()
    slots = lax.broadcasted_iota(jnp.int32, (rows, count * padded), 1)
    for j in range(2):
        hit = slots == table[:, 2 + j : 3 + j].astype(jnp.int32)
        marks[j] = jnp.where(hit, 1.0, 0.0).astype(BF16)
    start_two(1)
    for d in (3, 4, 5, 6, 7):
        forward(d)
    gains[0:1] = gain1
    gains[1:2] = gain2
    start_three(0)
    finish(0)
    start_three(1)
    finish(1)
    mixed_b = mixed[...]
    place_rows(jnp.dot(chooser, mixed_b, preferred_element_type=F32).astype(BF16), rows_two, rows_one)
    begin_rows()
    for d in range(count // 2, count):
        raw.hop_one(e ^ d)
    logits = outer_cols(mixed_b, router_t[...])
    names = lax.broadcasted_iota(jnp.int32, logits.shape, 1)
    chosen = [
        jnp.sum(
            jnp.where(names == table[:, j : j + 1].astype(jnp.int32), logits, 0.0),
            axis=1,
            keepdims=True,
        )
        for j in range(2)
    ]
    gate_top = jnp.maximum(chosen[0], chosen[1])
    lifted = [jnp.exp(value - gate_top) for value in chosen]
    gates = [value / (lifted[0] + lifted[1]) for value in lifted]
    lane = lax.broadcasted_iota(jnp.int32, (rows, 128), 1)
    cols[...] = jnp.where(lane == 2, gates[0], jnp.where(lane == 3, gates[1], table))
    for s in range(count):
        block = pl.ds(s * padded, padded)
        both = marks[0, :, block].astype(F32) * gates[0] + marks[1, :, block].astype(F32) * gates[1]
        gate_rows[s] = jnp.broadcast_to(jnp.sum(both, axis=0, keepdims=True), (8, padded))
    begin_gates()

    def close():
        raw.close()
        for p in range(2):
            one(p).wait_send()
            two(p).wait_send()
            three(p).wait_send()

    return raw, close


def front_parts(rows, width, count, quarter, head_count):
    tall = -(-rows // 16) * 16
    half = width // 2
    padded = 4 * quarter
    dma = pltpu.SemaphoreType.DMA
    piece = pltpu.VMEM((tall, half), BF16)
    outs = [
        pltpu.VMEM((rows, width), F32),
        pltpu.VMEM((rows, width), BF16),
        pltpu.VMEM((rows, width), BF16),
        pltpu.VMEM((head_count, 3, tall, DH), BF16),
        pltpu.VMEM((tall, head_count * DH), BF16),
        pltpu.VMEM((rows, 128), F32),
        pltpu.VMEM((2, rows, count * padded), BF16),
        pltpu.VMEM((count // 2, 2, quarter, width), BF16),
        pltpu.VMEM((count // 2, quarter, width), BF16),
        pltpu.VMEM((count, 8, padded), F32),
        pltpu.VMEM((8, width), F32),
        pltpu.VMEM((count, 4, quarter, width), BF16),
    ]
    scratch = (
        [pltpu.VMEM((count // 2, 2, quarter, width), BF16)]
        + [pltpu.VMEM((count // 2, quarter, width), BF16), pltpu.VMEM((128, 512), F32)]
        + [pltpu.VMEM((tall, width), BF16)]
        + [piece] * 5
        + [dma((count,)), dma((count,)), dma((count, 4)), dma((count, 4)), dma((12,)), dma(())]
    )
    return outs, scratch


def gates_copy(gate_rows, gate_got, send, recv, dst):
    e, t = lax.axis_index("expert"), lax.axis_index("tensor")
    return remote(gate_rows.at[dst], gate_got.at[e], send.at[dst], recv.at[e], (dst, t))


def expert_kernel(
    sent, rows, idle, keep,
    raw, gate_rows, up_w, up_b, down_w, shift,
    rows_in, grads_out, activ, pre_b, bias_grad, shift_grad, out0, out1,
    part, got1, half1, got2, ready, gate_got,
    send_far, send_across, send_core, recv, gate_send, gate_recv,
    send1, recv1, send2, recv2, send3, recv3, send4, recv4, local,
):
    e, t, a, c, core, across = place()
    count = raw.shape[0]
    outs = (out0, out1)
    high, width = part.shape[2] // 2, part.shape[3] // 2
    mine, other = pl.ds(c * high, high), pl.ds((1 - c) * high, high)
    left, right = lanes(a, width), lanes(1 - a, width)

    def origin_of(i):
        return e ^ (4 * (i // 2 % 2) + 2 * (i // 4) + i % 2)

    def gate_copy(dst):
        return gates_copy(gate_rows, gate_got, gate_send, gate_recv, dst)

    def one_copy(k, dst):
        return remote(part.at[k, dst, other], got1.at[k, dst], send1.at[k, dst], recv1.at[k, dst], core)

    def two_copy(k, dst):
        return remote(
            half1.at[k, dst, :, right], got2.at[k, dst], send2.at[k, dst], recv2.at[k, dst], across
        )

    def three_copy(k, dst):
        return remote(ready.at[k, dst], outs[k].at[e, c], send3.at[k, dst], recv3.at[k, e], (dst, t))

    def four_copy(k, origin, side):
        spot = outs[k].at[origin, side]
        return remote(spot, spot, send4.at[k, origin], recv4.at[k, origin], core)

    bias_grad[...] = jnp.zeros_like(bias_grad)
    shift_grad[...] = jnp.zeros_like(shift_grad)
    gate_got[e] = gate_rows[e]
    across_id = lax.broadcasted_iota(jnp.int32, (2 * high, 2 * high), 0)
    down_id = lax.broadcasted_iota(jnp.int32, (2 * high, 2 * high), 1)
    keep.wait()

    def step(i, carry):
        for j in range(2):

            @pl.when((i < count // 2) & (i % 2 == 0))
            def _():
                origin = origin_of(2 * i + j)
                if j == 0:

                    @pl.when(i > 0)
                    def _():
                        rows.wait_two(origin)

                else:
                    rows.wait_two(origin)
                rows.core_two(origin).start()

            @pl.when((i < count // 2) & (i % 2 == 1))
            def _():
                rows.pass_one(origin_of(2 * i + j))

            @pl.when((i >= 1) & (i < count // 2 + 1) & (i % 2 == 0))
            def _():
                rows.hop_one(origin_of(2 * i - 2 + j))

        @pl.when((i >= 2) & (i < count + 2))
        def _():
            origin = origin_of(i - 2)

            @pl.when(i > 2)
            def _():
                here = gate_got.at[origin]
                remote(here, here, gate_send.at[origin], gate_recv.at[origin], across).wait_recv()

            @pl.when(i // 2 % 2 == 1)
            def _():
                rows.ready_two(origin)
                sent.ready_two(origin)

            @pl.when(i // 2 % 2 == 0)
            def _():
                rows.ready_one(origin)
                sent.ready_one(origin)

            tokens = rows_in[origin].reshape(2 * high, 2 * width)
            gate = jnp.sum(
                jnp.where(across_id == down_id, gate_got[origin, 0:1], 0.0), axis=1, keepdims=True
            )
            grads = (gate * raw[origin].reshape(2 * high, 2 * width).astype(F32)).astype(BF16)
            grads_out[origin] = grads
            preact = jnp.dot(tokens, up_w[...], preferred_element_type=F32) + up_b[...]
            bell = 0.5 * (1.0 + lax.erf(preact * half_root))
            active = (preact * bell).astype(BF16)
            activ[origin] = active
            part[0, origin] = jnp.dot(active, down_w[...], preferred_element_type=F32).astype(BF16)
            one_copy(0, origin).start()
            slope = bell + preact * jnp.exp(-0.5 * preact * preact) * gauss_peak
            pre_grad = outer_cols(grads, down_w[...]) * slope
            bias_grad[...] += jnp.sum(pre_grad, axis=0, keepdims=True)
            shift_grad[...] += jnp.sum(grads.astype(F32), axis=0, keepdims=True)
            pre_low = pre_grad.astype(BF16)
            pre_b[origin] = pre_low
            part[1, origin] = outer_cols(pre_low, up_w[...]).astype(BF16)
            one_copy(1, origin).start()

        @pl.when((i >= 4) & (i < count + 4))
        def _():
            dst = origin_of(i - 4)
            for k in range(2):
                one_copy(k, dst).wait_recv()
                half1[k, dst] = (
                    part[k, dst, mine].astype(F32) + got1[k, dst].astype(F32)
                ).astype(BF16)
                two_copy(k, dst).start()

        @pl.when(i >= 6)
        def _():
            dst = origin_of(i - 6)
            for k in range(2):
                two_copy(k, dst).wait_recv()
                total = half1[k, dst, :, left].astype(F32) + got2[k, dst].astype(F32)
                if k == 0:
                    total = total + shift[:, left]
                ready[k, dst] = total.astype(BF16)

                @pl.when(i == 6)
                def _():
                    keep = pltpu.make_async_copy(ready.at[k, dst], outs[k].at[e, c], local.at[k])
                    keep.start()
                    keep.wait()
                    four_copy(k, e, c).start()

                @pl.when(i > 6)
                def _():
                    three_copy(k, dst).start()

        return carry

    lax.fori_loop(0, count + 6, step, 0)
    idle()
    for d in turns(count):
        origin = e ^ d
        for k in range(2):
            spot = outs[k].at[origin, c]
            remote(spot, spot, send4.at[k, origin], recv3.at[k, origin], core).wait_recv()
            four_copy(k, origin, c).start()

    def finish(d, carry):
        origin = e ^ d

        @pl.when(d > 0)
        def _():
            gate_copy(origin).wait_send()

        for k in range(2):
            four_copy(k, origin, 1 - c).wait_recv()
            one_copy(k, origin).wait_send()
            two_copy(k, origin).wait_send()
            four_copy(k, origin, c).wait_send()

            @pl.when(d > 0)
            def _():
                three_copy(k, origin).wait_send()

        return carry

    lax.fori_loop(0, count, finish, 0)
    rows.close()


def expert_parts(count, rows, width, hidden):
    dma = pltpu.SemaphoreType.DMA
    inner = pltpu.VMEM((count, 4 * rows, hidden), BF16)
    out = pltpu.VMEM((count, 2, 2 * rows, width // 2), BF16)
    full = pltpu.VMEM((2, count, 2 * rows, width), BF16)
    half = pltpu.VMEM((2, count, 2 * rows, width // 2), BF16)
    outs = [
        pltpu.VMEM((count, 4, rows, width), BF16),
        pltpu.VMEM((count, 4 * rows, width), BF16),
        inner,
        inner,
    ]
    scratch = (
        [pltpu.VMEM((2, count, 4 * rows, width), BF16), full, full, half, half]
        + [pltpu.VMEM((count, 8, 4 * rows), F32)]
        + [dma((count,)), dma((count,)), dma((count, 4)), dma((count, 4)), dma((count,)), dma((count,))]
        + [dma((2, count))] * 8
        + [dma((2,))]
    )
    return outs, [out, out], scratch


def split(index):
    return index * 192


def weight_sums(left, right, out, leave):
    width = out.shape[0]
    part = width // 3
    right_all = right[...].reshape(-1, out.shape[1])

    @pl.loop(0, 3)
    def _(i):
        spot = lanes(i, part)
        left_part = left[..., spot].reshape(-1, part)
        out[pl.ds(pl.multiple_of(i * part, 8), part)] = inner_rows(left_part, right_all)

    leave.start()


def back_kernel(
    ret, bak, marks, cols, cot, hid, mixed, router, gains, tok, normed, heads, ctx,
    proj_w, qkv_w, received, grad_recv, activ, pre_b, leave,
    out, tok_g, fin, sums, shrink_g, expand_g,
    back_s, back_r, added_s, added_r, gate_s, gate_r, wide_b, hid_g,
    upper, turned, gsrc, got1, part, got2,
    xsum, xgot1, xpart, xgot2, xdone, xgot3, sm, sgot, sq, sgy, sgz,
    bsem, asem, gsem, s1, r1, s2, r2, s3, r3, s4, r4, xsem, tsem, ysem, zsend, zrecv, osem,
):
    e, t, a, c, core, across = place()
    z, y = e // 2, e % 2
    diag = (e, 2 * (1 - a) + 1 - c)
    beside = (2 * z + 1 - y, t)
    deep = got2.shape[1]
    rows, width = tok.shape
    tall = wide_b.shape[0]
    half = width // 2
    block = back_s.shape[1]
    chunks = gsrc.shape[0]
    factor = DH ** (-0.5)
    left, right = lanes(a, half), lanes(1 - a, half)
    ymine, yother = lanes(y, half), lanes(1 - y, half)
    cmine, cother = lanes(c, half), lanes(1 - c, half)

    def peers(order=(2, 1, 3)):
        return [lax.rem(z + d, deep) for d in order]

    total_slots = ret.shape[0] * ret.shape[1] * ret.shape[2]
    ret_all = ret[...].reshape(total_slots, half)
    bak_all = bak[...].reshape(total_slots, half)
    back_here = jnp.dot(marks[0] + marks[1], bak_all, preferred_element_type=F32).astype(BF16)
    picked = [jnp.dot(marks[j], ret_all, preferred_element_type=F32) for j in range(2)]
    route = cols[:, 0:2].astype(jnp.int32)
    g = [cols[:, 2:3], cols[:, 3:4]]
    back_s[1, block - 32 :, :] = jnp.zeros((32, half), BF16)
    added_s[1, block - 32 :, :] = jnp.zeros((32, half), BF16)
    back_s[0] = back_here[:block]
    back_s[1, : rows - block] = back_here[block:]
    back_across = remote(back_s.at[c], back_r.at[c], bsem.at[0], bsem.at[1], across)
    back_across.start()
    cot_half = cot[:, left].astype(F32)
    lane = lax.broadcasted_iota(jnp.int32, (rows, 128), 1)
    dots = [jnp.sum(cot_half * value, axis=1, keepdims=True) for value in picked]
    turned[...] = jnp.zeros_like(turned)
    turned[:rows] = jnp.where(lane == 0, dots[0], jnp.where(lane == 1, dots[1], 0.0))
    gate_s[...] = jnp.transpose(turned[...])[:8]
    gate_across = remote(gate_s, gate_r, gsem.at[0], gsem.at[1], across)
    gate_across.start()
    added_here = (g[0] * picked[0] + g[1] * picked[1]).astype(BF16)
    added_s[0] = added_here[:block]
    added_s[1, : rows - block] = added_here[block:]
    added_across = remote(added_s.at[c], added_r.at[c], asem.at[0], asem.at[1], across)
    added_across.start()
    mixed_row = mixed[...]
    hidden = hid[...]
    centered = hidden - jnp.mean(hidden, axis=1, keepdims=True)
    inverse2 = lax.rsqrt(jnp.mean(centered * centered, axis=1, keepdims=True) + norm_eps)
    scaled2 = centered * inverse2
    wide_b[:rows, left] = back_here
    for i in range(3):
        upper[i, tall - 16 :] = jnp.zeros((16, DH), BF16)

    weight_sums(activ, grad_recv, shrink_g, leave[1])
    back_across.wait_recv()
    back_core = remote(back_r.at[c], back_r.at[c], bsem.at[2], bsem.at[3], core)
    back_core.start()
    gate_across.wait_recv()
    gate_sum = gate_s[...] + gate_r[...]
    gate_cols = jnp.transpose(jnp.concatenate([gate_sum] * 16, axis=0))[:rows]
    gate_grad = [gate_cols[:, 0:1], gate_cols[:, 1:2]]
    common = g[0] * gate_grad[0] + g[1] * gate_grad[1]
    experts = lax.broadcasted_iota(jnp.int32, (rows, router.shape[0]), 1)
    logit_grad = (
        jnp.where(experts == route[:, 0:1], g[0] * (gate_grad[0] - common), 0.0)
        + jnp.where(experts == route[:, 1:2], g[1] * (gate_grad[1] - common), 0.0)
    ).astype(BF16)
    sm[1] = inner_rows(logit_grad, mixed_row) * 0.25
    from_router = jnp.dot(logit_grad, router[...], preferred_element_type=F32)
    back_other = remote(back_r.at[1 - c], back_r.at[1 - c], bsem.at[2], bsem.at[3], core)
    back_other.wait_recv()
    wide_b[:block, right] = back_r[0]
    wide_b[block:rows, right] = back_r[1, : rows - block]
    mixed_grad = wide_b[:rows].astype(F32) + from_router
    hidden_grad = cot[...].astype(F32) + norm_back(mixed_grad, scaled2, inverse2, gains[1:2])
    hid_g[...] = hidden_grad
    hidden_low = hidden_grad.astype(BF16)
    gsrc[0] = inner_rows(ctx[:rows], hidden_low).astype(BF16).reshape(gsrc.shape[1:])

    def y_copy(k):
        return remote(gsrc.at[k, :, :, yother], got1.at[k], s1.at[k], r1.at[k], beside)

    def z_copy(k, zz):
        return remote(part.at[k, zz], got2.at[k, z], s2.at[k, zz], r2.at[k, z], (2 * zz + y, t))

    def spread_copy(k, zz):
        spot = fin.at[k, z, :, ymine]
        return remote(spot, spot, s3.at[k, zz], r3.at[k, z], (2 * zz + y, t))

    def pass_copy(k, zz):
        spot = fin.at[k, zz, :, ymine]
        return remote(spot, spot, s4.at[k, zz], r4.at[k, zz], beside)

    def step_two(k):
        y_copy(k).wait_recv()
        part[k] = (gsrc[k, :, :, ymine].astype(F32) + got1[k].astype(F32)).astype(BF16)
        for zz in peers():
            z_copy(k, zz).start()

    def step_three(k):
        value = part[k, z].astype(F32)
        for zz in peers((1, 3, 2)):
            spot = got2.at[k, zz]
            remote(spot, spot, s2.at[k, zz], r2.at[k, zz], beside).wait_recv()
            value = value + got2[k, zz].astype(F32)
        fin[k, z, :, ymine] = value.astype(BF16)
        for zz in peers():
            spread_copy(k, zz).start()
        pass_copy(k, z).start()

    def step_four(k):
        for zz in peers((1, 3, 2)):
            spot = fin.at[k, zz, :, ymine]
            remote(spot, spot, s3.at[k, zz], r3.at[k, zz], beside).wait_recv()
            pass_copy(k, zz).start()

    y_copy(0).start()
    context_grad = outer_cols(hidden_low, proj_w[...]).astype(BF16)
    for i in range(3):
        upper[i, :rows] = context_grad[:, DH * i : DH * (i + 1)]
    sm[0, 2:3] = jnp.sum(hidden_grad, axis=0, keepdims=True) * 0.25
    sm[0, 3:4] = jnp.sum(mixed_grad * scaled2, axis=0, keepdims=True) * 0.25
    sm[0, 4:5] = jnp.sum(mixed_grad, axis=0, keepdims=True) * 0.25
    sm[0, 5:8] = jnp.zeros((3, width), F32)

    span = block
    for i in range(3):
        for image in range(rows // SEQ):
            base = image * SEQ // 16 * 16
            area = pl.ds(base, span)
            spot_k = lax.broadcasted_iota(jnp.int32, (span, 1), 0) + base
            spot_q = lax.broadcasted_iota(jnp.int32, (1, span), 1) + base
            low, high = image * SEQ, (image + 1) * SEQ
            good_k = (spot_k >= low) & (spot_k < high)
            good_q = (spot_q >= low) & (spot_q < high)
            queries, keys_b, values_b = heads[i, 0, area], heads[i, 1, area], heads[i, 2, area]
            up = upper[i, area]
            scores = outer_cols(keys_b, queries) * factor
            scores = jnp.where(good_k, scores, -1e30)
            top = jnp.max(scores, axis=0, keepdims=True)
            weight = jnp.exp(scores - top)
            share = jnp.where(good_q, 1.0 / jnp.sum(weight, axis=0, keepdims=True), 0.0)
            attention = weight * share
            attn_b = attention.astype(BF16)
            value_grad = jnp.dot(attn_b, up, preferred_element_type=F32)
            attn_grad = outer_cols(values_b, up)
            row_dot = jnp.sum(attention * attn_grad, axis=0, keepdims=True)
            score_grad = (attention * (attn_grad - row_dot) * factor).astype(BF16)
            key_grad = jnp.dot(score_grad, queries, preferred_element_type=F32)
            query_grad = inner_rows(score_grad, keys_b)
            for j, value in enumerate((query_grad, key_grad, value_grad)):
                columns = pl.ds(split(i) + DH * j, DH)
                if image == 0:
                    xsum_low = value.astype(BF16)
                    wide_b[base : base + span, columns] = xsum_low
                else:
                    over = (image - 1) * SEQ // 16 * 16 + span - base
                    xsum_low = value.astype(BF16)
                    wide_b[base : base + over, columns] += xsum_low[:over]
                    wide_b[base + over : base + span, columns] = xsum_low[over:]
        mine = wide_b[:rows, split(i) : split(i + 1)]
        gsrc[1 + i] = inner_rows(mine, normed[...]).astype(BF16).reshape(gsrc.shape[1:])
        y_copy(1 + i).start()
        step_two(i)
        if i >= 1:
            step_three(i - 1)
        if i >= 2:
            step_four(i - 2)
    qkv_low = wide_b[:rows, : qkv_w.shape[0]]
    normed_part = jnp.dot(qkv_low, qkv_w[...], preferred_element_type=F32)
    xsum[tall - 16 :] = jnp.zeros((16, width), BF16)
    xsum[:rows] = normed_part.astype(BF16)
    x1 = remote(xsum.at[:, cother], xgot1, xsem.at[0], xsem.at[1], core)
    x1.start()
    step_two(3)
    token_f = tok[...].astype(F32)
    centered1 = token_f - jnp.mean(token_f, axis=1, keepdims=True)
    inverse1 = lax.rsqrt(jnp.mean(centered1 * centered1, axis=1, keepdims=True) + norm_eps)
    scaled1 = centered1 * inverse1
    sm[0, 0:1] = jnp.sum(normed_part * scaled1, axis=0, keepdims=True)
    sm[0, 1:2] = jnp.sum(normed_part, axis=0, keepdims=True)

    def quarter(aa, cc):
        return sm.at[aa, :, lanes(cc, half)]

    trade = [
        remote(quarter(a, 1 - c), sgot.at[0], tsem.at[0, 0], tsem.at[1, 0], core),
        remote(quarter(1 - a, c), sgot.at[1], tsem.at[0, 1], tsem.at[1, 1], across),
        remote(quarter(1 - a, 1 - c), sgot.at[2], tsem.at[0, 2], tsem.at[1, 2], diag),
    ]
    for copy in trade:
        copy.start()
    x1.wait_recv()
    xpart[...] = (xsum[:, cmine].astype(F32) + xgot1[...].astype(F32)).astype(BF16)
    x2 = remote(xpart, xgot2, xsem.at[2], xsem.at[3], across)
    x2.start()
    step_three(2)
    step_four(1)
    for copy in trade:
        copy.wait_recv()
    sq[0] = (sm[a, :, cmine] + sgot[0]) + (sgot[1] + sgot[2])
    small_y = remote(sq.at[0], sgy, ysem.at[0], ysem.at[1], beside)
    small_y.start()

    step_three(3)
    step_four(2)
    small_y.wait_recv()
    sq[1] = sq[0] + sgy[...]
    small_z = [
        remote(sq.at[1], sgz.at[z], zsend.at[zz], zrecv.at[z], (2 * zz + y, t)) for zz in peers()
    ]
    for copy in small_z:
        copy.start()
    sgz[z] = sq[1]
    step_four(3)
    for zz in peers((1, 3, 2)):
        spot = sgz.at[zz]
        remote(spot, spot, zsend.at[zz], zrecv.at[zz], beside).wait_recv()
    sums[a, :, cmine] = (sgz[0] + sgz[1]) + (sgz[2] + sgz[3])
    here = sums.at[a, :, cmine]
    tell = [
        remote(here, here, osem.at[0, i], osem.at[1, i], device)
        for i, device in enumerate((core, across, diag))
    ]
    for copy in tell:
        copy.start()
    added_across.wait_recv()
    added_core = remote(added_r.at[c], added_r.at[c], asem.at[2], asem.at[3], core)
    added_core.start()
    x2.wait_recv()
    xpart_sum = (xpart[...].astype(F32) + xgot2[...].astype(F32)).astype(BF16)
    xdone[...] = xpart_sum
    x3 = remote(xdone, xgot3, xsem.at[4], xsem.at[5], core)
    x3.start()
    wide_b[:, cmine] = xpart_sum
    added_other = remote(added_r.at[1 - c], added_r.at[1 - c], asem.at[2], asem.at[3], core)
    added_other.wait_recv()
    out[:, left] = hid[:, left] + jnp.concatenate([added_s[0], added_s[1, : rows - block]], 0).astype(F32)
    out[:, right] = hid[:, right] + jnp.concatenate([added_r[0], added_r[1, : rows - block]], 0).astype(F32)
    leave[2].start()
    x3.wait_recv()
    wide_b[:, cother] = xgot3[...]
    normed_grad = wide_b[:rows].astype(F32)
    tok_g[...] = hid_g[...] + norm_back(normed_grad, scaled1, inverse1, gains[0:1])
    leave[3].start()
    for k in range(chunks):
        for zz in range(deep):
            spot = fin.at[k, zz, :, yother]
            remote(spot, spot, s4.at[k, zz], r4.at[k, zz], beside).wait_recv()
    for copy, (aa, cc) in zip(tell, ((a, 1 - c), (1 - a, c), (1 - a, 1 - c))):
        copy.wait_recv()
    for copy in trade + tell + small_z:
        copy.wait_send()
    for copy in (
        back_across, back_core, gate_across, added_across, added_core, x1, x2, x3, small_y,
    ):
        copy.wait_send()
    for k in range(chunks):
        y_copy(k).wait_send()
        pass_copy(k, z).wait_send()
        for zz in peers():
            z_copy(k, zz).wait_send()
            spread_copy(k, zz).wait_send()
            pass_copy(k, zz).wait_send()


def back_parts(rows, width, count):
    half = width // 2
    tall = -(-rows // 16) * 16
    block = -(-rows // 32) * 16
    deep = count // 2
    chunks = 4
    depth = width // chunks // deep
    dma = pltpu.SemaphoreType.DMA

    def low(*shape):
        return pltpu.VMEM(shape, BF16)

    def wide(*shape):
        return pltpu.VMEM(shape, F32)

    pair = low(2, block, half)
    line = wide(8, 512)
    stage = low(chunks, deep, depth, half)
    quarter = wide(8, half)
    outs = [wide(rows, width), wide(rows, width), wide(width, width), wide(width, width)]
    scratch = (
        [pair, pair, pair, pair, line, line, low(tall, width), wide(rows, width)]
        + [low(3, tall, DH), wide(512, 128)]
        + [low(chunks, deep, depth, width), stage, stage, stage]
        + [low(tall, width)]
        + [low(tall, half)] * 5
        + [wide(2, 8, width), wide(3, 8, half), wide(2, 8, half), quarter, wide(deep, 8, half)]
        + [dma((4,)), dma((4,)), dma((2,)), dma((chunks,)), dma((chunks,))]
        + [dma((chunks, deep))] * 6
        + [dma((6,)), dma((2, 3)), dma((2,)), dma((deep,)), dma((deep,)), dma((2, 3))]
    )
    return outs, scratch, (chunks, deep, depth, width)


def whole_kernel(counts, *refs):
    groups = []
    at = 0
    for number in counts:
        groups.append(refs[at : at + number])
        at += number
    (
        ins, (out_h, tok_h, shrink_h, expand_h, fin, sums, bias_grad, shift_grad),
        held, front_outs, front_scratch, rows_outs, results, expert_scratch, back_outs,
        back_scratch, (load, save),
    ) = groups
    e, t, a, c, core, across = place()
    loads = [pltpu.make_async_copy(src, dst, load.at[i]) for i, (src, dst) in enumerate(zip(ins, held))]
    for copy in loads:
        copy.start()
    experts = front_outs[-1].shape[0]
    greet([(e ^ d, t) for d in range(1, experts)] + [core, across, (e, 2 * (1 - a) + 1 - c)])
    (
        experts_t, slots_t, cot, tok, gain1_v, shift1_v, qkv_t, proj_w, proj_shift_v, gain2_v,
        shift2_v, router_t, up_w, up_b, down_w, shift,
    ) = held
    hid, mixed, normed, heads, ctx, cols, marks, rows_two, rows_one, gate_rows, gains, raw = front_outs
    rows_in = rows_outs[0]
    gate_got, send_far, send_across, send_core, recv, gate_send, gate_recv = expert_scratch[5:12]
    rows = Rows(rows_two, rows_one, rows_in, send_far, send_across, send_core, recv)
    keep = rows.keep(expert_scratch[-1].at[0])

    def begin_rows():
        rows.begin()
        keep.start()

    def begin_gates():
        for d in turns(experts):
            gates_copy(gate_rows, gate_got, gate_send, gate_recv, e ^ d).start()

    sent, close = front_kernel(
        loads, begin_rows, begin_gates, *front_outs,
        tok, cot, experts_t, slots_t, gain1_v, shift1_v, qkv_t, proj_w, proj_shift_v, gain2_v,
        shift2_v, router_t,
        *front_scratch,
    )
    for copy in loads[12:]:
        copy.wait()
    out, tok_g, shrink_g, expand_g = back_outs
    pairs = ((expand_g, expand_h), (shrink_g, shrink_h), (out, out_h), (tok_g, tok_h))
    leave = [pltpu.make_async_copy(src, dst, save.at[i]) for i, (src, dst) in enumerate(pairs)]
    expert_kernel(
        sent, rows, lambda: weight_sums(rows_in, rows_outs[3], expand_g, leave[0]), keep,
        raw, gate_rows, up_w, up_b, down_w, shift,
        *rows_outs, bias_grad, shift_grad, *results, *expert_scratch,
    )
    back_kernel(
        *results, marks, cols, cot, hid, mixed, router_t, gains, tok, normed, heads, ctx,
        proj_w, qkv_t, *rows_outs, leave,
        out, tok_g, fin, sums, shrink_g, expand_g,
        *back_scratch,
    )
    close()
    for copy in leave:
        copy.wait()


def run_whole(args, experts, quarter):
    tok = args[3]
    rows, width = tok.shape
    hidden = args[12].shape[1]
    head_count = args[7].shape[0] // DH
    vmem = pl.BlockSpec(memory_space=pltpu.VMEM)
    hbm = pl.BlockSpec(memory_space=pltpu.HBM)
    dma = pltpu.SemaphoreType.DMA
    front_outs, front_scratch = front_parts(rows, width, experts, quarter, head_count)
    rows_outs, results, expert_scratch = expert_parts(experts, quarter, width, hidden)
    back_outs, back_scratch, big = back_parts(rows, width, experts)
    held = [pltpu.VMEM(value.shape, value.dtype) for value in args]
    outs = [jax.ShapeDtypeStruct(value.shape, F32) for value in back_outs]
    outs = outs + [
        jax.ShapeDtypeStruct(big, BF16),
        jax.ShapeDtypeStruct((2, 8, width), F32),
        jax.ShapeDtypeStruct((1, hidden), F32),
        jax.ShapeDtypeStruct((1, width), F32),
    ]
    parts = [
        held, front_outs, front_scratch, rows_outs, results, expert_scratch, back_outs,
        back_scratch, [dma((len(args),)), dma((4,))],
    ]
    counts = [len(args), len(outs)] + [len(part) for part in parts]
    return pl.pallas_call(
        functools.partial(whole_kernel, counts),
        out_shape=tuple(outs),
        in_specs=[hbm] * len(args),
        out_specs=(hbm,) * 4 + (vmem,) * 4,
        scratch_shapes=sum(parts, []),
        compiler_params=pltpu.CompilerParams(
            collective_id=1, has_side_effects=True, vmem_limit_bytes=LIMIT * 1024 * 1024
        ),
    )(*args)


def last_kernel(
    out, tok_g, big, expand_g, shrink_g, eshift, sshift, small,
    out_h, tok_h, qkv_h, proj_h, expand_h, shrink_h, eshift_h, sshift_h, router_h, *rest,
):
    lines_h, (full, fin, sums, *rest) = rest[:5], rest[5:]
    lines, held, (load, sem) = rest[:5], rest[5:11], rest[11:]
    chunks, deep, depth, width = fin.shape
    cut = deep * depth
    plain = (expand_g, shrink_g, out, tok_g, eshift, sshift)
    plain_h = (expand_h, shrink_h, out_h, tok_h, eshift_h, sshift_h)
    takes = [
        pltpu.make_async_copy(src, dst, load.at[i])
        for i, (src, dst) in enumerate(zip((small, big) + plain, (sums, fin) + tuple(held)))
    ]
    for copy in takes:
        copy.start()
    copies = []

    def send(src, dst):
        copy = pltpu.make_async_copy(src, dst, sem.at[len(copies)])
        copy.start()
        copies.append(copy)

    takes[0].wait()
    send(sums.at[1], router_h)
    for i in range(5):
        lines[i][...] = sums[0, i : i + 1].reshape(width)
        send(lines[i], lines_h[i])
    takes[1].wait()
    full[...] = fin[...].astype(F32).reshape(chunks * cut, width)
    send(full.at[pl.ds(0, cut)], proj_h)
    send(full.at[pl.ds(cut, (chunks - 1) * cut)], qkv_h)
    for i, dst in enumerate(plain_h):
        takes[2 + i].wait()
        send(held[i], dst)
    for copy in copies:
        copy.wait()


def run_last(args):
    big = args[2]
    chunks, deep, depth, width = big.shape
    cut = deep * depth
    hbm = pl.BlockSpec(memory_space=pltpu.HBM)

    def shape(*sizes):
        return jax.ShapeDtypeStruct(sizes, F32)

    outs = (
        args[0],
        args[1],
        shape((chunks - 1) * cut, width),
        shape(cut, width),
        args[3],
        args[4],
        args[5],
        args[6],
        shape(8, width),
    ) + (shape(width),) * 5
    outs = tuple(jax.ShapeDtypeStruct(value.shape, F32) for value in outs)
    return pl.pallas_call(
        last_kernel,
        out_shape=outs,
        in_specs=[hbm] * len(args),
        out_specs=(hbm,) * len(outs),
        scratch_shapes=[
            pltpu.VMEM((chunks * cut, width), F32),
            pltpu.VMEM(big.shape, BF16),
            pltpu.VMEM(args[7].shape, F32),
        ]
        + [pltpu.VMEM((width,), F32)] * 5
        + [pltpu.VMEM(args[i].shape, F32) for i in (3, 4, 0, 1, 5, 6)]
        + [pltpu.SemaphoreType.DMA((len(args),))]
        + [pltpu.SemaphoreType.DMA((len(outs),))],
        compiler_params=pltpu.CompilerParams(vmem_limit_bytes=LIMIT * 1024 * 1024),
    )(*args)


def fast_device(
    tokens,
    norm1_gain,
    norm1_shift,
    qkv_weight,
    proj_weight,
    proj_shift,
    norm2_gain,
    norm2_shift,
    router_weight,
    expand_weight,
    expand_shift,
    shrink_weight,
    shrink_shift,
    route_expert,
    route_slot,
    cotangent,
):
    experts = lax.axis_size("expert")
    tensor_count = lax.axis_size("tensor")
    tok_count = tokens.shape[0]
    capacity = tensor_count * (5 * tok_count // (2 * experts * tensor_count) + 1)
    quarter = -(-capacity // (16 * tensor_count)) * 16
    qkv_t = qkv_weight.T
    router_t = router_weight.T
    output, tokens_grad, shrink_g, expand_g, big, small, eshift_g, sshift_g = run_whole(
        (
            route_expert.T,
            route_slot.T,
            cotangent,
            tokens,
            norm1_gain,
            norm1_shift,
            qkv_t,
            proj_weight,
            proj_shift,
            norm2_gain,
            norm2_shift,
            router_t,
            expand_weight[0],
            expand_shift,
            shrink_weight[0],
            shrink_shift,
        ),
        experts,
        quarter,
    )
    (
        output,
        tokens_grad,
        qkv_g,
        proj_g,
        expand_g,
        shrink_g,
        eshift_g,
        sshift_g,
        router_g,
        gain1_g,
        shift1_g,
        pshift_g,
        gain2_g,
        shift2_g,
    ) = run_last((output, tokens_grad, big, expand_g, shrink_g, eshift_g, sshift_g, small))
    return (
        output,
        tokens_grad,
        gain1_g,
        shift1_g,
        qkv_g.T,
        proj_g,
        pshift_g,
        gain2_g,
        shift2_g,
        router_g.T,
        expand_g[None],
        eshift_g,
        shrink_g[None],
        sshift_g,
    )


def solution(mesh):
    small_mesh = mesh.shape["expert"] == 8 and mesh.shape["tensor"] == 4
    on_device = fast_device if small_mesh else plain_device
    return jax.shard_map(
        on_device,
        mesh=mesh,
        in_specs=(
            P("expert", None),
            P(),
            P(),
            P(None, "tensor"),
            P("tensor", None),
            P(),
            P(),
            P(),
            P(),
            P("expert", None, "tensor"),
            P("expert", "tensor"),
            P("expert", "tensor", None),
            P("expert", None),
            P("expert", None),
            P("expert", None),
            P("expert", None),
        ),
        out_specs=(
            P("expert", None),
            P("expert", None),
            P(),
            P(),
            P(None, "tensor"),
            P("tensor", None),
            P(),
            P(),
            P(),
            P(),
            P("expert", None, "tensor"),
            P("expert", "tensor"),
            P("expert", "tensor", None),
            P("expert", None),
        ),
        check_vma=False,
    )
```
